32 devices in a mesh: tm: 32 (over z, y, x, core).
Axes of the slice: x: 2, y: 2, z: 4, core: 2. Of those that a mesh axis runs over, the one named last changes fastest.
Arguments:
- schur_inverse: float32 [32, 320, 320], P('tm'), as said below
- sweep_factor: float32 [32, 320, 320], P('tm')
Outputs:
- diagonal_blocks: float32 [32, 320, 320], P('tm')
- coupling_blocks: float32 [32, 320, 320], P('tm')
Inputs may be any that keep to these rules, and one draw needn't show every extreme that they name: Every block of schur_inverse is symmetric.
All inputs are finite; a program needn't handle non-finite values.
Results may differ from the reference program's by a relative error of at most 0.0003.
Values sent between devices are 32-bit elements; how exact they have to be, the bound alone decides.
A program may use at most 192 MiB of HBM per device.

```python
import math
import jax
import jax.numpy as jnp
from jax import lax

B = 320
EPOCH_COUNT = 32


def product_high(left, right):
    return jnp.matmul(left, right, precision=lax.Precision.HIGHEST)


def joint_layout_profile(key):
    base_key = jax.random.fold_in(key, 101)
    stochastic_seeds = jax.random.split(base_key, 5)
    raw_matrix = jax.random.normal(stochastic_seeds[0], (B, B), jnp.float32)
    orthonormal_frame, _ = jnp.linalg.qr(raw_matrix)
    slow_share = 0.5
    reach = jax.random.uniform(stochastic_seeds[1], (B,), jnp.float32, 0.0, 0.5)
    slow_pick = jax.random.uniform(stochastic_seeds[2], (B,), jnp.float32, 0.0, 1.0) < slow_share
    fast_length = jnp.exp(jax.random.uniform(stochastic_seeds[3], (B,), jnp.float32, math.log(30.0), math.log(50.0)))
    lane_fading_speeds = jnp.where(slow_pick, 1.0 - reach / EPOCH_COUNT, 1.0 - 1.0 / fast_length)
    spike_indices = jax.random.randint(stochastic_seeds[4], (2,), 0, EPOCH_COUNT)
    return (orthonormal_frame, lane_fading_speeds, spike_indices)


def draw_schur_inverse(key, part):
    orthonormal_frame, lane_fading_speeds, spike_indices = joint_layout_profile(key)
    stochastic_seeds = jax.random.split(jax.random.fold_in(key, 7), 4)
    spread = 0.15 / math.sqrt(B)
    common_noise = jax.random.normal(stochastic_seeds[0], (B, B), jnp.float32) * spread
    common_noise = (common_noise + common_noise.T) * 0.7071
    own_noise = jax.random.normal(stochastic_seeds[1], (EPOCH_COUNT, B, B), jnp.float32) * spread
    own_noise = (own_noise + jnp.swapaxes(own_noise, 1, 2)) * 0.7071
    common_diag = jax.random.uniform(stochastic_seeds[2], (B,), jnp.float32, 0.7, 2.0)
    own_diag = jax.random.uniform(stochastic_seeds[3], (EPOCH_COUNT, B), jnp.float32, 0.9, 1.1)
    identity = jnp.eye(B, dtype=jnp.float32)
    inner = common_noise[None] + own_noise + identity[None] * (common_diag[None, :] * own_diag)[:, :, None]
    weight = jnp.sqrt(1.0 - lane_fading_speeds * lane_fading_speeds + 2.0 / EPOCH_COUNT)
    inner = inner * weight[None, :, None] * weight[None, None, :]
    blocks = product_high(product_high(orthonormal_frame[None], inner), orthonormal_frame.T[None])
    return 0.5 * (blocks + jnp.swapaxes(blocks, 1, 2))


def draw_sweep_factor(key, part):
    orthonormal_frame, lane_fading_speeds, spike_indices = joint_layout_profile(key)
    stochastic_seeds = jax.random.split(jax.random.fold_in(key, 11), 3)
    small_perturbation = jax.random.uniform(stochastic_seeds[0], (EPOCH_COUNT, B), jnp.float32, 0.0, 0.2) / EPOCH_COUNT
    magnitude_level = jax.random.uniform(stochastic_seeds[1], (EPOCH_COUNT, 1), jnp.float32, 0.75, 0.9)
    node_coordinates = jnp.arange(EPOCH_COUNT, dtype=jnp.int32)[:, None]
    spike_flag_grid = jnp.any(node_coordinates == spike_indices[None, :], axis=1)[:, None]
    increment_speeds = lane_fading_speeds[None, :] * (1.0 - small_perturbation) * jnp.where(spike_flag_grid, magnitude_level, 1.0)
    scaled_basis = orthonormal_frame[None, :, :] * increment_speeds[:, None, :]
    core = product_high(scaled_basis, orthonormal_frame.T[None])
    identity = jnp.eye(B, dtype=jnp.float32)
    tilt = identity[None] + jax.random.normal(stochastic_seeds[2], (EPOCH_COUNT, B, B), jnp.float32) * math.sqrt(0.15 / (B * EPOCH_COUNT))
    rotation, upper = jnp.linalg.qr(tilt)
    signs = jnp.sign(jnp.diagonal(upper, axis1=1, axis2=2))
    rotation = rotation * signs[:, None, :]
    return product_high(core, rotation)


def setup_inputs(seed: int = 0) -> dict:
    streams_of = jax.random.split(jax.random.key(seed), 3)
    schur_inverse = draw_schur_inverse(jax.random.fold_in(streams_of[2], 71), 0)
    sweep_factor = draw_sweep_factor(jax.random.fold_in(streams_of[2], 71), 0)
    return dict(schur_inverse=schur_inverse, sweep_factor=sweep_factor)


def matmul(left, right):
    return jnp.dot(left.astype(jnp.float32), right.astype(jnp.float32), precision=lax.Precision.HIGHEST, preferred_element_type=jnp.float32)

def reference(schur_inverse, sweep_factor):

    def advance(current, blocks):
        inverse, factor = blocks
        moved = matmul(factor, current)
        diagonal = inverse + matmul(moved, factor.T)
        return (diagonal, (diagonal, moved.T))
    start = jnp.zeros((B, B), jnp.float32)
    _, (diagonal_blocks, moved_rows) = lax.scan(advance, start, (schur_inverse, sweep_factor), reverse=True)
    coupling_blocks = jnp.concatenate([jnp.zeros((1, B, B), jnp.float32), moved_rows[:-1]], axis=0)
    return (diagonal_blocks, coupling_blocks)
```

```python
import functools

import jax
import jax.numpy as jnp
from jax import lax
from jax.experimental import pallas as pl
from jax.experimental.pallas import tpu as pltpu
from jax.sharding import PartitionSpec as P

MESH = pl.DeviceIdType.MESH
STRIP = 128
GROUP_LEVELS = 3
NN = (((1,), (0,)), ((), ()))
NT = (((1,), (1,)), ((), ()))


def dot(left, right, dims):
    return lax.dot_general(left, right, dims, preferred_element_type=jnp.float32)


def split(value, high, low):
    top = value.astype(jnp.bfloat16)
    high[...] = top
    low[...] = (value - top.astype(jnp.float32)).astype(jnp.bfloat16)


def product(left, right, dims):
    lh, ll = left
    rh, rl = right
    return (
        dot(lh[...], rl[...], dims) + dot(ll[...], rh[...], dims)
    ) + dot(lh[...], rh[...], dims)


def strips_of(order):
    return [(a, min(a + STRIP, order)) for a in range(0, order, STRIP)]


def kernel(n, levels, g_any, l_any, x_ref, q_ref, *scratch):
    (g_ref, l_ref, ro, rp, so, sp, to, tp, rx, prev, xt, xc, ph, pll, vh, vl, wh, wl,
     o_send, o_recv, p_send, p_recv, x_send, x_recv, n_send, n_recv, in_sem) = scratch
    order = g_ref.shape[0]
    strips = strips_of(order)
    count = len(strips)
    me = lax.axis_index("tm")
    size = 1 << levels
    j = lax.rem(me, size)
    group = me // size
    top = n // size - 1
    bits = [lax.rem(j // (1 << b), 2) for b in range(levels)]
    reach = [1 << b for b in range(levels)] + [size]
    even = bits[0] == 0
    odd = bits[0] == 1
    rest = group < top
    g_in = pltpu.make_async_copy(g_any, g_ref, in_sem.at[0])
    l_in = pltpu.make_async_copy(l_any, l_ref, in_sem.at[1])
    g_in.start()
    l_in.start()

    barrier = pltpu.get_barrier_semaphore()
    total = 0
    for d in reach:
        for other, inside in ((me + d, me + d < n), (me - d, me - d >= 0)):
            total = total + inside.astype(jnp.int32)

            @pl.when(inside)
            def _(other=other):
                pl.semaphore_signal(barrier, inc=1, device_id=(other,), device_id_type=MESH)

    g_in.wait()
    l_in.wait()
    pl.semaphore_wait(barrier, total)

    def copy(src, dst, send, recv, target):
        return pltpu.make_async_remote_copy(
            src_ref=src, dst_ref=dst, send_sem=send, recv_sem=recv,
            device_id=(target,), device_id_type=MESH,
        )

    pending = []

    def send(condition, make):
        @pl.when(condition)
        def _():
            make().start()
        pending.append((condition, make))

    wide = 2 * STRIP
    tail = order - wide

    def upper(ref, s):
        a, b = strips[s]
        return ref.at[a:b, :wide] if s < 2 else ref.at[a:b, wide:]

    def whole(ref, s):
        a, b = strips[s]
        return ref.at[a:b, :]

    def wanted(k):
        final = group == top
        for b in range(k + 1, levels):
            final = final & (bits[b] == 1)
        return jnp.logical_not(final)

    def put(value, rows, columns):
        split(value, vh.at[rows, columns], vl.at[rows, columns])

    first, second, third = slice(0, STRIP), slice(STRIP, wide), slice(wide, order)

    def split_strip(ref, s):
        if s == 0:
            put(ref[first, :wide], first, slice(0, wide))
            put(ref[first, second].T, second, first)
        elif s == 1:
            put(ref[second, second], second, second)
            tails = ref[second, first]
            turned = tails.T
            put(tails[:, :tail], first, third)
            put(tails[:, tail:2 * tail], second, third)
            put(turned[:tail], third, first)
            put(turned[tail:2 * tail], third, second)
        else:
            put(ref[third, third], third, third)

    def fold_strip(o_in, out, s):
        a, b = strips[s]
        rows = (ph.at[a:b, :], pll.at[a:b, :])
        split(product(rows, (vh, vl), NN), wh.at[a:b, :], wl.at[a:b, :])
        term = product((wh.at[a:b, :], wl.at[a:b, :]), (ph.at[a:, :], pll.at[a:, :]), NT)

        def store(rows, columns, value):
            out[rows, columns] = value if o_in is None else o_in[rows, columns] + value

        if s == 0:
            store(first, slice(0, wide), term[:, :wide])
            store(second, slice(0, tail), term[:, wide:])
        elif s == 1:
            store(second, second, term[:, :STRIP])
            store(second, slice(tail, 2 * tail), term[:, STRIP:])
        else:
            store(third, third, term)

    def factor_strip(out, s):
        a, b = strips[s]
        out[a:b, :] = product((ph.at[a:b, :], pll.at[a:b, :]), (vh, vl), NN)

    def partner(k):
        return jnp.where(bits[k] == 0, me + (1 << k), me - (1 << k))

    def arrive(ref, send_sem, recv_sem):
        copy(ref, ref, send_sem, recv_sem, me).wait_recv()

    def arrive_factor(k):
        for s in range(count):
            arrive(whole(rp.at[k], s), p_send.at[k, 0, s], p_recv.at[k, s])

    def arrive_offset(k, s):
        arrive(upper(ro.at[k], s), o_send.at[k, 0, s], o_recv.at[k, s])

    def send_factor(k, s, src, condition):
        send(
            even & condition & ((bits[k] == 0) | wanted(k)),
            lambda: copy(whole(src, s), whole(rp.at[k], s), p_send.at[k, 0, s], p_recv.at[k, s], partner(k)),
        )

    def send_offset(k, s, src, condition):
        send(
            even & condition,
            lambda: copy(upper(src, s), upper(ro.at[k], s), o_send.at[k, 0, s], o_recv.at[k, s], partner(k)),
        )

    def send_on(s, src, condition):
        send(
            even & condition & (group > 0),
            lambda: copy(upper(src, s), upper(rx, s), x_send.at[0, s], x_recv.at[s], me - size),
        )

    g_ref[second, :tail] = g_ref[first, third]
    g_ref[second, tail:2 * tail] = g_ref[second, third]

    for s in range(count):
        send(odd, lambda s=s: copy(whole(l_ref, s), whole(rp.at[0], s), p_send.at[0, 0, s], p_recv.at[0, s], me - 1))
    for s in range(count):
        send(odd, lambda s=s: copy(upper(g_ref, s), upper(ro.at[0], s), o_send.at[0, 0, s], o_recv.at[0, s], me - 1))

    @pl.when(even)
    def _():
        split(l_ref[...], ph, pll)
        arrive_factor(0)
        split(rp[0], vh, vl)

    for s in range(count):
        @pl.when(even)
        def _(s=s):
            factor_strip(sp.at[0], s)

        send_factor(1, s, sp.at[0], me >= 0)

    @pl.when(even)
    def _():
        for s in range(count):
            arrive_offset(0, s)
            split_strip(ro.at[0], s)

    for s in range(count):
        @pl.when(even)
        def _(s=s):
            fold_strip(g_ref, so.at[0], s)

        send_offset(1, s, so.at[0], me >= 0)

    send(me < n - 1, lambda: copy(l_ref, prev, n_send, n_recv, me + 1))

    @pl.when(odd)
    def _():
        so[0] = g_ref[...]
        sp[0] = l_ref[...]

    def own_phase(k, condition):
        early, late = bits[k] == 0, bits[k] == 1
        needed = wanted(k)
        same = even
        for b in range(1, k + 1):
            same = same & (bits[b] == 0)
        fold = condition & early & jnp.logical_not(same)

        @pl.when(condition & late)
        def _():
            so[k] = so[k - 1]
            sp[k] = sp[k - 1]

        @pl.when(condition & same)
        def _():
            so[k] = to[k]

        @pl.when(condition & same & needed)
        def _():
            sp[k] = tp[k]

        @pl.when(fold)
        def _():
            split(sp[k - 1], ph, pll)

        @pl.when(odd & fold & needed)
        def _():
            arrive_factor(k)

        @pl.when(fold & needed)
        def _():
            split(rp[k], vh, vl)
            for s in range(count):
                factor_strip(sp.at[k], s)

        @pl.when(odd & fold)
        def _():
            for s in range(count):
                arrive_offset(k, s)

        @pl.when(fold)
        def _():
            for s in range(count):
                split_strip(ro.at[k], s)
            for s in range(count):
                fold_strip(so.at[k - 1], so.at[k], s)

    inner = rest & even & (group > 0)

    for k in range(1, levels):
        early, late = bits[k] == 0, bits[k] == 1
        t_o = so.at[0] if k == 1 else to.at[k - 1]
        t_p = sp.at[0] if k == 1 else tp.at[k - 1]
        final = k == levels - 1
        needed = wanted(k)

        for s in range(count):
            @pl.when(even & (late | needed))
            def _(s=s):
                arrive(whole(rp.at[k], s), p_send.at[k, 0, s], p_recv.at[k, s])

            send(
                even & early & needed,
                lambda k=k, s=s: copy(whole(rp.at[k], s), whole(rp.at[k], s), p_send.at[k, 1, s], p_recv.at[k, s], me + 1),
            )

        @pl.when(even & early)
        def _():
            split(t_p[...], ph, pll)

        @pl.when(even & early & needed)
        def _():
            split(rp[k], vh, vl)

        @pl.when(even & late)
        def _():
            split(rp[k], ph, pll)
            split(t_p[...], vh, vl)

        for s in range(count):
            @pl.when(even & needed)
            def _(s=s):
                factor_strip(tp.at[k], s)

            if not final:
                send_factor(k + 1, s, tp.at[k], needed)

        @pl.when(even & late)
        def _():
            for s in range(count):
                split_strip(t_o, s)
            for s in range(count):
                fold_strip(None, xc, s)

        for s in range(count):
            @pl.when(even)
            def _(s=s):
                arrive_offset(k, s)

            send(
                even & early,
                lambda k=k, s=s: copy(upper(ro.at[k], s), upper(ro.at[k], s), o_send.at[k, 1, s], o_recv.at[k, s], me + 1),
            )

            @pl.when(even & early)
            def _(s=s):
                split_strip(ro.at[k], s)

            @pl.when(even & late)
            def _(s=s):
                upper(to.at[k], s)[...] = upper(ro.at[k], s)[...] + upper(xc, s)[...]

            if final:
                send_on(s, to.at[k], late & (group == top))
            else:
                send_offset(k + 1, s, to.at[k], late)

        for s in range(count):
            @pl.when(even & early)
            def _(s=s):
                fold_strip(t_o, to.at[k], s)

            if final:
                send_on(s, to.at[k], early & (group == top))
            else:
                send_offset(k + 1, s, to.at[k], early)

        own_phase(k, jnp.logical_not(inner) if final else me >= 0)

    last = levels - 1

    @pl.when(inner)
    def _():
        split(tp[last], ph, pll)

    @pl.when(rest & jnp.logical_not(inner))
    def _():
        split(sp[last], ph, pll)

    for s in range(count):
        @pl.when(rest)
        def _(s=s):
            arrive(upper(rx, s), x_send.at[0, s], x_recv.at[s])

        send(rest & even, lambda s=s: copy(upper(rx, s), upper(rx, s), x_send.at[1, s], x_recv.at[s], me + 1))

        @pl.when(rest)
        def _(s=s):
            split_strip(rx, s)

    for s in range(count):
        @pl.when(inner)
        def _(s=s):
            fold_strip(to.at[last], xc, s)

        send_on(s, xc, rest)

    own_phase(last, inner)

    @pl.when(inner)
    def _():
        split(sp[last], ph, pll)
        for s in range(count):
            split_strip(rx, s)

    @pl.when(rest)
    def _():
        for s in range(count):
            fold_strip(so.at[last], xt, s)

    @pl.when(group == top)
    def _():
        xt[...] = so[last]

    x_ref[first, :wide] = xt[first, :wide]
    x_ref[second, first] = xt[first, second].T
    x_ref[second, second] = xt[second, second]
    tails = xt[second, first]
    turned = tails.T
    x_ref[first, third] = tails[:, :tail]
    x_ref[second, third] = tails[:, tail:2 * tail]
    x_ref[third, first] = turned[:tail]
    x_ref[third, second] = turned[tail:2 * tail]
    x_ref[third, third] = xt[third, third]

    @pl.when(me > 0)
    def _():
        copy(prev, prev, n_send, n_recv, me).wait_recv()
        q_ref[...] = prev[...]

    @pl.when(me == 0)
    def _():
        q_ref[...] = jnp.zeros_like(q_ref)

    for condition, make in pending:
        @pl.when(condition)
        def _(make=make):
            make().wait_send()


def finish(x_ref, q_ref, d_any, c_any, c_ref, xh, xl, qh, ql, sem):
    d_out = pltpu.make_async_copy(x_ref, d_any, sem.at[0])
    d_out.start()
    split(x_ref[...], xh, xl)
    split(q_ref[...], qh, ql)
    c_ref[...] = product((xh, xl), (qh, ql), NT)
    c_out = pltpu.make_async_copy(c_ref, c_any, sem.at[1])
    c_out.start()
    d_out.wait()
    c_out.wait()


def local(n, levels, schur_inverse, sweep_factor):
    order = schur_inverse.shape[1]
    full = (order, order)
    count = len(strips_of(order))
    f32, bf16 = jnp.float32, jnp.bfloat16
    dma = pltpu.SemaphoreType.DMA
    current, previous = pl.pallas_call(
        functools.partial(kernel, n, levels),
        out_shape=[pltpu.VMEM(full, f32)] * 2,
        in_specs=[pl.BlockSpec(memory_space=pl.ANY)] * 2,
        out_specs=[pl.BlockSpec(memory_space=pltpu.VMEM)] * 2,
        scratch_shapes=[
            pltpu.VMEM(full, f32),
            pltpu.VMEM(full, f32),
            pltpu.VMEM((levels,) + full, f32),
            pltpu.VMEM((levels,) + full, f32),
            pltpu.VMEM((levels,) + full, f32),
            pltpu.VMEM((levels,) + full, f32),
            pltpu.VMEM((levels,) + full, f32),
            pltpu.VMEM((levels,) + full, f32),
            pltpu.VMEM(full, f32),
            pltpu.VMEM(full, f32),
            pltpu.VMEM(full, f32),
            pltpu.VMEM(full, f32),
        ] + [pltpu.VMEM(full, bf16)] * 6 + [
            dma((levels, levels + 1, count)), dma((levels, count)),
            dma((levels, levels + 1, count)), dma((levels, count)),
            dma((2, count)), dma((count,)), dma, dma, dma((2,)),
        ],
        compiler_params=pltpu.CompilerParams(
            collective_id=0, has_side_effects=True
        ),
    )(schur_inverse[0], sweep_factor[0])
    diagonal, coupling = pl.pallas_call(
        finish,
        out_shape=[jax.ShapeDtypeStruct(full, f32)] * 2,
        in_specs=[pl.BlockSpec(memory_space=pltpu.VMEM)] * 2,
        out_specs=[pl.BlockSpec(memory_space=pl.ANY)] * 2,
        scratch_shapes=[pltpu.VMEM(full, f32)] + [pltpu.VMEM(full, bf16)] * 4 + [dma((2,))],
    )(*(pltpu.with_memory_space_constraint(v, pltpu.VMEM) for v in (current, previous)))
    return diagonal[None], coupling[None]


def solution(mesh):
    n = mesh.shape["tm"]
    levels = 0
    while levels < GROUP_LEVELS and n % (2 << levels) == 0:
        levels += 1
    return jax.shard_map(
        functools.partial(local, n, levels),
        mesh=mesh,
        in_specs=(P("tm", None, None), P("tm", None, None)),
        out_specs=(P("tm", None, None), P("tm", None, None)),
        check_vma=False,
    )
```

```python
import functools

import jax
import jax.numpy as jnp
from jax import lax
from jax.experimental import pallas as pl
from jax.experimental.pallas import tpu as pltpu
from jax.sharding import PartitionSpec as P

MESH = pl.DeviceIdType.MESH
STRIP = 128
WIDE = 2 * STRIP
GROUP = 8
NN = (((1,), (0,)), ((), ()))
NT = (((1,), (1,)), ((), ()))

OWN, PAIR, ALL, LAST, XF, YF, ZF, LOW = range(8)
CHAIN, EVEN, XO, YO, LOWO, EDGE, ZO, BASE = range(3, 11)
SL, SM, SC, SX, SY, SP, SA, SB, SR, SZ, SW = range(11)
DIAG, EDGE2 = 11, 12


def dot(left, right, dims):
    return lax.dot_general(left, right, dims, preferred_element_type=jnp.float32)


def split(value, high, low):
    top = value.astype(jnp.bfloat16)
    high[...] = top
    low[...] = (value - top.astype(jnp.float32)).astype(jnp.bfloat16)


def product(left, right, dims):
    lh, ll = left
    rh, rl = right
    return (
        dot(lh[...], rl[...], dims) + dot(ll[...], rh[...], dims)
    ) + dot(lh[...], rh[...], dims)


def kernel(n, g_any, l_any, x_ref, q_ref, *scratch):
    (g_ref, l_ref, other, prev, acc, pm, pt, so, high, low,
     p_send, p_recv, s_send, s_recv, l_send, l_recv, n_send, n_recv, in_sem, turn) = scratch
    order = g_ref.shape[0]
    half = order // 2
    tail = order - WIDE
    groups = n // GROUP
    joined = groups >= 3
    me = lax.axis_index("tm")
    j = lax.rem(me, GROUP)
    group = me // GROUP
    b0, b1, b2 = (lax.rem(j // d, 2) for d in (1, 2, 4))
    even, odd = b0 == 0, b0 == 1
    chip = j // 2
    xe, xl, ye, yl = b1 == 0, b1 == 1, b2 == 0, b2 == 1
    top = group == groups - 1
    rest = group < groups - 1
    bottom = (group == 0) & joined
    chain = rest & (group >= (2 if joined else 1))
    core = me + 1 - 2 * b0
    px = me + 2 - 4 * b1
    py = me + 4 - 8 * b2

    g_in = pltpu.make_async_copy(g_any, g_ref, in_sem.at[0])
    l_in = pltpu.make_async_copy(l_any, l_ref, in_sem.at[1])
    l_in.start()
    g_in.start()

    barrier = pltpu.get_barrier_semaphore()
    total = 0
    always = me >= 0
    for other_id, inside in (
        (core, always), (px, always), (py, always),
        (me + 2, odd & top & (chip == 1)), (me - 2, odd & top & (chip == 2)),
        (me - GROUP, group > 0), (me + GROUP, rest),
        (me - 2 * GROUP, odd & (group == 2)), (me + 2 * GROUP, odd & (group == 0) & (groups > 2)),
        (me - GROUP + 4, odd & top & ye & (group > 0)), (me + GROUP - 4, odd & yl & (group == groups - 2)),
        (me - 2 * GROUP + 4, odd & top & ye & (group == 2)),
        (me + 2 * GROUP - 4, odd & yl & (group == 0) & (groups == 3)),
        (me + 1, odd & (me < n - 1)), (me - 1, even & (me > 0)),
    ):
        total = total + inside.astype(jnp.int32)

        @pl.when(inside)
        def _(other_id=other_id):
            pl.semaphore_signal(barrier, inc=1, device_id=(other_id,), device_id_type=MESH)

    first, second, third = slice(0, STRIP), slice(STRIP, WIDE), slice(WIDE, order)
    left, right = slice(0, tail), slice(tail, 2 * tail)

    def slot(i, a=0, b=order):
        return high.at[i, a:b, :], low.at[i, a:b, :]

    def fill(i, value):
        split(value, *slot(i))

    def copy(src, dst, send, recv, target):
        return pltpu.make_async_remote_copy(
            src_ref=src, dst_ref=dst, send_sem=send, recv_sem=recv,
            device_id=(target,), device_id_type=MESH,
        )

    pending = []

    def send(condition, make, wait=True):
        @pl.when(condition)
        def _():
            make().start()
        if wait:
            pending.append((condition, make))

    def factor(i):
        return pm.at[i, :half, :WIDE], pm.at[i, half:, :WIDE], pt.at[i]

    def offset(i):
        return so.at[i, first, :], so.at[i, second, :]

    def send_factor(condition, src, dst, target, parts=(0, 1, 2), wait=True, sem=None):
        sem = dst if sem is None else sem
        for s in parts:
            send(
                condition,
                lambda s=s: copy(factor(src)[s], factor(dst)[s], p_send.at[sem, s], p_recv.at[dst, s], target),
                wait,
            )

    def sent_factor(condition, dst):
        @pl.when(condition)
        def _():
            for s in range(3):
                copy(factor(dst)[s], factor(dst)[s], p_send.at[dst, s], p_recv.at[dst, s], core).wait_send()

    def send_offset(condition, src, dst, target, parts=(0, 1), sem=None):
        sem = dst if sem is None else sem
        for s in parts:
            send(
                condition,
                lambda s=s: copy(offset(src)[s], offset(dst)[s], s_send.at[sem, s], s_recv.at[dst, s], target),
            )

    def got_factor(i):
        for s, ref in enumerate(factor(i)):
            copy(ref, ref, p_send.at[i, s], p_recv.at[i, s], me).wait_recv()

    def got_offset(i, s):
        ref = offset(i)[s]
        copy(ref, ref, s_send.at[i, s], s_recv.at[i, s], me).wait_recv()

    def got_offsets(i):
        got_offset(i, 0)
        got_offset(i, 1)

    def load_factor(i, k):
        h, l = high.at[k], low.at[k]
        split(pm[i, :, :WIDE], h.at[:, :WIDE], l.at[:, :WIDE])
        ends = pt[i]
        split(ends[:, :tail], h.at[:half, third], l.at[:half, third])
        split(ends[:, tail:2 * tail], h.at[half:, third], l.at[half:, third])

    def multiply(i, k, r, out, into=None):
        rows = slice(i * half, (i + 1) * half)
        value = product(slot(k, rows.start, rows.stop), slot(r), NN)
        if out is not None:
            pm[out, rows, :WIDE] = value[:, :WIDE]
            pt[out, :, i * tail:(i + 1) * tail] = value[:, third]
        if into is not None:
            split(value, *slot(into, rows.start, rows.stop))

    def pack(ref, i):
        so[i, first, :] = ref[first, :WIDE]
        so[i, second, left] = ref[first, third]
        so[i, second, right] = ref[second, third]
        so[i, STRIP:STRIP + tail, second] = ref[STRIP:STRIP + tail, second]
        so[i, STRIP + tail:WIDE, STRIP + tail:] = ref[STRIP + tail:WIDE, STRIP + tail:WIDE]
        so[i, STRIP + tail:WIDE, STRIP:STRIP + tail] = ref[third, third]

    def spread(i, put, parts=(0, 1)):
        if 0 in parts:
            put(so[i, first, :], first, slice(0, WIDE))
            put(so[i, first, second].T, second, first)
        if 1 in parts:
            ends = so[i, second, first]
            turned = ends.T
            put(ends[:, :tail], first, third)
            put(ends[:, tail:2 * tail], second, third)
            put(turned[:tail], third, first)
            put(turned[tail:2 * tail], third, second)
            block = so[i, second, second]
            lanes = lax.broadcasted_iota(jnp.int32, (STRIP - tail, STRIP), 1)
            put(block[:tail], slice(STRIP, STRIP + tail), second)
            put(jnp.where(lanes < tail, block.T[tail:], block[tail:]), slice(STRIP + tail, WIDE), second)
            put(block[tail:, :tail], third, third)

    def to_slot(k):
        def put(value, rows, columns):
            split(value, high.at[k, rows, columns], low.at[k, rows, columns])
        return put

    def to_ref(ref):
        def put(value, rows, columns):
            ref[rows, columns] = value
        return put

    def fold_strip(s, k, base, out):
        a, b = ((0, STRIP), (STRIP, order))[s]
        split(product(slot(k, a, b), slot(SZ), NN), *slot(SW, a, b))
        term = product(slot(SW, a, b), slot(k, a), NT)
        if s == 0:
            so[out, first, :] = so[base, first, :] + term[:, :WIDE]
            so[out, second, left] = so[base, second, left] + term[:, WIDE:]
        else:
            lower = slice(STRIP + tail, WIDE)
            so[out, second, right] = so[base, second, right] + term[:STRIP, STRIP:]
            so[out, STRIP:STRIP + tail, second] = so[base, STRIP:STRIP + tail, second] + term[:tail, :STRIP]
            so[out, lower, lower] = so[base, lower, lower] + term[tail:STRIP, tail:STRIP]
            so[out, lower, STRIP:STRIP + tail] = so[base, lower, STRIP:STRIP + tail] + term[STRIP:, STRIP:]

    def fold(condition, k, base, out, after=None):
        for s in range(2):
            @pl.when(condition)
            def _(s=s):
                fold_strip(s, k, base, out)
            if after is not None:
                after(s)

    def fold_whole(k, base, out):
        fill(SW, product(slot(k), slot(SZ), NN))
        out[...] = base[...] + product(slot(SW), slot(k), NT)

    l_in.wait()

    @pl.when(even)
    def _():
        fill(SL, l_ref[...])

    @pl.when(odd)
    def _():
        fill(SM, l_ref[...])

    g_in.wait()

    @pl.when(even)
    def _():
        pack(g_ref, BASE)

    @pl.when(odd)
    def _():
        fill(SZ, g_ref[...])

    pl.semaphore_wait(barrier, total)

    send(always, lambda: copy(l_ref, other, l_send, l_recv, core))
    send_offset(even, BASE, BASE, core)

    swap_x = even & (rest | ye)

    copy(other, other, l_send, l_recv, me).wait_recv()

    @pl.when(even)
    def _():
        fill(SM, other[...])

    for i in range(2):
        @pl.when(even)
        def _(i=i):
            multiply(i, SL, SM, OWN, SC)
        send_factor(swap_x, OWN, XF, px, (i,), wait=False)
    send_factor(swap_x, OWN, XF, px, (2,), wait=False)

    @pl.when(odd)
    def _():
        fill(SL, other[...])
        got_offsets(BASE)

    early_o = odd & top & ((chip == 1) | (chip == 3))
    fold(odd, SL, BASE, OWN, lambda s: send_offset(early_o, OWN, XO, px, (s,)))

    @pl.when(odd)
    def _():
        for i in range(2):
            multiply(i, SL, SM, None, SC)

    sent_factor(swap_x, XF)

    @pl.when(even & rest)
    def _():
        pl.semaphore_signal(turn.at[0], inc=1, device_id=(core,), device_id_type=MESH)

    @pl.when(odd & rest)
    def _():
        pl.semaphore_wait(turn.at[0], 1)

    send_offset(odd & rest, OWN, XO, px)

    @pl.when(swap_x)
    def _():
        got_factor(XF)

    send_factor(swap_x, XF, LOW, core)

    @pl.when(swap_x)
    def _():
        load_factor(XF, SX)

    def ordered(condition, early, k, r, a, b):
        @pl.when(condition & early)
        def _():
            high[a], low[a], high[b], low[b] = high[k], low[k], high[r], low[r]

        @pl.when(condition & jnp.logical_not(early))
        def _():
            high[a], low[a], high[b], low[b] = high[r], low[r], high[k], low[k]

    ordered(swap_x, xe, SC, SX, SA, SB)
    swap_y = even & rest
    for i in range(2):
        @pl.when(swap_x)
        def _(i=i):
            multiply(i, SA, SB, PAIR, SP)
        send_factor(swap_y, PAIR, YF, py, (i,), wait=False)
    send_factor(swap_y, PAIR, YF, py, (2,), wait=False)
    send_factor(swap_x & ye, PAIR, ZF, core)

    o_fold = odd & (rest | (chip == 0) | (chip == 2))

    @pl.when(odd & (rest | ye))
    def _():
        got_factor(LOW)
        load_factor(LOW, SX)

    @pl.when(o_fold)
    def _():
        got_offsets(XO)

    @pl.when(o_fold & xe)
    def _():
        spread(XO, to_slot(SZ))
        high[SA], low[SA] = high[SC], low[SC]
        so[BASE] = so[OWN]

    @pl.when(o_fold & xl)
    def _():
        spread(OWN, to_slot(SZ))
        high[SA], low[SA] = high[SX], low[SX]
        so[BASE] = so[XO]

    def after_pair(s):
        send_offset(odd & top & (chip == 2), PAIR, YO, py, (s,))
        send_offset(odd & top & (chip == 2), PAIR, YO, me - 2, (s,), DIAG)
        send_offset(odd & top & (chip == 0), PAIR, LOWO, px, (s,))

    fold(o_fold, SA, BASE, PAIR, after_pair)

    sent_factor(swap_y, YF)

    @pl.when(swap_y)
    def _():
        pl.semaphore_signal(turn.at[1], inc=1, device_id=(core,), device_id_type=MESH)

    @pl.when(odd & rest)
    def _():
        pl.semaphore_wait(turn.at[1], 1)

    send_offset(odd & rest, PAIR, YO, py)

    @pl.when(swap_y)
    def _():
        got_factor(YF)

    send_factor(swap_y & yl, YF, ZF, core)

    @pl.when(swap_y)
    def _():
        load_factor(YF, SY)

    ordered(swap_y, ye, SP, SY, SA, SB)
    down = even & (group == 1) & rest & joined
    for i in range(2):
        @pl.when(swap_y)
        def _(i=i):
            multiply(i, SA, SB, ALL, SR)
        send_factor(down, ALL, ZF, me - GROUP, (i,), sem=OWN)
    send_factor(down, ALL, ZF, me - GROUP, (2,), sem=OWN)
    send_factor(even & chain, ALL, ALL, core)

    @pl.when(swap_y & (chip == 0))
    def _():
        for i in range(2):
            multiply(i, SX, SY, None, SB)
        high[SA], low[SA] = high[SR], low[SR]

    @pl.when(swap_y & (chip == 1))
    def _():
        for i in range(2):
            multiply(i, SC, SY, None, SA)
        high[SB], low[SB] = high[SY], low[SY]

    @pl.when(swap_y & (chip == 2))
    def _():
        high[SA], low[SA] = high[SP], low[SP]
        high[SB], low[SB] = high[SX], low[SX]

    @pl.when(swap_y & (chip == 3))
    def _():
        high[SA], low[SA] = high[SC], low[SC]

    hand = swap_y & (chip < 3)

    @pl.when(hand)
    def _():
        for i in range(2):
            multiply(i, SM, SB, LAST)

    send_factor(hand, LAST, LAST, core)

    z_fold = odd & (rest | ye)

    @pl.when(z_fold)
    def _():
        got_factor(ZF)
        load_factor(ZF, SP)

    @pl.when(odd & top & (chip == 1))
    def _():
        got_offsets(LOWO)

    @pl.when(z_fold)
    def _():
        got_offsets(YO)

    @pl.when(odd & rest & yl)
    def _():
        spread(PAIR, to_slot(SZ))
        so[BASE] = so[YO]

    @pl.when(z_fold & ye)
    def _():
        spread(YO, to_slot(SZ))

    @pl.when(odd & ye & (rest | (chip == 0)))
    def _():
        so[BASE] = so[PAIR]

    @pl.when(odd & top & (chip == 1))
    def _():
        so[BASE] = so[LOWO]

    far = group == 2 if joined else me < 0
    near = (group >= 2) if joined else (group >= 1)

    def after_all(s):
        send_offset(odd & top & ye & near, ALL, EDGE, me - GROUP, (s,))
        send_offset(odd & top & ye & far, ALL, EDGE, me - 2 * GROUP, (s,), ZO)

    fold(z_fold, SP, BASE, ALL, after_all)
    send_offset(odd & top & ye & near, ALL, EDGE, me - GROUP + 4, (0, 1), EDGE2)
    send_offset(odd & top & ye & far, ALL, EDGE, me - 2 * GROUP + 4, (0, 1), DIAG)
    send_offset(odd & rest & (group == 1) & joined, ALL, ZO, me - GROUP)

    @pl.when(odd & chain)
    def _():
        got_factor(ALL)
        load_factor(ALL, SR)

    for s in range(2):
        @pl.when(odd & chain)
        def _(s=s):
            got_offset(EDGE, s)
        send_offset(odd & chain, EDGE, EDGE, core, (s,), CHAIN)

        @pl.when(odd & chain)
        def _(s=s):
            spread(EDGE, to_slot(SZ), (s,))

    def after_chain(s):
        send_offset(odd & chain & far, CHAIN, EDGE, me - 2 * GROUP, (s,), EDGE2)
        send_offset(odd & chain & near, CHAIN, EDGE, me - GROUP, (s,))

    fold(odd & chain, SR, ALL, CHAIN, after_chain)
    send(odd & (me < n - 1), lambda: copy(l_ref, prev, n_send, n_recv, me + 1))

    send_offset(odd & (chip == 0), ALL, EVEN, core)
    send_offset(odd & (chip == 2), PAIR, EVEN, core)
    send_offset(odd & (chip == 3), OWN, EVEN, core)
    low_y = odd & ye

    @pl.when(low_y)
    def _():
        spread(YO, to_slot(SZ))

    @pl.when(low_y & (chip == 1))
    def _():
        high[SA], low[SA] = high[SC], low[SC]
        so[BASE] = so[OWN]

    @pl.when(low_y & (chip == 0))
    def _():
        high[SA], low[SA] = high[SX], low[SX]
        so[BASE] = so[XO]

    fold(low_y, SA, BASE, EVEN)
    send_offset(odd & (chip == 1), EVEN, EVEN, core)

    @pl.when(odd & (chip == 0))
    def _():
        spread(EVEN, to_slot(SZ))

    @pl.when(odd & (chip == 1))
    def _():
        spread(YO, to_slot(SZ))

    @pl.when(odd & (chip == 2))
    def _():
        spread(XO, to_slot(SZ))

    @pl.when(odd & (chip < 3))
    def _():
        fold_whole(SM, g_ref, acc)

    @pl.when(odd & (chip == 3))
    def _():
        acc[...] = g_ref[...]

    @pl.when(odd & rest & (chip < 3))
    def _():
        got_factor(LAST)
        load_factor(LAST, SA)

    @pl.when(odd & rest & (chip == 3))
    def _():
        high[SA], low[SA] = high[SM], low[SM]

    @pl.when(even)
    def _():
        got_offsets(EVEN)
        spread(EVEN, to_ref(acc))

    @pl.when(bottom & even)
    def _():
        got_factor(ZF)

    send_factor(bottom & even, ZF, YF, core)

    @pl.when(bottom & even)
    def _():
        load_factor(ZF, SR)

    @pl.when(bottom & odd)
    def _():
        got_factor(YF)
        load_factor(YF, SR)

    @pl.when(bottom)
    def _():
        for i in range(2):
            multiply(i, SA, SR, None, SB)
        got_offsets(ZO)

    send_offset(bottom & odd, ZO, ZO, core)

    @pl.when(bottom)
    def _():
        spread(ZO, to_slot(SZ))
        fold_whole(SA, acc, acc)
        high[SA], low[SA] = high[SB], low[SB]

    @pl.when(odd)
    def _():
        q_ref[...] = other[...]

    @pl.when(even & (me > 0))
    def _():
        copy(prev, prev, n_send, n_recv, me).wait_recv()
        q_ref[...] = prev[...]

    @pl.when(me == 0)
    def _():
        q_ref[...] = jnp.zeros_like(q_ref)

    for s in range(2):
        @pl.when(rest & (even | jnp.logical_not(chain)))
        def _(s=s):
            got_offset(EDGE, s)

        send_offset(rest & odd & jnp.logical_not(chain), EDGE, EDGE, core, (s,), CHAIN)

        @pl.when(rest)
        def _(s=s):
            spread(EDGE, to_slot(SZ), (s,))

    @pl.when(rest)
    def _():
        fold_whole(SA, acc, x_ref)

    @pl.when(top)
    def _():
        x_ref[...] = acc[...]

    for condition, make in pending:
        @pl.when(condition)
        def _(make=make):
            make().wait_send()


def finish(x_ref, q_ref, d_any, c_any, c_ref, xh, xl, qh, ql, sem):
    d_out = pltpu.make_async_copy(x_ref, d_any, sem.at[0])
    d_out.start()
    split(x_ref[...], xh, xl)
    split(q_ref[...], qh, ql)
    c_ref[...] = product((xh, xl), (qh, ql), NT)
    c_out = pltpu.make_async_copy(c_ref, c_any, sem.at[1])
    c_out.start()
    d_out.wait()
    c_out.wait()


def local(n, schur_inverse, sweep_factor):
    order = schur_inverse.shape[1]
    full = (order, order)
    f32, bf16 = jnp.float32, jnp.bfloat16
    dma = pltpu.SemaphoreType.DMA
    current, previous = pl.pallas_call(
        functools.partial(kernel, n),
        out_shape=[pltpu.VMEM(full, f32)] * 2,
        in_specs=[pl.BlockSpec(memory_space=pl.ANY)] * 2,
        out_specs=[pl.BlockSpec(memory_space=pltpu.VMEM)] * 2,
        scratch_shapes=[pltpu.VMEM(full, f32)] * 5 + [
            pltpu.VMEM((8,) + full, f32),
            pltpu.VMEM((8, order // 2, STRIP), f32),
            pltpu.VMEM((11, WIDE, WIDE), f32),
            pltpu.VMEM((11,) + full, bf16),
            pltpu.VMEM((11,) + full, bf16),
            dma((8, 3)), dma((8, 3)), dma((13, 2)), dma((13, 2)),
            dma, dma, dma, dma, dma((2,)), pltpu.SemaphoreType.REGULAR((2,)),
        ],
        compiler_params=pltpu.CompilerParams(
            collective_id=0, has_side_effects=True
        ),
    )(schur_inverse[0], sweep_factor[0])
    diagonal, coupling = pl.pallas_call(
        finish,
        out_shape=[jax.ShapeDtypeStruct(full, f32)] * 2,
        in_specs=[pl.BlockSpec(memory_space=pltpu.VMEM)] * 2,
        out_specs=[pl.BlockSpec(memory_space=pl.ANY)] * 2,
        scratch_shapes=[pltpu.VMEM(full, f32)] + [pltpu.VMEM(full, bf16)] * 4 + [dma((2,))],
    )(*(pltpu.with_memory_space_constraint(v, pltpu.VMEM) for v in (current, previous)))
    return diagonal[None], coupling[None]


def solution(mesh):
    n = mesh.shape["tm"]
    return jax.shard_map(
        functools.partial(local, n),
        mesh=mesh,
        in_specs=(P("tm", None, None), P("tm", None, None)),
        out_specs=(P("tm", None, None), P("tm", None, None)),
        check_vma=False,
    )
```

```python
import functools

import jax
import jax.numpy as jnp
from jax import lax
from jax.experimental import pallas as pl
from jax.experimental.pallas import tpu as pltpu
from jax.sharding import PartitionSpec as P

MESH = pl.DeviceIdType.MESH
STRIP = 128
WIDE = 2 * STRIP
GROUP = 8
NN = (((1,), (0,)), ((), ()))
NT = (((1,), (1,)), ((), ()))

OWN, PAIR, ALL, LAST, XF, YF, ZF, LOW = range(8)
CHAIN, EVEN, XO, YO, EDGE, ZO, BASE = range(3, 10)
SL, SM, SC, SX, SY, SP, SA, SB, SR, SZ, SW = range(11)
E_BASE, E_X, E_X2, E_LOW, E_PAIR, E_Y, E_Y2, E_ALL, E_LAST = range(9)
O_X, O_Y, O_TO, O_NEAR, O_NEAR2, O_FAR, O_FAR2, O_Z, O_EVEN = range(9)
R_FACTOR = {XF: 0, YF: 1, ZF: 2, LOW: 0, ALL: 3, LAST: 4}
R_OFFSET = {BASE: 5, EVEN: 5, XO: 6, YO: 7, ZO: 8, EDGE: 9}
PARTS = 4


def dot(left, right, dims):
    return lax.dot_general(left, right, dims, preferred_element_type=jnp.float32)


def split(value, high, low):
    top = value.astype(jnp.bfloat16)
    high[...] = top
    low[...] = (value - top.astype(jnp.float32)).astype(jnp.bfloat16)


def product(left, right, dims):
    lh, ll = left
    rh, rl = right
    return (
        dot(lh[...], rl[...], dims) + dot(ll[...], rh[...], dims)
    ) + dot(lh[...], rh[...], dims)


def kernel(n, g_any, l_any, x_ref, q_ref, *scratch):
    (g_ref, l_ref, other, prev, acc, pm, pt, so, high, low, tally,
     sent, got, l_send, l_recv, n_send, n_recv, in_sem, turn) = scratch
    order = g_ref.shape[0]
    half = order // 2
    tail = order - WIDE
    groups = n // GROUP
    joined = groups >= 3
    me = lax.axis_index("tm")
    j = lax.rem(me, GROUP)
    group = me // GROUP
    b0, b1, b2 = (lax.rem(j // d, 2) for d in (1, 2, 4))
    even, odd = b0 == 0, b0 == 1
    chip = j // 2
    xe, xl, ye, yl = b1 == 0, b1 == 1, b2 == 0, b2 == 1
    top = group == groups - 1
    rest = group < groups - 1
    bottom = (group == 0) & joined
    chain = rest & (group >= (2 if joined else 1))
    core = me + 1 - 2 * b0
    px = me + 2 - 4 * b1
    py = me + 4 - 8 * b2

    g_in = pltpu.make_async_copy(g_any, g_ref, in_sem.at[0])
    l_in = pltpu.make_async_copy(l_any, l_ref, in_sem.at[1])
    l_in.start()
    g_in.start()

    barrier = pltpu.get_barrier_semaphore()
    total = 0
    always = me >= 0
    for other_id, inside in (
        (core, always), (px, always), (py, always),
        (me + 2, odd & top & (chip == 1)), (me - 2, odd & top & (chip == 2)),
        (me - GROUP, group > 0), (me + GROUP, rest),
        (me - 2 * GROUP, odd & (group == 2)), (me + 2 * GROUP, odd & (group == 0) & (groups > 2)),
        (me - GROUP + 4, odd & top & ye & (group > 0)), (me + GROUP - 4, odd & yl & (group == groups - 2)),
        (me - 2 * GROUP + 4, odd & top & ye & (group == 2)),
        (me + 2 * GROUP - 4, odd & yl & (group == 0) & (groups == 3)),
        (me + 1, odd & (me < n - 1)), (me - 1, even & (me > 0)),
    ):
        total = total + inside.astype(jnp.int32)

        @pl.when(inside)
        def _(other_id=other_id):
            pl.semaphore_signal(barrier, inc=1, device_id=(other_id,), device_id_type=MESH)

    first, second, third = slice(0, STRIP), slice(STRIP, WIDE), slice(WIDE, order)
    left, right = slice(0, tail), slice(tail, 2 * tail)

    def slot(i, a=0, b=order):
        return high.at[i, a:b, :], low.at[i, a:b, :]

    def fill(i, value):
        split(value, *slot(i))

    def copy(src, dst, send, recv, target):
        return pltpu.make_async_remote_copy(
            src_ref=src, dst_ref=dst, send_sem=send, recv_sem=recv,
            device_id=(target,), device_id_type=MESH,
        )

    pending = []

    def start(condition, make):
        @pl.when(condition)
        def _():
            make().start()

    def send(condition, make):
        start(condition, make)
        pending.append((condition, make))

    def drain():
        for condition, make in pending:
            @pl.when(condition)
            def _(make=make):
                make().wait_send()
        pending.clear()

    def factor(i):
        return pm.at[i, :half, :WIDE], pm.at[i, half:, :WIDE], pt.at[i]

    def quarter(s, count=1):
        return slice(s * WIDE // PARTS, (s + count) * WIDE // PARTS)

    def leave(condition, ref, sem):
        pending.append((condition, lambda: copy(ref, ref, sent.at[sem], got.at[0], core)))

    def send_factor(condition, src, dst, target, sem, parts=(0, 1, 2), ends=None):
        for s in parts:
            start(
                condition,
                lambda s=s: copy(
                    factor(src)[s], factor(dst)[s],
                    sent.at[ends if s == 2 and ends is not None else sem], got.at[R_FACTOR[dst]], target,
                ),
            )
        if 2 in parts and ends is None:
            leave(condition, tally, sem)

    def send_offset(condition, src, dst, target, sem, parts=range(PARTS), count=PARTS):
        for s in parts:
            start(
                condition,
                lambda s=s: copy(
                    so.at[src, quarter(s), :], so.at[dst, quarter(s), :],
                    sent.at[sem], got.at[R_OFFSET[dst] + (s if dst == EDGE else 0)], target,
                ),
            )
        if PARTS - 1 in parts:
            leave(condition, so.at[src, quarter(0, count), :], sem)

    def wait_sent(condition, ref, sem):
        @pl.when(condition)
        def _():
            copy(ref, ref, sent.at[sem], got.at[0], core).wait_send()

    def got_factor(i):
        copy(tally, tally, sent.at[0], got.at[R_FACTOR[i]], me).wait_recv()

    def got_offset(i):
        copy(so.at[i], so.at[i], sent.at[0], got.at[R_OFFSET[i]], me).wait_recv()

    def got_edge(s):
        ref = so.at[EDGE, quarter(s), :]
        copy(ref, ref, sent.at[0], got.at[R_OFFSET[EDGE] + s], me).wait_recv()

    def load_factor(i, k):
        h, l = high.at[k], low.at[k]
        split(pm[i, :, :WIDE], h.at[:, :WIDE], l.at[:, :WIDE])
        ends = pt[i]
        split(ends[:, :tail], h.at[:half, third], l.at[:half, third])
        split(ends[:, tail:2 * tail], h.at[half:, third], l.at[half:, third])

    def multiply(i, k, r, out, into=None):
        rows = slice(i * half, (i + 1) * half)
        value = product(slot(k, rows.start, rows.stop), slot(r), NN)
        if out is not None:
            pm[out, rows, :WIDE] = value[:, :WIDE]
            pt[out, :, i * tail:(i + 1) * tail] = value[:, third]
        if into is not None:
            split(value, *slot(into, rows.start, rows.stop))

    def pack(ref, i):
        so[i, first, :] = ref[first, :WIDE]
        so[i, second, left] = ref[first, third]
        so[i, second, right] = ref[second, third]
        so[i, STRIP:STRIP + tail, second] = ref[STRIP:STRIP + tail, second]
        so[i, STRIP + tail:WIDE, STRIP + tail:] = ref[STRIP + tail:WIDE, STRIP + tail:WIDE]
        so[i, STRIP + tail:WIDE, STRIP:STRIP + tail] = ref[third, third]

    def spread(i, put, parts=(0, 1)):
        if 0 in parts:
            put(so[i, first, :], first, slice(0, WIDE))
            put(so[i, first, second].T, second, first)
        if 1 in parts:
            ends = so[i, second, first]
            turned = ends.T
            put(ends[:, :tail], first, third)
            put(ends[:, tail:2 * tail], second, third)
            put(turned[:tail], third, first)
            put(turned[tail:2 * tail], third, second)
            block = so[i, second, second]
            lanes = lax.broadcasted_iota(jnp.int32, (STRIP - tail, STRIP), 1)
            put(block[:tail], slice(STRIP, STRIP + tail), second)
            put(jnp.where(lanes < tail, block.T[tail:], block[tail:]), slice(STRIP + tail, WIDE), second)
            put(block[tail:, :tail], third, third)

    def to_slot(k):
        def put(value, rows, columns):
            split(value, high.at[k, rows, columns], low.at[k, rows, columns])
        return put

    def to_ref(ref):
        def put(value, rows, columns):
            ref[rows, columns] = value
        return put

    def fold_left(s, k):
        a, b = ((0, STRIP), (STRIP, order))[s]
        split(product(slot(k, a, b), slot(SZ), NN), *slot(SW, a, b))

    def fold_right(s, k, base, out):
        a, b = ((0, STRIP), (STRIP, order))[s]
        term = product(slot(SW, a, b), slot(k, a), NT)
        if s == 0:
            so[out, first, :] = so[base, first, :] + term[:, :WIDE]
            so[out, second, left] = so[base, second, left] + term[:, WIDE:]
        else:
            lower = slice(STRIP + tail, WIDE)
            so[out, second, right] = so[base, second, right] + term[:STRIP, STRIP:]
            so[out, STRIP:STRIP + tail, second] = so[base, STRIP:STRIP + tail, second] + term[:tail, :STRIP]
            so[out, lower, lower] = so[base, lower, lower] + term[tail:STRIP, tail:STRIP]
            so[out, lower, STRIP:STRIP + tail] = so[base, lower, STRIP:STRIP + tail] + term[STRIP:, STRIP:]

    def fold(condition, k, base, out, after):
        for s in range(2):
            @pl.when(condition)
            def _(s=s):
                fold_left(s, k)
                fold_right(s, k, base, out)
            after(s)

    def fold_at_once(k, base, out):
        fold_left(0, k)
        fold_left(1, k)
        fold_right(0, k, base, out)
        fold_right(1, k, base, out)

    def fold_whole(k, base, out):
        for a in (0, half):
            split(product(slot(k, a, a + half), slot(SZ), NN), *slot(SW, a, a + half))
        for a in (0, half):
            out[a:a + half, :] = base[a:a + half, :] + product(slot(SW, a, a + half), slot(k), NT)

    l_in.wait()

    @pl.when(even)
    def _():
        fill(SL, l_ref[...])

    @pl.when(odd)
    def _():
        fill(SM, l_ref[...])

    g_in.wait()

    @pl.when(even)
    def _():
        pack(g_ref, BASE)

    @pl.when(odd)
    def _():
        fill(SZ, g_ref[...])

    pl.semaphore_wait(barrier, total)

    send(always, lambda: copy(l_ref, other, l_send, l_recv, core))
    send_offset(even, BASE, BASE, core, E_BASE)

    swap_x = even & (rest | ye)

    copy(other, other, l_send, l_recv, me).wait_recv()

    @pl.when(even)
    def _():
        fill(SM, other[...])

    for i in range(2):
        @pl.when(even)
        def _(i=i):
            multiply(i, SL, SM, OWN, SC)
        send_factor(swap_x, OWN, XF, px, E_X, (i,))
    send_factor(swap_x, OWN, XF, px, E_X, (2,), ends=E_X2)

    early_o = odd & top & (chip == 3)

    @pl.when(odd)
    def _():
        fill(SL, other[...])
        fold_left(0, SL)
        got_offset(BASE)
        fold_right(0, SL, BASE, OWN)

    send_offset(early_o, OWN, XO, px, O_X, (0, 1))

    @pl.when(odd)
    def _():
        fold_left(1, SL)
        fold_right(1, SL, BASE, OWN)

    send_offset(early_o, OWN, XO, px, O_X, (2, 3))

    @pl.when(odd)
    def _():
        for i in range(2):
            multiply(i, SL, SM, None, SC)

    turns = rest | ye
    wait_sent(swap_x, pm.at[OWN, :, :WIDE], E_X)

    @pl.when(swap_x)
    def _():
        pl.semaphore_signal(turn, inc=1, device_id=(core,), device_id_type=MESH)

    @pl.when(odd & turns)
    def _():
        pl.semaphore_wait(turn, 1)

    send_offset(odd & turns, OWN, XO, px, O_X)
    wait_sent(swap_x, pt.at[OWN], E_X2)

    @pl.when(swap_x)
    def _():
        got_factor(XF)

    send_factor(swap_x, XF, LOW, core, E_LOW)

    @pl.when(swap_x)
    def _():
        load_factor(XF, SX)

    def ordered(condition, early, k, r, a, b):
        @pl.when(condition & early)
        def _():
            high[a], low[a], high[b], low[b] = high[k], low[k], high[r], low[r]

        @pl.when(condition & jnp.logical_not(early))
        def _():
            high[a], low[a], high[b], low[b] = high[r], low[r], high[k], low[k]

    ordered(swap_x, xe, SC, SX, SA, SB)
    swap_y = even & rest
    for i in range(2):
        @pl.when(swap_x)
        def _(i=i):
            multiply(i, SA, SB, PAIR, SP)
        send_factor(swap_y, PAIR, YF, py, E_Y, (i,))
    send_factor(swap_y, PAIR, YF, py, E_Y, (2,), ends=E_Y2)
    send_factor(swap_x & ye, PAIR, ZF, core, E_PAIR)

    o_fold = odd & (rest | (chip < 3))

    def neighbour(condition):
        @pl.when(condition)
        def _():
            got_factor(LOW)
            load_factor(LOW, SX)

    neighbour(odd & turns & xl)

    @pl.when(o_fold)
    def _():
        got_offset(XO)

    @pl.when(o_fold & xe)
    def _():
        spread(XO, to_slot(SZ))
        high[SA], low[SA] = high[SC], low[SC]
        so[BASE] = so[OWN]

    @pl.when(o_fold & xl)
    def _():
        spread(OWN, to_slot(SZ))
        high[SA], low[SA] = high[SX], low[SX]
        so[BASE] = so[XO]

    def after_pair(s):
        parts = (2 * s, 2 * s + 1)
        send_offset(odd & top & (chip == 2), PAIR, YO, py, O_Y, parts)
        send_offset(odd & top & (chip == 2), PAIR, YO, me - 2, O_TO, parts)

    fold(o_fold, SA, BASE, PAIR, after_pair)
    neighbour(odd & turns & xe)

    wait_sent(swap_y, pm.at[PAIR, :, :WIDE], E_Y)

    @pl.when(swap_y)
    def _():
        pl.semaphore_signal(turn, inc=1, device_id=(core,), device_id_type=MESH)

    @pl.when(odd & rest)
    def _():
        pl.semaphore_wait(turn, 1)

    send_offset(odd & rest, PAIR, YO, py, O_Y)
    wait_sent(swap_y, pt.at[PAIR], E_Y2)

    @pl.when(swap_y)
    def _():
        got_factor(YF)

    send_factor(swap_y & yl, YF, ZF, core, E_PAIR)

    @pl.when(swap_y)
    def _():
        load_factor(YF, SY)

    ordered(swap_y, ye, SP, SY, SA, SB)
    down = even & (group == 1) & rest & joined
    for i in range(2):
        @pl.when(swap_y)
        def _(i=i):
            multiply(i, SA, SB, ALL, SR)
        send_factor(down, ALL, ZF, me - GROUP, E_ALL, (i,))
    send_factor(down, ALL, ZF, me - GROUP, E_ALL, (2,))
    send_factor(even & chain, ALL, ALL, core, E_ALL)

    @pl.when(swap_y & (chip == 0))
    def _():
        for i in range(2):
            multiply(i, SX, SY, None, SB)
        high[SA], low[SA] = high[SR], low[SR]

    @pl.when(swap_y & (chip == 1))
    def _():
        for i in range(2):
            multiply(i, SC, SY, None, SA)
        high[SB], low[SB] = high[SY], low[SY]

    @pl.when(swap_y & (chip == 2))
    def _():
        high[SA], low[SA] = high[SP], low[SP]
        high[SB], low[SB] = high[SX], low[SX]

    @pl.when(swap_y & (chip == 3))
    def _():
        high[SA], low[SA] = high[SC], low[SC]

    hand = swap_y & (chip < 3)

    @pl.when(hand)
    def _():
        for i in range(2):
            multiply(i, SM, SB, LAST)

    send_factor(hand, LAST, LAST, core, E_LAST)

    z_fold = odd & (rest | ye)

    @pl.when(z_fold)
    def _():
        got_factor(ZF)
        load_factor(ZF, SP)

    @pl.when(z_fold)
    def _():
        got_offset(YO)

    late = top | ((chip == 1) & (group == groups - 2))
    send(odd & jnp.logical_not(late), lambda: copy(l_ref, prev, n_send, n_recv, me + 1))

    @pl.when(odd & rest & yl)
    def _():
        spread(PAIR, to_slot(SZ))
        so[BASE] = so[YO]

    @pl.when(z_fold & ye)
    def _():
        spread(YO, to_slot(SZ))

    @pl.when(odd & ye)
    def _():
        so[BASE] = so[PAIR]

    far = group == 2 if joined else me < 0
    near = (group >= 2) if joined else (group >= 1)

    def after_all(s):
        parts = (2 * s, 2 * s + 1)
        send_offset(odd & top & ye & near, ALL, EDGE, me - GROUP, O_NEAR, parts)
        send_offset(odd & top & ye & far, ALL, EDGE, me - 2 * GROUP, O_FAR, parts[1 - s:], PARTS - 1)

    @pl.when(odd & rest)
    def _():
        fold_at_once(SP, BASE, ALL)

    fold(odd & top & ye, SP, BASE, ALL, after_all)
    send_offset(odd & top & ye & near, ALL, EDGE, me - GROUP + 4, O_NEAR2)
    send_offset(odd & top & ye & far, ALL, EDGE, me - 2 * GROUP + 4, O_FAR2, (1, 2, 3), PARTS - 1)
    send_offset(odd & rest & (group == 1) & joined, ALL, ZO, me - GROUP, O_Z)

    @pl.when(odd & chain)
    def _():
        got_factor(ALL)
        load_factor(ALL, SR)

    def take_edge(condition, hand_on, relay, s):
        for q in (2 * s, 2 * s + 1):
            @pl.when(condition)
            def _(q=q):
                got_edge(q)

            send_offset(hand_on, EDGE, EDGE, core, O_TO, (q,))
            if q == 0 and relay is not None:
                start(relay, lambda: copy(
                    so.at[EDGE, quarter(0), :], so.at[EDGE, quarter(0), :],
                    sent.at[O_FAR], got.at[R_OFFSET[EDGE]], me - GROUP,
                ))
                leave(relay, so.at[EDGE, quarter(0), :], O_FAR)

    for s in range(2):
        take_edge(odd & chain, odd & chain, None, s)

        @pl.when(odd & chain)
        def _(s=s):
            spread(EDGE, to_slot(SZ), (s,))

    def after_chain(s):
        to_near, to_far = odd & chain & near, odd & chain & far
        if s == 0:
            send_offset(to_near, CHAIN, EDGE, me - GROUP, O_NEAR, (0,))
            send_offset(to_far, CHAIN, EDGE, me - 2 * GROUP, O_FAR, (1,))
            send_offset(to_near & jnp.logical_not(far), CHAIN, EDGE, me - GROUP, O_NEAR, (1,))
        else:
            send_offset(to_far, CHAIN, EDGE, me - 2 * GROUP, O_FAR, (2, 3), PARTS - 1)
            send_offset(to_near & far, CHAIN, EDGE, me - GROUP, O_NEAR, (1,))
            send_offset(to_near, CHAIN, EDGE, me - GROUP, O_NEAR, (2, 3))

    fold(odd & chain, SR, ALL, CHAIN, after_chain)
    send(odd & late & (me < n - 1), lambda: copy(l_ref, prev, n_send, n_recv, me + 1))

    send_offset(odd & (chip == 0), ALL, EVEN, core, O_EVEN)
    send_offset(odd & (chip == 2), PAIR, EVEN, core, O_EVEN)
    send_offset(odd & (chip == 3), OWN, EVEN, core, O_EVEN)
    low_y = odd & ye

    @pl.when(low_y)
    def _():
        spread(YO, to_slot(SZ))

    @pl.when(low_y & (chip == 1))
    def _():
        high[SA], low[SA] = high[SC], low[SC]
        so[BASE] = so[OWN]

    @pl.when(low_y & (chip == 0))
    def _():
        high[SA], low[SA] = high[SX], low[SX]
        so[BASE] = so[XO]

    @pl.when(low_y)
    def _():
        fold_at_once(SA, BASE, EVEN)

    send_offset(odd & (chip == 1), EVEN, EVEN, core, O_EVEN)

    @pl.when(odd & (chip == 0))
    def _():
        spread(EVEN, to_slot(SZ))

    @pl.when(odd & (chip == 1))
    def _():
        spread(YO, to_slot(SZ))

    @pl.when(odd & (chip == 2))
    def _():
        spread(XO, to_slot(SZ))

    @pl.when(odd & (chip < 3))
    def _():
        fold_whole(SM, g_ref, acc)

    @pl.when(odd & (chip == 3))
    def _():
        acc[...] = g_ref[...]

    @pl.when(odd & rest & (chip < 3))
    def _():
        got_factor(LAST)
        load_factor(LAST, SA)

    @pl.when(odd & rest & (chip == 3))
    def _():
        high[SA], low[SA] = high[SM], low[SM]

    @pl.when(even)
    def _():
        got_offset(EVEN)
        spread(EVEN, to_ref(acc))

    @pl.when(bottom & even)
    def _():
        got_factor(ZF)

    send_factor(bottom & even, ZF, YF, core, E_ALL)

    @pl.when(bottom & even)
    def _():
        load_factor(ZF, SR)

    @pl.when(bottom & odd)
    def _():
        got_factor(YF)
        load_factor(YF, SR)

    @pl.when(bottom)
    def _():
        for i in range(2):
            multiply(i, SA, SR, None, SB)
        got_offset(ZO)

    send_offset(bottom & odd, ZO, ZO, core, O_Z)

    @pl.when(bottom)
    def _():
        spread(ZO, to_slot(SZ))
        fold_whole(SA, acc, acc)
        high[SA], low[SA] = high[SB], low[SB]

    @pl.when(odd)
    def _():
        q_ref[...] = other[...]

    @pl.when(even & (me > 0))
    def _():
        copy(prev, prev, n_send, n_recv, me).wait_recv()
        q_ref[...] = prev[...]

    @pl.when(me == 0)
    def _():
        q_ref[...] = jnp.zeros_like(q_ref)

    drain()

    apart = rest & jnp.logical_not(chain)
    for s in range(2):
        take_edge(
            rest & (even | jnp.logical_not(chain)), odd & apart,
            odd & (group == 1) & rest if joined else None, s,
        )

        @pl.when(rest)
        def _(s=s):
            spread(EDGE, to_slot(SZ), (s,))

    @pl.when(rest)
    def _():
        fold_whole(SA, acc, x_ref)

    @pl.when(top)
    def _():
        x_ref[...] = acc[...]

    drain()


def finish(x_ref, q_ref, d_any, c_any, c_ref, xh, xl, qh, ql, sem):
    d_out = pltpu.make_async_copy(x_ref, d_any, sem.at[0])
    d_out.start()
    split(q_ref[...], qh, ql)
    half = x_ref.shape[0] // 2
    copies = [d_out]
    for i in range(2):
        rows = slice(i * half, (i + 1) * half)
        split(x_ref[rows, :], xh.at[rows, :], xl.at[rows, :])
        c_ref[rows, :] = product((xh.at[rows, :], xl.at[rows, :]), (qh, ql), NT)
        copies.append(pltpu.make_async_copy(c_ref.at[rows, :], c_any.at[rows, :], sem.at[1 + i]))
        copies[-1].start()
    for c in copies:
        c.wait()


def local(n, schur_inverse, sweep_factor):
    order = schur_inverse.shape[1]
    full = (order, order)
    f32, bf16 = jnp.float32, jnp.bfloat16
    dma = pltpu.SemaphoreType.DMA
    current, previous = pl.pallas_call(
        functools.partial(kernel, n),
        out_shape=[pltpu.VMEM(full, f32)] * 2,
        in_specs=[pl.BlockSpec(memory_space=pl.ANY)] * 2,
        out_specs=[pl.BlockSpec(memory_space=pltpu.VMEM)] * 2,
        scratch_shapes=[pltpu.VMEM(full, f32)] * 5 + [
            pltpu.VMEM((8,) + full, f32),
            pltpu.VMEM((8, order // 2, STRIP), f32),
            pltpu.VMEM((10, WIDE, WIDE), f32),
            pltpu.VMEM((11,) + full, bf16),
            pltpu.VMEM((11,) + full, bf16),
            pltpu.VMEM((order * WIDE // STRIP + order // 2, STRIP), f32),
            dma((9,)), dma((9 + PARTS,)), dma, dma, dma, dma, dma((2,)), pltpu.SemaphoreType.REGULAR,
        ],
        compiler_params=pltpu.CompilerParams(
            collective_id=0, has_side_effects=True
        ),
    )(schur_inverse[0], sweep_factor[0])
    diagonal, coupling = pl.pallas_call(
        finish,
        out_shape=[jax.ShapeDtypeStruct(full, f32)] * 2,
        in_specs=[pl.BlockSpec(memory_space=pltpu.VMEM)] * 2,
        out_specs=[pl.BlockSpec(memory_space=pl.ANY)] * 2,
        scratch_shapes=[pltpu.VMEM(full, f32)] + [pltpu.VMEM(full, bf16)] * 4 + [dma((3,))],
    )(*(pltpu.with_memory_space_constraint(v, pltpu.VMEM) for v in (current, previous)))
    return diagonal[None], coupling[None]


def solution(mesh):
    n = mesh.shape["tm"]
    return jax.shard_map(
        functools.partial(local, n),
        mesh=mesh,
        in_specs=(P("tm", None, None), P("tm", None, None)),
        out_specs=(P("tm", None, None), P("tm", None, None)),
        check_vma=False,
    )
```

```python
import functools

import jax
import jax.numpy as jnp
from jax import lax
from jax.experimental import pallas as pl
from jax.experimental.pallas import tpu as pltpu
from jax.sharding import PartitionSpec as P

MESH = pl.DeviceIdType.MESH
STRIP = 128
WIDE = 2 * STRIP
GROUP = 8
NN = (((1,), (0,)), ((), ()))
NT = (((1,), (1,)), ((), ()))

OWN, PAIR, ALL, LAST, XF, YF, ZF, LOW = range(8)
CHAIN, EVEN, XO, YO, EDGE, ZO, BASE = range(3, 10)
SL, SM, SC, SX, SY, SP, SA, SB, SR, SZ, SW = range(11)
E_BASE, E_X, E_X2, E_LOW, E_PAIR, E_Y, E_Y2, E_ALL, E_LAST = range(9)
O_X, O_Y, O_TO, O_NEAR, O_NEAR2, O_FAR, O_FAR2, O_Z, O_EVEN = range(9)
R_FACTOR = {XF: 0, YF: 1, ZF: 2, LOW: 0, ALL: 3, LAST: 4}
R_OFFSET = {BASE: 5, EVEN: 5, XO: 6, YO: 7, ZO: 8, EDGE: 9}
R_ZF2 = 13
PARTS = 4


def dot(left, right, dims):
    return lax.dot_general(left, right, dims, preferred_element_type=jnp.float32)


def split(value, high, low):
    top = value.astype(jnp.bfloat16)
    high[...] = top
    low[...] = (value - top.astype(jnp.float32)).astype(jnp.bfloat16)


def product(left, right, dims):
    lh, ll = left
    rh, rl = right
    return (
        dot(lh[...], rl[...], dims) + dot(ll[...], rh[...], dims)
    ) + dot(lh[...], rh[...], dims)


def kernel(n, g_any, l_any, x_ref, q_ref, *scratch):
    (g_ref, l_ref, other, prev, acc, pm, pt, so, high, low, tally,
     sent, got, l_send, l_recv, n_send, n_recv, in_sem, turn) = scratch
    order = g_ref.shape[0]
    half = order // 2
    tail = order - WIDE
    groups = n // GROUP
    joined = groups >= 3
    me = lax.axis_index("tm")
    j = lax.rem(me, GROUP)
    group = me // GROUP
    b0, b1, b2 = (lax.rem(j // d, 2) for d in (1, 2, 4))
    even, odd = b0 == 0, b0 == 1
    chip = j // 2
    xe, xl, ye, yl = b1 == 0, b1 == 1, b2 == 0, b2 == 1
    top = group == groups - 1
    rest = group < groups - 1
    bottom = (group == 0) & joined
    chain = rest & (group >= (2 if joined else 1))
    core = me + 1 - 2 * b0
    px = me + 2 - 4 * b1
    py = me + 4 - 8 * b2

    g_in = pltpu.make_async_copy(g_any, g_ref, in_sem.at[0])
    l_in = pltpu.make_async_copy(l_any, l_ref, in_sem.at[1])
    l_in.start()
    g_in.start()

    barrier = pltpu.get_barrier_semaphore()
    total = 0
    always = me >= 0
    for other_id, inside in (
        (core, always), (px, always), (py, always),
        (me + 2, odd & top & (chip == 1)), (me - 2, odd & top & (chip == 2)),
        (me - GROUP, group > 0), (me + GROUP, rest),
        (me - 2 * GROUP, odd & (group == 2)), (me + 2 * GROUP, odd & (group == 0) & (groups > 2)),
        (me - GROUP + 4, odd & top & ye & (group > 0)), (me + GROUP - 4, odd & yl & (group == groups - 2)),
        (me - 2 * GROUP + 4, odd & top & ye & (group == 2)),
        (me + 2 * GROUP - 4, odd & yl & (group == 0) & (groups == 3)),
        (me + 1, odd & (me < n - 1)), (me - 1, even & (me > 0)),
    ):
        total = total + inside.astype(jnp.int32)

        @pl.when(inside)
        def _(other_id=other_id):
            pl.semaphore_signal(barrier, inc=1, device_id=(other_id,), device_id_type=MESH)

    first, second, third = slice(0, STRIP), slice(STRIP, WIDE), slice(WIDE, order)
    left, right = slice(0, tail), slice(tail, 2 * tail)

    def slot(i, a=0, b=order):
        return high.at[i, a:b, :], low.at[i, a:b, :]

    def fill(i, value):
        split(value, *slot(i))

    def copy(src, dst, send, recv, target):
        return pltpu.make_async_remote_copy(
            src_ref=src, dst_ref=dst, send_sem=send, recv_sem=recv,
            device_id=(target,), device_id_type=MESH,
        )

    pending = []

    def start(condition, make):
        @pl.when(condition)
        def _():
            make().start()

    def send(condition, make):
        start(condition, make)
        pending.append((condition, make))

    def drain():
        for condition, make in pending:
            @pl.when(condition)
            def _(make=make):
                make().wait_send()
        pending.clear()

    def factor(i):
        mid = half // 2
        return pm.at[i, :half, :WIDE], pm.at[i, half:, :WIDE], pt.at[i, :mid], pt.at[i, mid:]

    def quarter(s, count=1):
        return slice(s * WIDE // PARTS, (s + count) * WIDE // PARTS)

    half_tally = tally.at[:tally.shape[0] // 2, :]

    def leave(condition, ref, sem):
        pending.append((condition, lambda: copy(ref, ref, sent.at[sem], got.at[0], core)))

    def send_factor(condition, src, dst, target, sem, parts=(0, 1, 2, 3), ends=None, recv=None, last=3):
        for s in parts:
            start(
                condition,
                lambda s=s: copy(
                    factor(src)[s], factor(dst)[s],
                    sent.at[ends if s >= 2 and ends is not None else sem],
                    got.at[R_FACTOR[dst] if recv is None else recv], target,
                ),
            )
        if last in parts and ends is None:
            leave(condition, tally, sem)

    def send_offset(condition, src, dst, target, sem, parts=range(PARTS), count=PARTS, recv=None, last=PARTS - 1):
        for s in parts:
            start(
                condition,
                lambda s=s: copy(
                    so.at[src, quarter(s), :], so.at[dst, quarter(s), :],
                    sent.at[sem],
                    got.at[R_OFFSET[dst] + (s if dst == EDGE else 0) if recv is None else recv], target,
                ),
            )
        if last in parts:
            leave(condition, so.at[src, quarter(0, count), :], sem)

    def wait_sent(condition, ref, sem):
        @pl.when(condition)
        def _():
            copy(ref, ref, sent.at[sem], got.at[0], core).wait_send()

    def got_factor(i):
        copy(tally, tally, sent.at[0], got.at[R_FACTOR[i]], me).wait_recv()

    def got_offset(i):
        copy(so.at[i], so.at[i], sent.at[0], got.at[R_OFFSET[i]], me).wait_recv()

    def got_edge(s):
        ref = so.at[EDGE, quarter(s), :]
        copy(ref, ref, sent.at[0], got.at[R_OFFSET[EDGE] + s], me).wait_recv()

    def load_factor(i, k):
        h, l = high.at[k], low.at[k]
        split(pm[i, :, :WIDE], h.at[:, :WIDE], l.at[:, :WIDE])
        ends = pt[i]
        split(ends[:, :tail], h.at[:half, third], l.at[:half, third])
        split(ends[:, tail:2 * tail], h.at[half:, third], l.at[half:, third])

    def multiply(i, k, r, out, into=None):
        rows = slice(i * half, (i + 1) * half)
        value = product(slot(k, rows.start, rows.stop), slot(r), NN)
        if out is not None:
            pm[out, rows, :WIDE] = value[:, :WIDE]
            pt[out, :, i * tail:(i + 1) * tail] = value[:, third]
        if into is not None:
            split(value, *slot(into, rows.start, rows.stop))

    def pack(ref, i):
        so[i, first, :] = ref[first, :WIDE]
        so[i, second, left] = ref[first, third]
        so[i, second, right] = ref[second, third]
        so[i, STRIP:STRIP + tail, second] = ref[STRIP:STRIP + tail, second]
        so[i, STRIP + tail:WIDE, STRIP + tail:] = ref[STRIP + tail:WIDE, STRIP + tail:WIDE]
        so[i, STRIP + tail:WIDE, STRIP:STRIP + tail] = ref[third, third]

    def spread(i, put, parts=(0, 1)):
        if 0 in parts:
            put(so[i, first, :], first, slice(0, WIDE))
            put(so[i, first, second].T, second, first)
        if 1 in parts:
            ends = so[i, second, first]
            turned = ends.T
            put(ends[:, :tail], first, third)
            put(ends[:, tail:2 * tail], second, third)
            put(turned[:tail], third, first)
            put(turned[tail:2 * tail], third, second)
            block = so[i, second, second]
            lanes = lax.broadcasted_iota(jnp.int32, (STRIP - tail, STRIP), 1)
            put(block[:tail], slice(STRIP, STRIP + tail), second)
            put(jnp.where(lanes < tail, block.T[tail:], block[tail:]), slice(STRIP + tail, WIDE), second)
            put(block[tail:, :tail], third, third)

    def to_slot(k):
        def put(value, rows, columns):
            split(value, high.at[k, rows, columns], low.at[k, rows, columns])
        return put

    def to_ref(ref):
        def put(value, rows, columns):
            ref[rows, columns] = value
        return put

    def fold_left(s, k):
        a, b = ((0, STRIP), (STRIP, order))[s]
        split(product(slot(k, a, b), slot(SZ), NN), *slot(SW, a, b))

    def fold_right(s, k, base, out):
        a, b = ((0, STRIP), (STRIP, order))[s]
        term = product(slot(SW, a, b), slot(k, a), NT)
        if s == 0:
            so[out, first, :] = so[base, first, :] + term[:, :WIDE]
            so[out, second, left] = so[base, second, left] + term[:, WIDE:]
        else:
            lower = slice(STRIP + tail, WIDE)
            so[out, second, right] = so[base, second, right] + term[:STRIP, STRIP:]
            so[out, STRIP:STRIP + tail, second] = so[base, STRIP:STRIP + tail, second] + term[:tail, :STRIP]
            so[out, lower, lower] = so[base, lower, lower] + term[tail:STRIP, tail:STRIP]
            so[out, lower, STRIP:STRIP + tail] = so[base, lower, STRIP:STRIP + tail] + term[STRIP:, STRIP:]

    def fold(condition, k, base, out, after):
        for s in range(2):
            @pl.when(condition)
            def _(s=s):
                fold_left(s, k)
                fold_right(s, k, base, out)
            after(s)

    def fold_at_once(k, base, out):
        fold_left(0, k)
        fold_left(1, k)
        fold_right(0, k, base, out)
        fold_right(1, k, base, out)

    def fold_whole(k, base, out):
        for a in (0, half):
            split(product(slot(k, a, a + half), slot(SZ), NN), *slot(SW, a, a + half))
        for a in (0, half):
            out[a:a + half, :] = base[a:a + half, :] + product(slot(SW, a, a + half), slot(k), NT)

    l_in.wait()

    @pl.when(even)
    def _():
        fill(SL, l_ref[...])

    @pl.when(odd)
    def _():
        fill(SM, l_ref[...])

    g_in.wait()

    @pl.when(even)
    def _():
        pack(g_ref, BASE)

    @pl.when(odd)
    def _():
        fill(SZ, g_ref[...])

    pl.semaphore_wait(barrier, total)

    send(always, lambda: copy(l_ref, other, l_send, l_recv, core))
    send_offset(even, BASE, BASE, core, E_BASE)

    swap_x = even & (rest | ye)

    copy(other, other, l_send, l_recv, me).wait_recv()

    @pl.when(even)
    def _():
        fill(SM, other[...])

    for i in range(2):
        @pl.when(even)
        def _(i=i):
            multiply(i, SL, SM, OWN, SC)
        send_factor(swap_x, OWN, XF, px, E_X, (i,))
    send_factor(swap_x, OWN, XF, px, E_X, (2, 3), ends=E_X2)

    early_o = odd & top & (chip == 3)

    @pl.when(odd)
    def _():
        fill(SL, other[...])
        fold_left(0, SL)
        got_offset(BASE)
        fold_right(0, SL, BASE, OWN)

    send_offset(early_o, OWN, XO, px, O_X, (0, 1))

    @pl.when(odd)
    def _():
        fold_left(1, SL)
        fold_right(1, SL, BASE, OWN)

    send_offset(early_o, OWN, XO, px, O_X, (2, 3))

    @pl.when(odd)
    def _():
        for i in range(2):
            multiply(i, SL, SM, None, SC)

    turns = rest | ye
    wait_sent(swap_x, pm.at[OWN, :, :WIDE], E_X)

    @pl.when(swap_x)
    def _():
        pl.semaphore_signal(turn, inc=1, device_id=(core,), device_id_type=MESH)

    @pl.when(odd & turns)
    def _():
        pl.semaphore_wait(turn, 1)

    send_offset(odd & turns, OWN, XO, px, O_X)

    def send_coupling(condition):
        send(odd & condition & (me < n - 1), lambda: copy(l_ref, prev, n_send, n_recv, me + 1))

    soon = (rest & xe) | (bottom & (chip == 1)) | (top & (chip == 0))
    late = (top & (chip > 0)) | (jnp.logical_not(bottom) & (chip == 1) & (group == groups - 2))
    send_coupling(soon)
    leave(swap_x, pt.at[OWN], E_X2)

    @pl.when(swap_x)
    def _():
        got_factor(XF)

    send_factor(swap_x, XF, LOW, core, E_LOW)

    @pl.when(swap_x)
    def _():
        load_factor(XF, SX)

    def ordered(condition, early, k, r, a, b):
        @pl.when(condition & early)
        def _():
            high[a], low[a], high[b], low[b] = high[k], low[k], high[r], low[r]

        @pl.when(condition & jnp.logical_not(early))
        def _():
            high[a], low[a], high[b], low[b] = high[r], low[r], high[k], low[k]

    ordered(swap_x, xe, SC, SX, SA, SB)
    swap_y = even & rest
    tells = rest & jnp.logical_not(bottom & (chip == 0))
    hears = rest & jnp.logical_not(bottom & (chip == 2))
    for i in range(2):
        @pl.when(swap_x)
        def _(i=i):
            multiply(i, SA, SB, PAIR, SP)
        send_factor(even & tells, PAIR, YF, py, E_Y, (i,))
    send_factor(even & tells, PAIR, YF, py, E_Y, (2, 3), ends=E_Y2)
    send_factor(swap_x & ye, PAIR, ZF, core, E_PAIR)

    o_fold = odd & (rest | (chip < 3))

    def neighbour(condition):
        @pl.when(condition)
        def _():
            got_factor(LOW)
            load_factor(LOW, SX)

    neighbour(odd & turns & xl)

    @pl.when(o_fold)
    def _():
        got_offset(XO)

    @pl.when(o_fold & xe)
    def _():
        spread(XO, to_slot(SZ))
        high[SA], low[SA] = high[SC], low[SC]
        so[BASE] = so[OWN]

    @pl.when(o_fold & xl)
    def _():
        spread(OWN, to_slot(SZ))
        high[SA], low[SA] = high[SX], low[SX]
        so[BASE] = so[XO]

    def after_pair(s):
        parts = (2 * s, 2 * s + 1)
        send_offset(odd & top & (chip == 2), PAIR, YO, py, O_Y, parts)
        send_offset(odd & top & (chip == 2), PAIR, YO, me - 2, O_TO, parts)

    fold(o_fold, SA, BASE, PAIR, after_pair)
    neighbour(odd & turns & xe)

    wait_sent(even & tells, pm.at[PAIR, :, :WIDE], E_Y)

    @pl.when(swap_y)
    def _():
        pl.semaphore_signal(turn, inc=1, device_id=(core,), device_id_type=MESH)

    @pl.when(odd & rest)
    def _():
        pl.semaphore_wait(turn, 1)

    send_offset(odd & tells, PAIR, YO, py, O_Y)
    leave(even & tells, pt.at[PAIR], E_Y2)

    @pl.when(even & hears)
    def _():
        got_factor(YF)

    send_factor(even & hears & yl, YF, ZF, core, E_PAIR)

    @pl.when(even & hears)
    def _():
        load_factor(YF, SY)

    ordered(even & hears, ye, SP, SY, SA, SB)
    down = even & (group == 1) & rest & joined
    for i in range(2):
        @pl.when(even & hears)
        def _(i=i):
            multiply(i, SA, SB, ALL, SR)
        send_factor(down & (b1 == i), ALL, ZF, me - GROUP, E_ALL, (i,))
    for i in range(2):
        send_factor(down & (b1 == i), ALL, ZF, me - GROUP, E_ALL, (2 + i,), last=None)
    leave(down, half_tally, E_ALL)
    send_factor(even & chain, ALL, ALL, core, E_ALL)

    @pl.when(swap_y & (chip == 0))
    def _():
        for i in range(2):
            multiply(i, SX, SY, None, SB)
        high[SA], low[SA] = high[SR], low[SR]

    @pl.when(swap_y & (chip == 1))
    def _():
        for i in range(2):
            multiply(i, SC, SY, None, SA)
        high[SB], low[SB] = high[SY], low[SY]

    @pl.when(swap_y & (chip == 2))
    def _():
        high[SA], low[SA] = high[SP], low[SP]
        high[SB], low[SB] = high[SX], low[SX]

    @pl.when(swap_y & (chip == 3))
    def _():
        high[SA], low[SA] = high[SC], low[SC]

    hand = swap_y & (chip < 3)

    @pl.when(hand)
    def _():
        for i in range(2):
            multiply(i, SM, SB, LAST)

    send_factor(hand, LAST, LAST, core, E_LAST)

    z_fold = odd & (hears | (top & ye))

    @pl.when(z_fold)
    def _():
        got_factor(ZF)
        load_factor(ZF, SP)

    @pl.when(z_fold)
    def _():
        got_offset(YO)

    send_coupling(jnp.logical_not(soon | late))

    @pl.when(odd & hears & yl)
    def _():
        spread(PAIR, to_slot(SZ))
        so[BASE] = so[YO]

    @pl.when(z_fold & ye)
    def _():
        spread(YO, to_slot(SZ))

    @pl.when(odd & ye)
    def _():
        so[BASE] = so[PAIR]

    far = group == 2 if joined else me < 0
    near = (group >= 2) if joined else (group >= 1)

    def after_all(s):
        parts = (2 * s, 2 * s + 1)
        send_offset(odd & top & ye & near, ALL, EDGE, me - GROUP, O_NEAR, parts)
        send_offset(odd & top & ye & far, ALL, EDGE, me - 2 * GROUP, O_FAR, parts[1 - s:], PARTS - 1)

    @pl.when(odd & hears)
    def _():
        fold_at_once(SP, BASE, ALL)

    fold(odd & top & ye, SP, BASE, ALL, after_all)
    send_offset(odd & top & ye & near, ALL, EDGE, me - GROUP + 4, O_NEAR2)
    send_offset(odd & top & ye & far, ALL, EDGE, me - 2 * GROUP + 4, O_FAR2, (1, 2, 3), PARTS - 1)
    send_offset(odd & rest & (group == 1) & joined, ALL, ZO, me - GROUP, O_Z)

    @pl.when(odd & chain)
    def _():
        got_factor(ALL)
        load_factor(ALL, SR)

    def take_edge(condition, hand_on, relay, quarters):
        for q in quarters:
            @pl.when(condition)
            def _(q=q):
                got_edge(q)

            send_offset(hand_on, EDGE, EDGE, core, O_TO, (q,), last=None)
            if relay is not None:
                send_offset(relay, EDGE, EDGE, me - GROUP, O_FAR, (q,), 1, last=q)

    for s in range(2):
        take_edge(odd & chain, odd & chain, None, (2 * s, 2 * s + 1))

        @pl.when(odd & chain)
        def _(s=s):
            spread(EDGE, to_slot(SZ), (s,))

    leave(odd & chain, so.at[EDGE], O_TO)

    def after_chain(s):
        to_near, to_far = odd & chain & near, odd & chain & far
        if s == 0:
            send_offset(to_near, CHAIN, EDGE, me - GROUP, O_NEAR, (0,))
            send_offset(to_far, CHAIN, EDGE, me - 2 * GROUP, O_FAR, (1,))
            send_offset(to_near & jnp.logical_not(far), CHAIN, EDGE, me - GROUP, O_NEAR, (1,))
        else:
            send_offset(to_far, CHAIN, EDGE, me - 2 * GROUP, O_FAR, (2, 3), PARTS - 1)
            send_offset(to_near & far, CHAIN, EDGE, me - GROUP, O_NEAR, (1,))
            send_offset(to_near, CHAIN, EDGE, me - GROUP, O_NEAR, (2, 3))

    fold(odd & chain, SR, ALL, CHAIN, after_chain)
    send_coupling(late)

    send_offset(odd & (chip == 0), ALL, EVEN, core, O_EVEN)
    send_offset(odd & (chip == 2), PAIR, EVEN, core, O_EVEN)
    send_offset(odd & (chip == 3), OWN, EVEN, core, O_EVEN)
    low_y = odd & ye

    @pl.when(low_y)
    def _():
        spread(YO, to_slot(SZ))

    @pl.when(low_y & (chip == 1))
    def _():
        high[SA], low[SA] = high[SC], low[SC]
        so[BASE] = so[OWN]

    @pl.when(low_y & (chip == 0))
    def _():
        high[SA], low[SA] = high[SX], low[SX]
        so[BASE] = so[XO]

    @pl.when(low_y)
    def _():
        fold_at_once(SA, BASE, EVEN)

    send_offset(odd & (chip == 1), EVEN, EVEN, core, O_EVEN)

    @pl.when(odd & (chip == 0))
    def _():
        spread(EVEN, to_slot(SZ))

    @pl.when(odd & (chip == 1))
    def _():
        spread(YO, to_slot(SZ))

    @pl.when(odd & (chip == 2))
    def _():
        spread(XO, to_slot(SZ))

    @pl.when(odd & (chip < 3))
    def _():
        fold_whole(SM, g_ref, acc)

    @pl.when(odd & (chip == 3))
    def _():
        acc[...] = g_ref[...]

    @pl.when(odd & rest & (chip < 3))
    def _():
        got_factor(LAST)
        load_factor(LAST, SA)

    @pl.when(odd & rest & (chip == 3))
    def _():
        high[SA], low[SA] = high[SM], low[SM]

    @pl.when(bottom & even)
    def _():
        copy(half_tally, half_tally, sent.at[0], got.at[R_FACTOR[ZF]], me).wait_recv()

    for i in range(2):
        send_factor(bottom & even & (b1 == i), ZF, ZF, px, E_X, (i, 2 + i), recv=R_ZF2, last=None)
        send_factor(bottom & even & (b1 == i), ZF, YF, core, E_ALL, (i, 2 + i), last=None)
    leave(bottom & even, half_tally, E_X)

    @pl.when(even)
    def _():
        got_offset(EVEN)
        spread(EVEN, to_ref(acc))

    @pl.when(bottom & even)
    def _():
        copy(half_tally, half_tally, sent.at[0], got.at[R_ZF2], me).wait_recv()

    for i in range(2):
        send_factor(bottom & even & (b1 != i), ZF, YF, core, E_ALL, (i, 2 + i), last=None)
    leave(bottom & even, tally, E_ALL)

    @pl.when(bottom & odd)
    def _():
        got_offset(ZO)

    send_offset(bottom & odd, ZO, ZO, core, O_Z)

    @pl.when(bottom & even)
    def _():
        load_factor(ZF, SR)

    @pl.when(bottom & odd)
    def _():
        got_factor(YF)
        load_factor(YF, SR)

    @pl.when(odd)
    def _():
        q_ref[...] = other[...]

    @pl.when(even & (me > 0))
    def _():
        copy(prev, prev, n_send, n_recv, me).wait_recv()
        q_ref[...] = prev[...]

    @pl.when(me == 0)
    def _():
        q_ref[...] = jnp.zeros_like(q_ref)

    apart = odd & rest & jnp.logical_not(chain)
    waits = rest & (even | jnp.logical_not(chain))
    above = waits & jnp.logical_not(bottom)
    take_edge(above, apart & jnp.logical_not(bottom), odd & rest & (group == 1) if joined else None, (0,))
    drain()
    take_edge(above, apart & jnp.logical_not(bottom), None, (1,))

    @pl.when(rest & jnp.logical_not(bottom))
    def _():
        spread(EDGE, to_slot(SZ), (0,))

    take_edge(above, apart & jnp.logical_not(bottom), None, (2, 3))

    @pl.when(rest & jnp.logical_not(bottom))
    def _():
        spread(EDGE, to_slot(SZ), (1,))

    take_edge(bottom, apart & bottom, None, (1, 2, 3))

    @pl.when(bottom)
    def _():
        spread(EDGE, to_slot(SZ), (1,))

    take_edge(bottom, apart & bottom, None, (0,))
    leave(apart, so.at[EDGE], O_TO)

    @pl.when(bottom)
    def _():
        spread(EDGE, to_slot(SZ), (0,))
        fold_left(0, SR)
        fold_left(1, SR)

    @pl.when(bottom & even)
    def _():
        got_offset(ZO)

    @pl.when(bottom)
    def _():
        fold_right(0, SR, ZO, CHAIN)
        fold_right(1, SR, ZO, CHAIN)
        spread(CHAIN, to_slot(SZ))

    @pl.when(rest)
    def _():
        fold_whole(SA, acc, x_ref)

    @pl.when(top)
    def _():
        x_ref[...] = acc[...]

    drain()


def finish(x_ref, q_ref, d_any, c_any, c_ref, xh, xl, qh, ql, sem):
    d_out = pltpu.make_async_copy(x_ref, d_any, sem.at[0])
    d_out.start()
    split(q_ref[...], qh, ql)
    half = x_ref.shape[0] // 2
    copies = [d_out]
    for i in range(2):
        rows = slice(i * half, (i + 1) * half)
        split(x_ref[rows, :], xh.at[rows, :], xl.at[rows, :])
        c_ref[rows, :] = product((xh.at[rows, :], xl.at[rows, :]), (qh, ql), NT)
        copies.append(pltpu.make_async_copy(c_ref.at[rows, :], c_any.at[rows, :], sem.at[1 + i]))
        copies[-1].start()
    for c in copies:
        c.wait()


def local(n, schur_inverse, sweep_factor):
    order = schur_inverse.shape[1]
    full = (order, order)
    f32, bf16 = jnp.float32, jnp.bfloat16
    dma = pltpu.SemaphoreType.DMA
    current, previous = pl.pallas_call(
        functools.partial(kernel, n),
        out_shape=[pltpu.VMEM(full, f32)] * 2,
        in_specs=[pl.BlockSpec(memory_space=pl.ANY)] * 2,
        out_specs=[pl.BlockSpec(memory_space=pltpu.VMEM)] * 2,
        scratch_shapes=[pltpu.VMEM(full, f32)] * 5 + [
            pltpu.VMEM((8,) + full, f32),
            pltpu.VMEM((8, order // 2, STRIP), f32),
            pltpu.VMEM((10, WIDE, WIDE), f32),
            pltpu.VMEM((11,) + full, bf16),
            pltpu.VMEM((11,) + full, bf16),
            pltpu.VMEM((order * WIDE // STRIP + order // 2, STRIP), f32),
            dma((9,)), dma((10 + PARTS,)), dma, dma, dma, dma, dma((2,)), pltpu.SemaphoreType.REGULAR,
        ],
        compiler_params=pltpu.CompilerParams(
            collective_id=0, has_side_effects=True
        ),
    )(schur_inverse[0], sweep_factor[0])
    diagonal, coupling = pl.pallas_call(
        finish,
        out_shape=[jax.ShapeDtypeStruct(full, f32)] * 2,
        in_specs=[pl.BlockSpec(memory_space=pltpu.VMEM)] * 2,
        out_specs=[pl.BlockSpec(memory_space=pl.ANY)] * 2,
        scratch_shapes=[pltpu.VMEM(full, f32)] + [pltpu.VMEM(full, bf16)] * 4 + [dma((3,))],
    )(*(pltpu.with_memory_space_constraint(v, pltpu.VMEM) for v in (current, previous)))
    return diagonal[None], coupling[None]


def solution(mesh):
    n = mesh.shape["tm"]
    return jax.shard_map(
        functools.partial(local, n),
        mesh=mesh,
        in_specs=(P("tm", None, None), P("tm", None, None)),
        out_specs=(P("tm", None, None), P("tm", None, None)),
        check_vma=False,
    )
```

```python
import functools

import jax
import jax.numpy as jnp
from jax import lax
from jax.experimental import pallas as pl
from jax.experimental.pallas import tpu as pltpu
from jax.sharding import PartitionSpec as P

MESH = pl.DeviceIdType.MESH
STRIP = 128
WIDE = 2 * STRIP
GROUP = 8
NN = (((1,), (0,)), ((), ()))
NT = (((1,), (1,)), ((), ()))

OWN, PAIR, ALL, LAST, XF, YF, ZF, LOW = range(8)
CHAIN, EVEN, XO, YO, EDGE, ZO, BASE = range(3, 10)
SL, SM, SC, SX, SY, SP, SA, SB, SR, SZ, SW, SE, SV = range(13)
E_BASE, E_X, E_X2, E_LOW, E_PAIR, E_Y, E_Y2, E_ALL, E_LAST = range(9)
O_X, O_Y, O_TO, O_NEAR, O_NEAR2, O_FAR, O_FAR2, O_Z, O_EVEN = range(9)
R_FACTOR = {XF: 0, YF: 1, ZF: 2, LOW: 0, ALL: 3, LAST: 4}
R_OFFSET = {BASE: 5, EVEN: 5, XO: 6, YO: 7, ZO: 8, EDGE: 9}
R_ZF2 = 13
PARTS = 4


def dot(left, right, dims):
    return lax.dot_general(left, right, dims, preferred_element_type=jnp.float32)


def split(value, high, low):
    top = value.astype(jnp.bfloat16)
    high[...] = top
    low[...] = (value - top.astype(jnp.float32)).astype(jnp.bfloat16)


def product(left, right, dims):
    lh, ll = left
    rh, rl = right
    return (
        dot(lh[...], rl[...], dims) + dot(ll[...], rh[...], dims)
    ) + dot(lh[...], rh[...], dims)


def kernel(n, g_any, l_any, x_ref, q_ref, *scratch):
    (g_ref, l_ref, other, prev, acc, pm, pt, so, high, low, tally,
     sent, got, l_send, l_recv, n_send, n_recv, in_sem, turn) = scratch
    order = g_ref.shape[0]
    half = order // 2
    tail = order - WIDE
    groups = n // GROUP
    joined = groups >= 3
    me = lax.axis_index("tm")
    j = lax.rem(me, GROUP)
    group = me // GROUP
    b0, b1, b2 = (lax.rem(j // d, 2) for d in (1, 2, 4))
    even, odd = b0 == 0, b0 == 1
    chip = j // 2
    xe, xl, ye, yl = b1 == 0, b1 == 1, b2 == 0, b2 == 1
    top = group == groups - 1
    rest = group < groups - 1
    bottom = (group == 0) & joined
    chain = rest & (group >= (2 if joined else 1))
    core = me + 1 - 2 * b0
    px = me + 2 - 4 * b1
    py = me + 4 - 8 * b2

    g_in = pltpu.make_async_copy(g_any, g_ref, in_sem.at[0])
    l_in = pltpu.make_async_copy(l_any, l_ref, in_sem.at[1])
    l_in.start()
    g_in.start()

    barrier = pltpu.get_barrier_semaphore()
    total = 0
    always = me >= 0
    for other_id, inside in (
        (core, always), (px, always), (py, always),
        (me + 2, odd & top & (chip == 1)), (me - 2, odd & top & (chip == 2)),
        (me - GROUP, group > 0), (me + GROUP, rest),
        (me - 2 * GROUP, odd & (group == 2)), (me + 2 * GROUP, odd & (group == 0) & (groups > 2)),
        (me - GROUP + 4, odd & top & ye & (group > 0)), (me + GROUP - 4, odd & yl & (group == groups - 2)),
        (me - 2 * GROUP + 4, odd & top & ye & (group == 2)),
        (me + 2 * GROUP - 4, odd & yl & (group == 0) & (groups == 3)),
        (me + 1, odd & (me < n - 1)), (me - 1, even & (me > 0)),
    ):
        total = total + inside.astype(jnp.int32)

        @pl.when(inside)
        def _(other_id=other_id):
            pl.semaphore_signal(barrier, inc=1, device_id=(other_id,), device_id_type=MESH)

    first, second, third = slice(0, STRIP), slice(STRIP, WIDE), slice(WIDE, order)
    left, right = slice(0, tail), slice(tail, 2 * tail)

    def slot(i, a=0, b=order):
        return high.at[i, a:b, :], low.at[i, a:b, :]

    def fill(i, value):
        split(value, *slot(i))

    def copy(src, dst, send, recv, target):
        return pltpu.make_async_remote_copy(
            src_ref=src, dst_ref=dst, send_sem=send, recv_sem=recv,
            device_id=(target,), device_id_type=MESH,
        )

    pending = []

    def start(condition, make):
        @pl.when(condition)
        def _():
            make().start()

    def send(condition, make):
        start(condition, make)
        pending.append((condition, make))

    def drain():
        for condition, make in pending:
            @pl.when(condition)
            def _(make=make):
                make().wait_send()
        pending.clear()

    def factor(i):
        mid = half // 2
        return pm.at[i, :half, :WIDE], pm.at[i, half:, :WIDE], pt.at[i, :mid], pt.at[i, mid:]

    def quarter(s, count=1):
        return slice(s * WIDE // PARTS, (s + count) * WIDE // PARTS)

    half_tally = tally.at[:tally.shape[0] // 2, :]

    def leave(condition, ref, sem):
        pending.append((condition, lambda: copy(ref, ref, sent.at[sem], got.at[0], core)))

    def send_factor(condition, src, dst, target, sem, parts=(0, 1, 2, 3), ends=None, recv=None, last=3):
        for s in parts:
            start(
                condition,
                lambda s=s: copy(
                    factor(src)[s], factor(dst)[s],
                    sent.at[ends if s >= 2 and ends is not None else sem],
                    got.at[R_FACTOR[dst] if recv is None else recv], target,
                ),
            )
        if last in parts and ends is None:
            leave(condition, tally, sem)

    def send_offset(condition, src, dst, target, sem, parts=range(PARTS), count=PARTS, recv=None, last=PARTS - 1):
        for s in parts:
            start(
                condition,
                lambda s=s: copy(
                    so.at[src, quarter(s), :], so.at[dst, quarter(s), :],
                    sent.at[sem],
                    got.at[R_OFFSET[dst] + (s if dst == EDGE else 0) if recv is None else recv], target,
                ),
            )
        if last in parts:
            leave(condition, so.at[src, quarter(0, count), :], sem)

    def wait_sent(condition, ref, sem):
        @pl.when(condition)
        def _():
            copy(ref, ref, sent.at[sem], got.at[0], core).wait_send()

    def got_factor(i):
        copy(tally, tally, sent.at[0], got.at[R_FACTOR[i]], me).wait_recv()

    def got_offset(i):
        copy(so.at[i], so.at[i], sent.at[0], got.at[R_OFFSET[i]], me).wait_recv()

    def got_edge(s):
        ref = so.at[EDGE, quarter(s), :]
        copy(ref, ref, sent.at[0], got.at[R_OFFSET[EDGE] + s], me).wait_recv()

    def load_factor(i, k):
        h, l = high.at[k], low.at[k]
        split(pm[i, :, :WIDE], h.at[:, :WIDE], l.at[:, :WIDE])
        ends = pt[i]
        split(ends[:, :tail], h.at[:half, third], l.at[:half, third])
        split(ends[:, tail:2 * tail], h.at[half:, third], l.at[half:, third])

    def multiply(i, k, r, out, into=None):
        rows = slice(i * half, (i + 1) * half)
        value = product(slot(k, rows.start, rows.stop), slot(r), NN)
        if out is not None:
            pm[out, rows, :WIDE] = value[:, :WIDE]
            pt[out, :, i * tail:(i + 1) * tail] = value[:, third]
        if into is not None:
            split(value, *slot(into, rows.start, rows.stop))

    def pack(ref, i):
        so[i, first, :] = ref[first, :WIDE]
        so[i, second, left] = ref[first, third]
        so[i, second, right] = ref[second, third]
        so[i, STRIP:STRIP + tail, second] = ref[STRIP:STRIP + tail, second]
        so[i, STRIP + tail:WIDE, STRIP + tail:] = ref[STRIP + tail:WIDE, STRIP + tail:WIDE]
        so[i, STRIP + tail:WIDE, STRIP:STRIP + tail] = ref[third, third]

    def spread(i, put, parts=(0, 1)):
        if 0 in parts:
            put(so[i, first, :], first, slice(0, WIDE))
            put(so[i, first, second].T, second, first)
        if 1 in parts:
            ends = so[i, second, first]
            turned = ends.T
            put(ends[:, :tail], first, third)
            put(ends[:, tail:2 * tail], second, third)
            put(turned[:tail], third, first)
            put(turned[tail:2 * tail], third, second)
            block = so[i, second, second]
            lanes = lax.broadcasted_iota(jnp.int32, (STRIP - tail, STRIP), 1)
            put(block[:tail], slice(STRIP, STRIP + tail), second)
            put(jnp.where(lanes < tail, block.T[tail:], block[tail:]), slice(STRIP + tail, WIDE), second)
            put(block[tail:, :tail], third, third)

    def to_slot(k):
        def put(value, rows, columns):
            split(value, high.at[k, rows, columns], low.at[k, rows, columns])
        return put

    def to_ref(ref):
        def put(value, rows, columns):
            ref[rows, columns] = value
        return put

    def fold_left(s, k, z=SZ, w=SW):
        a, b = ((0, STRIP), (STRIP, order))[s]
        split(product(slot(k, a, b), slot(z), NN), *slot(w, a, b))

    def fold_right(s, k, base, out, w=SW):
        a, b = ((0, STRIP), (STRIP, order))[s]
        term = product(slot(w, a, b), slot(k, a), NT)
        if s == 0:
            so[out, first, :] = so[base, first, :] + term[:, :WIDE]
            so[out, second, left] = so[base, second, left] + term[:, WIDE:]
        else:
            lower = slice(STRIP + tail, WIDE)
            so[out, second, right] = so[base, second, right] + term[:STRIP, STRIP:]
            so[out, STRIP:STRIP + tail, second] = so[base, STRIP:STRIP + tail, second] + term[:tail, :STRIP]
            so[out, lower, lower] = so[base, lower, lower] + term[tail:STRIP, tail:STRIP]
            so[out, lower, STRIP:STRIP + tail] = so[base, lower, STRIP:STRIP + tail] + term[STRIP:, STRIP:]

    def fold(condition, k, base, out, after):
        for s in range(2):
            @pl.when(condition)
            def _(s=s):
                fold_left(s, k)
                fold_right(s, k, base, out)
            after(s)

    def fold_at_once(k, base, out):
        fold_left(0, k)
        fold_left(1, k)
        fold_right(0, k, base, out)
        fold_right(1, k, base, out)

    def fold_whole(k, base, out):
        for a in (0, half):
            split(product(slot(k, a, a + half), slot(SZ), NN), *slot(SW, a, a + half))
        for a in (0, half):
            out[a:a + half, :] = base[a:a + half, :] + product(slot(SW, a, a + half), slot(k), NT)

    l_in.wait()

    @pl.when(even)
    def _():
        fill(SL, l_ref[...])

    @pl.when(odd)
    def _():
        fill(SM, l_ref[...])

    g_in.wait()

    @pl.when(even)
    def _():
        pack(g_ref, BASE)

    @pl.when(odd)
    def _():
        fill(SZ, g_ref[...])

    pl.semaphore_wait(barrier, total)

    send(always, lambda: copy(l_ref, other, l_send, l_recv, core))
    send_offset(even, BASE, BASE, core, E_BASE)

    swap_x = even & (rest | ye)

    copy(other, other, l_send, l_recv, me).wait_recv()

    @pl.when(even)
    def _():
        fill(SM, other[...])

    for i in range(2):
        @pl.when(even)
        def _(i=i):
            multiply(i, SL, SM, OWN, SC)
        send_factor(swap_x, OWN, XF, px, E_X, (i,))
    send_factor(swap_x, OWN, XF, px, E_X, (2, 3), ends=E_X2)

    early_o = odd & top & (chip == 3)

    @pl.when(odd)
    def _():
        fill(SL, other[...])
        fold_left(0, SL)
        got_offset(BASE)
        fold_right(0, SL, BASE, OWN)

    send_offset(early_o, OWN, XO, px, O_X, (0, 1))

    @pl.when(odd)
    def _():
        fold_left(1, SL)
        fold_right(1, SL, BASE, OWN)

    send_offset(early_o, OWN, XO, px, O_X, (2, 3))

    @pl.when(odd)
    def _():
        for i in range(2):
            multiply(i, SL, SM, None, SC)

    turns = rest | ye
    wait_sent(swap_x, pm.at[OWN, :, :WIDE], E_X)

    @pl.when(swap_x)
    def _():
        pl.semaphore_signal(turn, inc=1, device_id=(core,), device_id_type=MESH)

    @pl.when(odd & turns)
    def _():
        pl.semaphore_wait(turn, 1)

    send_offset(odd & turns, OWN, XO, px, O_X)

    def send_coupling(condition):
        send(odd & condition & (me < n - 1), lambda: copy(l_ref, prev, n_send, n_recv, me + 1))

    soon = (rest & xe) | (bottom & (chip == 1)) | (top & (chip == 0))
    late = (top & (chip > 0)) | (jnp.logical_not(bottom) & (chip == 1) & (group == groups - 2))
    send_coupling(soon)
    leave(swap_x, pt.at[OWN], E_X2)

    @pl.when(swap_x)
    def _():
        got_factor(XF)

    send_factor(swap_x, XF, LOW, core, E_LOW)

    @pl.when(swap_x)
    def _():
        load_factor(XF, SX)

    def ordered(condition, early, k, r, a, b):
        @pl.when(condition & early)
        def _():
            high[a], low[a], high[b], low[b] = high[k], low[k], high[r], low[r]

        @pl.when(condition & jnp.logical_not(early))
        def _():
            high[a], low[a], high[b], low[b] = high[r], low[r], high[k], low[k]

    ordered(swap_x, xe, SC, SX, SA, SB)
    swap_y = even & rest
    tells = rest & jnp.logical_not(bottom & (chip == 0))
    hears = rest & jnp.logical_not(bottom & (chip == 2))
    for i in range(2):
        @pl.when(swap_x)
        def _(i=i):
            multiply(i, SA, SB, PAIR, SP)
        send_factor(even & tells, PAIR, YF, py, E_Y, (i,))
    send_factor(even & tells, PAIR, YF, py, E_Y, (2, 3), ends=E_Y2)
    send_factor(swap_x & ye, PAIR, ZF, core, E_PAIR)

    o_fold = odd & (rest | (chip < 3))

    def neighbour(condition):
        @pl.when(condition)
        def _():
            got_factor(LOW)
            load_factor(LOW, SX)

    neighbour(odd & turns & xl)

    @pl.when(o_fold)
    def _():
        got_offset(XO)

    @pl.when(o_fold & xe)
    def _():
        spread(XO, to_slot(SZ))
        high[SA], low[SA] = high[SC], low[SC]
        so[BASE] = so[OWN]

    @pl.when(o_fold & xl)
    def _():
        spread(OWN, to_slot(SZ))
        high[SA], low[SA] = high[SX], low[SX]
        so[BASE] = so[XO]

    def after_pair(s):
        parts = (2 * s, 2 * s + 1)
        send_offset(odd & top & (chip == 2), PAIR, YO, py, O_Y, parts)
        send_offset(odd & top & (chip == 2), PAIR, YO, me - 2, O_TO, parts)

    stepped = odd & top & (chip == 2)
    fold(stepped, SA, BASE, PAIR, after_pair)

    @pl.when(o_fold & jnp.logical_not(stepped))
    def _():
        fold_at_once(SA, BASE, PAIR)


    wait_sent(even & tells, pm.at[PAIR, :, :WIDE], E_Y)

    @pl.when(swap_y)
    def _():
        pl.semaphore_signal(turn, inc=1, device_id=(core,), device_id_type=MESH)

    @pl.when(odd & rest)
    def _():
        pl.semaphore_wait(turn, 1)

    send_offset(odd & tells, PAIR, YO, py, O_Y)
    leave(even & tells, pt.at[PAIR], E_Y2)

    @pl.when(even & hears)
    def _():
        got_factor(YF)

    send_factor(even & hears & yl, YF, ZF, core, E_PAIR)

    @pl.when(even & hears)
    def _():
        load_factor(YF, SY)

    ordered(even & hears, ye, SP, SY, SA, SB)
    down = even & (group == 1) & rest & joined
    for i in range(2):
        @pl.when(even & hears)
        def _(i=i):
            multiply(i, SA, SB, ALL, SR)
        send_factor(down & (b1 == i), ALL, ZF, me - GROUP, E_ALL, (i,))
    for i in range(2):
        send_factor(down & (b1 == i), ALL, ZF, me - GROUP, E_ALL, (2 + i,), last=None)
    leave(down, half_tally, E_ALL)
    send_factor(even & chain, ALL, ALL, core, E_ALL)

    @pl.when(swap_y & (chip == 0))
    def _():
        for i in range(2):
            multiply(i, SX, SY, None, SB)
        high[SA], low[SA] = high[SR], low[SR]

    @pl.when(swap_y & (chip == 1))
    def _():
        for i in range(2):
            multiply(i, SC, SY, None, SA)
        high[SB], low[SB] = high[SY], low[SY]

    @pl.when(swap_y & (chip == 2))
    def _():
        high[SA], low[SA] = high[SP], low[SP]
        high[SB], low[SB] = high[SX], low[SX]

    @pl.when(swap_y & (chip == 3))
    def _():
        high[SA], low[SA] = high[SC], low[SC]

    hand = swap_y & (chip < 3)

    @pl.when(hand)
    def _():
        for i in range(2):
            multiply(i, SM, SB, LAST)

    send_factor(hand, LAST, LAST, core, E_LAST)

    z_fold = odd & (hears | (top & ye))

    @pl.when(z_fold)
    def _():
        got_factor(ZF)
        load_factor(ZF, SP)

    sharing = groups >= 4
    hands = odd & ye & (group == groups - 2) & sharing
    passes = odd & top & yl & sharing
    for q in range(PARTS // 2):
        @pl.when(passes)
        def _(q=q):
            got_edge(q)

        send_offset(passes, EDGE, EDGE, me - GROUP, O_NEAR, (q,), PARTS // 2, last=1)

    @pl.when(z_fold)
    def _():
        got_offset(YO)

    send_coupling(jnp.logical_not(soon | late))

    @pl.when(odd & hears & yl)
    def _():
        spread(PAIR, to_slot(SZ))
        so[BASE] = so[YO]

    @pl.when(z_fold & ye)
    def _():
        spread(YO, to_slot(SZ))

    @pl.when(odd & ye)
    def _():
        so[BASE] = so[PAIR]

    far = group == 2 if joined else me < 0
    near = (group >= 2) if joined else (group >= 1)

    shared = (2, 3) if sharing else range(PARTS)

    def after_all(s):
        parts = (2 * s, 2 * s + 1)
        send_offset(odd & top & ye & near, ALL, EDGE, me - GROUP, O_NEAR, parts)
        send_offset(odd & top & ye & far, ALL, EDGE, me - 2 * GROUP, O_FAR, parts)
        if s == 0:
            send_offset(odd & top & ye & sharing, ALL, EDGE, py, O_TO, parts, PARTS // 2, last=1)
        else:
            send_offset(odd & top & ye & near, ALL, EDGE, me - GROUP + 4, O_NEAR2, shared, len(shared))

    @pl.when(odd & hears & jnp.logical_not(hands))
    def _():
        fold_at_once(SP, BASE, ALL)

    fold(odd & top & ye, SP, BASE, ALL, after_all)
    send_offset(odd & top & ye & far, ALL, EDGE, me - 2 * GROUP + 4, O_FAR2)
    send_offset(odd & rest & (group == 1) & joined, ALL, ZO, me - GROUP, O_Z)

    @pl.when(odd & chain)
    def _():
        got_factor(ALL)
        load_factor(ALL, SR)

    def take_edge(condition, hand_on, quarters):
        for q in quarters:
            @pl.when(condition)
            def _(q=q):
                got_edge(q)

            send_offset(hand_on, EDGE, EDGE, core, O_TO, (q,), last=None)

    alone = odd & chain & jnp.logical_not(hands)
    for s in range(2):
        take_edge(odd & chain, odd & chain, (2 * s, 2 * s + 1))

        @pl.when(odd & chain)
        def _(s=s):
            spread(EDGE, to_slot(SE), (s,))

    leave(odd & chain, so.at[EDGE], O_TO)

    def after_chain(condition, s):
        to_near, to_far = condition & near, condition & far
        parts = (2 * s, 2 * s + 1)
        send_offset(to_far, CHAIN, EDGE, me - 2 * GROUP, O_FAR, parts)
        send_offset(to_near & jnp.logical_not(far), CHAIN, EDGE, me - GROUP, O_NEAR, parts)
        if s == 1:
            send_offset(to_near & far, CHAIN, EDGE, me - GROUP, O_NEAR2)

    for s in range(2):
        @pl.when(hands)
        def _(s=s):
            fold_left(s, SR, SE, SV)
            fold_left(s, SP)
            fold_right(s, SP, BASE, ALL)
            fold_right(s, SR, ALL, CHAIN, SV)

        after_chain(hands, s)

    for s in range(2):
        @pl.when(alone)
        def _(s=s):
            fold_left(s, SR, SE)
            fold_right(s, SR, ALL, CHAIN)

        after_chain(alone, s)

    neighbour(odd & turns & xe)
    send_coupling(late)

    send_offset(odd & (chip == 0), ALL, EVEN, core, O_EVEN)
    send_offset(odd & (chip == 2), PAIR, EVEN, core, O_EVEN)
    send_offset(odd & (chip == 3), OWN, EVEN, core, O_EVEN)
    low_y = odd & ye

    @pl.when(low_y)
    def _():
        spread(YO, to_slot(SZ))

    @pl.when(low_y & (chip == 1))
    def _():
        high[SA], low[SA] = high[SC], low[SC]
        so[BASE] = so[OWN]

    @pl.when(low_y & (chip == 0))
    def _():
        high[SA], low[SA] = high[SX], low[SX]
        so[BASE] = so[XO]

    @pl.when(low_y)
    def _():
        fold_at_once(SA, BASE, EVEN)

    send_offset(odd & (chip == 1), EVEN, EVEN, core, O_EVEN)

    @pl.when(odd & (chip == 0))
    def _():
        spread(EVEN, to_slot(SZ))

    @pl.when(odd & (chip == 1))
    def _():
        spread(YO, to_slot(SZ))

    @pl.when(odd & (chip == 2))
    def _():
        spread(XO, to_slot(SZ))

    @pl.when(odd & (chip < 3))
    def _():
        fold_whole(SM, g_ref, acc)

    @pl.when(odd & (chip == 3))
    def _():
        acc[...] = g_ref[...]

    @pl.when(odd & rest & (chip < 3))
    def _():
        got_factor(LAST)
        load_factor(LAST, SA)

    @pl.when(odd & rest & (chip == 3))
    def _():
        high[SA], low[SA] = high[SM], low[SM]

    @pl.when(bottom & even)
    def _():
        copy(half_tally, half_tally, sent.at[0], got.at[R_FACTOR[ZF]], me).wait_recv()

    for i in range(2):
        send_factor(bottom & even & (b1 == i), ZF, ZF, px, E_X, (i, 2 + i), recv=R_ZF2, last=None)
        send_factor(bottom & even & (b1 == i), ZF, YF, core, E_ALL, (i, 2 + i), last=None)
    leave(bottom & even, half_tally, E_X)

    @pl.when(even)
    def _():
        got_offset(EVEN)
        spread(EVEN, to_ref(acc))

    @pl.when(bottom & even)
    def _():
        copy(half_tally, half_tally, sent.at[0], got.at[R_ZF2], me).wait_recv()

    for i in range(2):
        send_factor(bottom & even & (b1 != i), ZF, YF, core, E_ALL, (i, 2 + i), last=None)
    leave(bottom & even, tally, E_ALL)

    @pl.when(bottom & even)
    def _():
        load_factor(ZF, SR)

    @pl.when(odd)
    def _():
        q_ref[...] = other[...]

    @pl.when(even & (me > 0))
    def _():
        copy(prev, prev, n_send, n_recv, me).wait_recv()
        q_ref[...] = prev[...]

    @pl.when(me == 0)
    def _():
        q_ref[...] = jnp.zeros_like(q_ref)

    apart = odd & rest & jnp.logical_not(chain)
    waits = rest & (even | jnp.logical_not(chain))
    drain()
    for s in range(2):
        take_edge(waits, apart, (2 * s, 2 * s + 1))

        @pl.when(rest)
        def _(s=s):
            spread(EDGE, to_slot(SZ), (s,))

    leave(apart, so.at[EDGE], O_TO)

    @pl.when(bottom & odd)
    def _():
        got_offset(ZO)

    send_offset(bottom & odd, ZO, ZO, core, O_Z)

    @pl.when(bottom & odd)
    def _():
        got_factor(YF)
        load_factor(YF, SR)

    @pl.when(bottom)
    def _():
        fold_left(0, SR)
        fold_left(1, SR)

    @pl.when(bottom & even)
    def _():
        got_offset(ZO)

    @pl.when(bottom)
    def _():
        fold_right(0, SR, ZO, CHAIN)
        fold_right(1, SR, ZO, CHAIN)
        spread(CHAIN, to_slot(SZ))

    @pl.when(rest)
    def _():
        fold_whole(SA, acc, x_ref)

    @pl.when(top)
    def _():
        x_ref[...] = acc[...]

    drain()


def finish(x_ref, q_ref, d_any, c_any, c_ref, xh, xl, qh, ql, sem):
    d_out = pltpu.make_async_copy(x_ref, d_any, sem.at[0])
    d_out.start()
    split(q_ref[...], qh, ql)
    half = x_ref.shape[0] // 2
    copies = [d_out]
    for i in range(2):
        rows = slice(i * half, (i + 1) * half)
        split(x_ref[rows, :], xh.at[rows, :], xl.at[rows, :])
        c_ref[rows, :] = product((xh.at[rows, :], xl.at[rows, :]), (qh, ql), NT)
        copies.append(pltpu.make_async_copy(c_ref.at[rows, :], c_any.at[rows, :], sem.at[1 + i]))
        copies[-1].start()
    for c in copies:
        c.wait()


def local(n, schur_inverse, sweep_factor):
    order = schur_inverse.shape[1]
    full = (order, order)
    f32, bf16 = jnp.float32, jnp.bfloat16
    dma = pltpu.SemaphoreType.DMA
    current, previous = pl.pallas_call(
        functools.partial(kernel, n),
        out_shape=[pltpu.VMEM(full, f32)] * 2,
        in_specs=[pl.BlockSpec(memory_space=pl.ANY)] * 2,
        out_specs=[pl.BlockSpec(memory_space=pltpu.VMEM)] * 2,
        scratch_shapes=[pltpu.VMEM(full, f32)] * 5 + [
            pltpu.VMEM((8,) + full, f32),
            pltpu.VMEM((8, order // 2, STRIP), f32),
            pltpu.VMEM((10, WIDE, WIDE), f32),
            pltpu.VMEM((13,) + full, bf16),
            pltpu.VMEM((13,) + full, bf16),
            pltpu.VMEM((order * WIDE // STRIP + order // 2, STRIP), f32),
            dma((9,)), dma((10 + PARTS,)), dma, dma, dma, dma, dma((2,)), pltpu.SemaphoreType.REGULAR,
        ],
        compiler_params=pltpu.CompilerParams(
            collective_id=0, has_side_effects=True
        ),
    )(schur_inverse[0], sweep_factor[0])
    diagonal, coupling = pl.pallas_call(
        finish,
        out_shape=[jax.ShapeDtypeStruct(full, f32)] * 2,
        in_specs=[pl.BlockSpec(memory_space=pltpu.VMEM)] * 2,
        out_specs=[pl.BlockSpec(memory_space=pl.ANY)] * 2,
        scratch_shapes=[pltpu.VMEM(full, f32)] + [pltpu.VMEM(full, bf16)] * 4 + [dma((3,))],
    )(*(pltpu.with_memory_space_constraint(v, pltpu.VMEM) for v in (current, previous)))
    return diagonal[None], coupling[None]


def solution(mesh):
    n = mesh.shape["tm"]
    return jax.shard_map(
        functools.partial(local, n),
        mesh=mesh,
        in_specs=(P("tm", None, None), P("tm", None, None)),
        out_specs=(P("tm", None, None), P("tm", None, None)),
        check_vma=False,
    )
```

```python
import functools

import jax
import jax.numpy as jnp
from jax import lax
from jax.experimental import pallas as pl
from jax.experimental.pallas import tpu as pltpu
from jax.sharding import PartitionSpec as P

MESH = pl.DeviceIdType.MESH
STRIP = 128
WIDE = 2 * STRIP
GROUP = 8
NN = (((1,), (0,)), ((), ()))
NT = (((1,), (1,)), ((), ()))

OWN, PAIR, ALL, LAST, XF, YF, ZF, LOW = range(8)
CHAIN, EVEN, XO, YO, EDGE, ZO, BASE = range(3, 10)
SL, SM, SC, SX, SY, SP, SA, SB, SR, SZ, SW, SE, SV = range(13)
E_BASE, E_X, E_X2, E_LOW, E_PAIR, E_Y, E_Y2, E_ALL, E_LAST = range(9)
O_X, O_Y, O_TO, O_NEAR, O_NEAR2, O_FAR, O_FAR2, O_Z, O_EVEN = range(9)
R_FACTOR = {XF: 0, YF: 1, ZF: 2, LOW: 0, ALL: 3, LAST: 4}
R_OFFSET = {BASE: 5, EVEN: 5, XO: 6, YO: 7, ZO: 8, EDGE: 9}
R_ZF2, R_ENDS, R_ZO = 13, 14, (8, 15)
PARTS = 4


def dot(left, right, dims):
    return lax.dot_general(left, right, dims, preferred_element_type=jnp.float32)


def split(value, high, low):
    top = value.astype(jnp.bfloat16)
    high[...] = top
    low[...] = (value - top.astype(jnp.float32)).astype(jnp.bfloat16)


def product(left, right, dims):
    lh, ll = left
    rh, rl = right
    return (
        dot(lh[...], rl[...], dims) + dot(ll[...], rh[...], dims)
    ) + dot(lh[...], rh[...], dims)


def kernel(n, g_any, l_any, x_ref, xh_ref, xl_ref, qh_ref, ql_ref, *scratch):
    (g_ref, l_ref, other, prev, acc, pm, pt, so, high, low, tally,
     sent, got, l_send, l_recv, n_send, n_recv, in_sem, turn) = scratch
    order = g_ref.shape[0]
    half = order // 2
    tail = order - WIDE
    groups = n // GROUP
    joined = groups >= 3
    me = lax.axis_index("tm")
    j = lax.rem(me, GROUP)
    group = me // GROUP
    b0, b1, b2 = (lax.rem(j // d, 2) for d in (1, 2, 4))
    even, odd = b0 == 0, b0 == 1
    chip = j // 2
    xe, xl, ye, yl = b1 == 0, b1 == 1, b2 == 0, b2 == 1
    top = group == groups - 1
    rest = group < groups - 1
    bottom = (group == 0) & joined
    chain = rest & (group >= (2 if joined else 1))
    core = me + 1 - 2 * b0
    px = me + 2 - 4 * b1
    py = me + 4 - 8 * b2

    g_in = pltpu.make_async_copy(g_any, g_ref, in_sem.at[0])
    l_in = pltpu.make_async_copy(l_any, l_ref, in_sem.at[1])
    l_in.start()
    g_in.start()

    barrier = pltpu.get_barrier_semaphore()
    total = 0
    always = me >= 0
    for other_id, inside in (
        (core, always), (px, always), (py, always),
        (me + 2, odd & top & (chip == 1)), (me - 2, odd & top & (chip == 2)),
        (me - GROUP, group > 0), (me + GROUP, rest),
        (me - 2 * GROUP, odd & (group == 2)), (me + 2 * GROUP, odd & (group == 0) & (groups > 2)),
        (me - GROUP + 4, odd & top & ye & (group > 0)), (me + GROUP - 4, odd & yl & (group == groups - 2)),
        (me - 2 * GROUP + 4, odd & top & ye & (group == 2)),
        (me + 2 * GROUP - 4, odd & yl & (group == 0) & (groups == 3)),
        (me + 1, odd & (me < n - 1)), (me - 1, even & (me > 0)),
    ):
        total = total + inside.astype(jnp.int32)

        @pl.when(inside)
        def _(other_id=other_id):
            pl.semaphore_signal(barrier, inc=1, device_id=(other_id,), device_id_type=MESH)

    first, second, third = slice(0, STRIP), slice(STRIP, WIDE), slice(WIDE, order)
    left, right = slice(0, tail), slice(tail, 2 * tail)

    def slot(i, a=0, b=order):
        return high.at[i, a:b, :], low.at[i, a:b, :]

    def fill(i, value):
        split(value, *slot(i))

    def copy(src, dst, send, recv, target):
        return pltpu.make_async_remote_copy(
            src_ref=src, dst_ref=dst, send_sem=send, recv_sem=recv,
            device_id=(target,), device_id_type=MESH,
        )

    pending = []

    def start(condition, make):
        @pl.when(condition)
        def _():
            make().start()

    def send(condition, make):
        start(condition, make)
        pending.append((condition, make))

    def drain():
        for condition, make in pending:
            @pl.when(condition)
            def _(make=make):
                make().wait_send()
        pending.clear()

    def factor(i):
        mid = half // 2
        return pm.at[i, :half, :WIDE], pm.at[i, half:, :WIDE], pt.at[i, :mid], pt.at[i, mid:]

    def quarter(s, count=1):
        return slice(s * WIDE // PARTS, (s + count) * WIDE // PARTS)

    half_tally = tally.at[:tally.shape[0] // 2, :]

    def leave(condition, make_ref, sem):
        def make():
            ref = make_ref()
            return copy(ref, ref, sent.at[sem], got.at[0], core)

        pending.append((condition, make))

    def send_factor(condition, src, dst, target, sem, parts=(0, 1, 2, 3), ends=None, recv=None, last=3):
        for s in parts:
            start(
                condition,
                lambda s=s: copy(
                    factor(src)[s], factor(dst)[s],
                    sent.at[ends if s >= 2 and ends is not None else sem],
                    got.at[R_FACTOR[dst] if recv is None else recv], target,
                ),
            )
        if last in parts and ends is None:
            leave(condition, lambda: tally, sem)

    def send_offset(condition, src, dst, target, sem, parts=range(PARTS), count=PARTS, recv=None, last=PARTS - 1):
        for s in parts:
            start(
                condition,
                lambda s=s: copy(
                    so.at[src, quarter(s), :], so.at[dst, quarter(s), :],
                    sent.at[sem],
                    got.at[R_OFFSET[dst] + (s if dst == EDGE else 0) if recv is None else recv], target,
                ),
            )
        if last in parts:
            leave(condition, lambda: so.at[src, quarter(0, count), :], sem)

    def wait_sent(condition, ref, sem):
        @pl.when(condition)
        def _():
            copy(ref, ref, sent.at[sem], got.at[0], core).wait_send()

    def got_factor(i):
        copy(tally, tally, sent.at[0], got.at[R_FACTOR[i]], me).wait_recv()

    def got_offset(i):
        copy(so.at[i], so.at[i], sent.at[0], got.at[R_OFFSET[i]], me).wait_recv()

    def got_edge(s):
        ref = so.at[EDGE, quarter(s), :]
        copy(ref, ref, sent.at[0], got.at[R_OFFSET[EDGE] + s], me).wait_recv()

    def load_factor(i, k):
        h, l = high.at[k], low.at[k]
        split(pm[i, :, :WIDE], h.at[:, :WIDE], l.at[:, :WIDE])
        ends = pt[i]
        split(ends[:, :tail], h.at[:half, third], l.at[:half, third])
        split(ends[:, tail:2 * tail], h.at[half:, third], l.at[half:, third])

    def multiply(i, k, r, out, into=None):
        rows = slice(i * half, (i + 1) * half)
        value = product(slot(k, rows.start, rows.stop), slot(r), NN)
        if out is not None:
            pm[out, rows, :WIDE] = value[:, :WIDE]
            pt[out, :, i * tail:(i + 1) * tail] = value[:, third]
        if into is not None:
            split(value, *slot(into, rows.start, rows.stop))

    def pack(ref, i):
        so[i, first, :] = ref[first, :WIDE]
        so[i, second, left] = ref[first, third]
        so[i, second, right] = ref[second, third]
        so[i, STRIP:STRIP + tail, second] = ref[STRIP:STRIP + tail, second]
        so[i, STRIP + tail:WIDE, STRIP + tail:] = ref[STRIP + tail:WIDE, STRIP + tail:WIDE]
        so[i, STRIP + tail:WIDE, STRIP:STRIP + tail] = ref[third, third]

    def spread(i, put, parts=(0, 1)):
        if 0 in parts:
            put(so[i, first, :], first, slice(0, WIDE))
            put(so[i, first, second].T, second, first)
        if 1 in parts:
            ends = so[i, second, first]
            turned = ends.T
            put(ends[:, :tail], first, third)
            put(ends[:, tail:2 * tail], second, third)
            put(turned[:tail], third, first)
            put(turned[tail:2 * tail], third, second)
            block = so[i, second, second]
            lanes = lax.broadcasted_iota(jnp.int32, (STRIP - tail, STRIP), 1)
            put(block[:tail], slice(STRIP, STRIP + tail), second)
            put(jnp.where(lanes < tail, block.T[tail:], block[tail:]), slice(STRIP + tail, WIDE), second)
            put(block[tail:, :tail], third, third)

    def to_slot(k):
        def put(value, rows, columns):
            split(value, high.at[k, rows, columns], low.at[k, rows, columns])
        return put

    def to_ref(ref):
        def put(value, rows, columns):
            ref[rows, columns] = value
        return put

    def fold_left(s, k, z=SZ, w=SW):
        a, b = ((0, STRIP), (STRIP, order))[s]
        split(product(slot(k, a, b), slot(z), NN), *slot(w, a, b))

    def fold_right(s, k, base, out, w=SW):
        a, b = ((0, STRIP), (STRIP, order))[s]
        term = product(slot(w, a, b), slot(k, a), NT)
        if s == 0:
            so[out, first, :] = so[base, first, :] + term[:, :WIDE]
            so[out, second, left] = so[base, second, left] + term[:, WIDE:]
        else:
            lower = slice(STRIP + tail, WIDE)
            so[out, second, right] = so[base, second, right] + term[:STRIP, STRIP:]
            so[out, STRIP:STRIP + tail, second] = so[base, STRIP:STRIP + tail, second] + term[:tail, :STRIP]
            so[out, lower, lower] = so[base, lower, lower] + term[tail:STRIP, tail:STRIP]
            so[out, lower, STRIP:STRIP + tail] = so[base, lower, STRIP:STRIP + tail] + term[STRIP:, STRIP:]

    def fold(condition, k, base, out, after):
        for s in range(2):
            @pl.when(condition)
            def _(s=s):
                fold_left(s, k)
                fold_right(s, k, base, out)
            after(s)

    def fold_at_once(k, base, out):
        fold_left(0, k)
        fold_left(1, k)
        fold_right(0, k, base, out)
        fold_right(1, k, base, out)

    def fold_whole(k, base, out, parts=None):
        for a in (0, half):
            split(product(slot(k, a, a + half), slot(SZ), NN), *slot(SW, a, a + half))
        for a in (0, half):
            value = base[a:a + half, :] + product(slot(SW, a, a + half), slot(k), NT)
            out[a:a + half, :] = value
            if parts is not None:
                split(value, parts[0].at[a:a + half, :], parts[1].at[a:a + half, :])

    l_in.wait()

    @pl.when(even)
    def _():
        fill(SL, l_ref[...])

    @pl.when(odd)
    def _():
        fill(SM, l_ref[...])

    g_in.wait()

    @pl.when(even)
    def _():
        pack(g_ref, BASE)

    @pl.when(odd)
    def _():
        fill(SZ, g_ref[...])

    pl.semaphore_wait(barrier, total)

    send(always, lambda: copy(l_ref, other, l_send, l_recv, core))
    send_offset(even, BASE, BASE, core, E_BASE)

    swap_x = even & (rest | ye)

    copy(other, other, l_send, l_recv, me).wait_recv()

    @pl.when(even)
    def _():
        fill(SM, other[...])

    for i in range(2):
        @pl.when(even)
        def _(i=i):
            multiply(i, SL, SM, OWN, SC)
        send_factor(swap_x, OWN, XF, px, E_X, (i,))
    send_factor(swap_x, OWN, XF, px, E_X, (2, 3), ends=E_X2)

    early_o = odd & top & (chip == 3)

    @pl.when(odd)
    def _():
        fill(SL, other[...])
        fold_left(0, SL)
        got_offset(BASE)
        fold_right(0, SL, BASE, OWN)

    send_offset(early_o, OWN, XO, px, O_X, (0, 1))

    @pl.when(odd)
    def _():
        fold_left(1, SL)
        fold_right(1, SL, BASE, OWN)

    send_offset(early_o, OWN, XO, px, O_X, (2, 3))

    @pl.when(odd)
    def _():
        for i in range(2):
            multiply(i, SL, SM, None, SC)

    turns = rest | ye
    wait_sent(swap_x, pm.at[OWN, :, :WIDE], E_X)

    @pl.when(swap_x)
    def _():
        pl.semaphore_signal(turn, inc=1, device_id=(core,), device_id_type=MESH)

    @pl.when(odd & turns)
    def _():
        pl.semaphore_wait(turn, 1)

    send_offset(odd & turns, OWN, XO, px, O_X)

    def send_coupling(condition):
        send(odd & condition & (me < n - 1), lambda: copy(l_ref, prev, n_send, n_recv, me + 1))

    soon = (rest & xe) | (bottom & (chip == 1)) | (top & (chip == 0))
    late = (top & (chip > 0)) | (jnp.logical_not(bottom) & (chip == 1) & (group == groups - 2))
    send_coupling(soon)
    leave(swap_x, lambda: pt.at[OWN], E_X2)

    @pl.when(swap_x)
    def _():
        got_factor(XF)

    send_factor(swap_x, XF, LOW, core, E_LOW)

    @pl.when(swap_x)
    def _():
        load_factor(XF, SX)

    def ordered(condition, early, k, r, a, b):
        @pl.when(condition & early)
        def _():
            high[a], low[a], high[b], low[b] = high[k], low[k], high[r], low[r]

        @pl.when(condition & jnp.logical_not(early))
        def _():
            high[a], low[a], high[b], low[b] = high[r], low[r], high[k], low[k]

    ordered(swap_x, xe, SC, SX, SA, SB)
    swap_y = even & rest
    tells = rest & jnp.logical_not(bottom & (chip == 0))
    hears = rest & jnp.logical_not(bottom & (chip == 2))
    for i in range(2):
        @pl.when(swap_x)
        def _(i=i):
            multiply(i, SA, SB, PAIR, SP)
        send_factor(even & tells, PAIR, YF, py, E_Y, (i,))
    send_factor(even & tells, PAIR, YF, py, E_Y, (2, 3), ends=E_Y2)
    send_factor(swap_x & ye, PAIR, ZF, core, E_PAIR)

    o_fold = odd & (rest | (chip < 3))

    def neighbour(condition):
        @pl.when(condition)
        def _():
            got_factor(LOW)
            load_factor(LOW, SX)

    neighbour(odd & turns & xl)

    @pl.when(o_fold)
    def _():
        got_offset(XO)

    @pl.when(o_fold & xe)
    def _():
        spread(XO, to_slot(SZ))

    @pl.when(o_fold & xl)
    def _():
        spread(OWN, to_slot(SZ))

    stepped = odd & top & (chip == 2)

    def after_pair(s):
        parts = (2 * s, 2 * s + 1)
        send_offset(stepped, PAIR, YO, py, O_Y, parts)
        send_offset(stepped, PAIR, YO, me - 2, O_TO, parts)

    @pl.when(stepped)
    def _():
        fold(stepped, SC, OWN, PAIR, after_pair)

    @pl.when(o_fold & xe & jnp.logical_not(stepped))
    def _():
        fold_at_once(SC, OWN, PAIR)

    @pl.when(o_fold & xl)
    def _():
        fold_at_once(SX, XO, PAIR)

    wait_sent(even & tells, pm.at[PAIR, :, :WIDE], E_Y)

    @pl.when(swap_y)
    def _():
        pl.semaphore_signal(turn, inc=1, device_id=(core,), device_id_type=MESH)

    @pl.when(odd & rest)
    def _():
        pl.semaphore_wait(turn, 1)

    send_offset(odd & tells, PAIR, YO, py, O_Y)
    leave(even & tells, lambda: pt.at[PAIR], E_Y2)
    hears_late = even & hears & yl
    down = even & (group == 1) & rest & joined
    even_chain = even & chain
    hand = swap_y & (chip < 3)

    @pl.when(even)
    def _():

        @pl.when(even & hears)
        def _():
            got_factor(YF)

        send_factor(hears_late, YF, ZF, core, E_PAIR)

        @pl.when(even & hears)
        def _():
            load_factor(YF, SY)

        ordered(even & hears, ye, SP, SY, SA, SB)
        for i in range(2):
            @pl.when(even & hears)
            def _(i=i):
                multiply(i, SA, SB, ALL, SR)
            send_factor(down & (b1 == i), ALL, ZF, me - GROUP, E_ALL, (i,))
        for i in range(2):
            send_factor(down & (b1 == i), ALL, ZF, me - GROUP, E_ALL, (2 + i,), recv=R_ENDS, last=None)
        leave(down, lambda: half_tally, E_ALL)
        send_factor(even_chain, ALL, ALL, core, E_ALL)

        @pl.when(swap_y & (chip == 0))
        def _():
            for i in range(2):
                multiply(i, SX, SY, None, SB)
            high[SA], low[SA] = high[SR], low[SR]

        @pl.when(swap_y & (chip == 1))
        def _():
            for i in range(2):
                multiply(i, SC, SY, None, SA)
            high[SB], low[SB] = high[SY], low[SY]

        @pl.when(swap_y & (chip == 2))
        def _():
            high[SA], low[SA] = high[SP], low[SP]
            high[SB], low[SB] = high[SX], low[SX]

        @pl.when(swap_y & (chip == 3))
        def _():
            high[SA], low[SA] = high[SC], low[SC]


        @pl.when(hand)
        def _():
            for i in range(2):
                multiply(i, SM, SB, LAST)

        send_factor(hand, LAST, LAST, core, E_LAST)

    z_fold = odd & (hears | (top & ye))

    @pl.when(z_fold)
    def _():
        got_factor(ZF)
        load_factor(ZF, SP)

    sharing = groups >= 4
    hands = odd & ye & (group == groups - 2) & sharing
    passes = odd & top & yl & sharing
    @pl.when(passes)
    def _():
        for q in range(PARTS // 2):
            @pl.when(passes)
            def _(q=q):
                got_edge(q)

            send_offset(passes, EDGE, EDGE, me - GROUP, O_NEAR, (q,), PARTS // 2, last=1)

    def take_edge(condition, hand_on, quarters):
        for q in quarters:
            @pl.when(condition)
            def _(q=q):
                got_edge(q)

            send_offset(hand_on, EDGE, EDGE, core, O_TO, (q,), last=None)

    take_edge(hands, hands, (0, 1))

    @pl.when(hands)
    def _():
        spread(EDGE, to_slot(SE), (0,))

    @pl.when(z_fold)
    def _():
        got_offset(YO)

    send_coupling(jnp.logical_not(soon | late))

    @pl.when(odd & hears & yl)
    def _():
        spread(PAIR, to_slot(SZ))

    @pl.when(z_fold & ye)
    def _():
        spread(YO, to_slot(SZ))

    far = group == 2 if joined else me < 0
    near = (group >= 2) if joined else (group >= 1)

    shared = (2, 3) if sharing else range(PARTS)
    heads = odd & top & ye
    heads_near, heads_far, heads_share = heads & near, heads & far, heads & sharing

    def after_all(s):
        parts = (2 * s, 2 * s + 1)
        send_offset(heads_near, ALL, EDGE, me - GROUP, O_NEAR, parts)
        send_offset(heads_far, ALL, EDGE, me - 2 * GROUP, O_FAR, parts)
        if s == 0:
            send_offset(heads_share, ALL, EDGE, py, O_TO, parts, PARTS // 2, last=1)
        else:
            send_offset(heads_near, ALL, EDGE, me - GROUP + 4, O_NEAR2, shared, len(shared))

    gives = odd & rest & (group == 1) & joined

    @pl.when(odd & hears & ye & jnp.logical_not(hands | gives))
    def _():
        fold_at_once(SP, PAIR, ALL)

    @pl.when(odd & hears & yl & jnp.logical_not(gives))
    def _():
        fold_at_once(SP, YO, ALL)

    def after_given(s):
        send_offset(gives, ALL, ZO, me - GROUP, O_Z, (2 * s, 2 * s + 1), recv=R_ZO[s])

    @pl.when(gives)
    def _():
        @pl.when(gives & ye)
        def _():
            so[BASE] = so[PAIR]

        @pl.when(gives & yl)
        def _():
            so[BASE] = so[YO]

        fold(gives & jnp.logical_not(hands), SP, BASE, ALL, after_given)

    @pl.when(heads)
    def _():
        fold(heads, SP, PAIR, ALL, after_all)
        send_offset(heads_far, ALL, EDGE, me - 2 * GROUP + 4, O_FAR2)

    @pl.when(odd & chain)
    def _():
        got_factor(ALL)
        load_factor(ALL, SR)

    alone = odd & chain & jnp.logical_not(hands)
    for s in range(2):
        taken = alone if s == 0 else odd & chain
        take_edge(taken, taken, (2 * s, 2 * s + 1))

        @pl.when(taken)
        def _(s=s):
            spread(EDGE, to_slot(SE), (s,))

    leave(odd & chain, lambda: so.at[EDGE], O_TO)

    routes = {
        who: (condition & near & jnp.logical_not(far), condition & near & far, condition & far)
        for who, condition in (("hands", hands), ("alone", alone))
    }

    def after_chain(who, s):
        parts = (2 * s, 2 * s + 1)
        only, also, to_far = routes[who]
        send_offset(to_far, CHAIN, EDGE, me - 2 * GROUP, O_FAR, parts)
        send_offset(only, CHAIN, EDGE, me - GROUP, O_NEAR, parts)
        if s == 1:
            send_offset(also, CHAIN, EDGE, me - GROUP, O_NEAR2)

    @pl.when(hands)
    def _():
        for s in range(2):
            @pl.when(hands)
            def _(s=s):
                fold_left(s, SR, SE, SV)
                fold_left(s, SP)
                fold_right(s, SP, PAIR, ALL)
                fold_right(s, SR, ALL, CHAIN, SV)

            after_chain("hands", s)

    @pl.when(alone)
    def _():
        for s in range(2):
            @pl.when(alone)
            def _(s=s):
                fold_left(s, SR, SE)
                fold_right(s, SR, ALL, CHAIN)

            after_chain("alone", s)

    neighbour(odd & turns & xe)
    send_coupling(late)

    send_offset(odd & (chip == 0), ALL, EVEN, core, O_EVEN)
    send_offset(odd & (chip == 2), PAIR, EVEN, core, O_EVEN)
    send_offset(odd & (chip == 3), OWN, EVEN, core, O_EVEN)
    low_y = odd & ye

    @pl.when(low_y)
    def _():
        spread(YO, to_slot(SZ))

    @pl.when(low_y & (chip == 1))
    def _():
        high[SA], low[SA] = high[SC], low[SC]
        so[BASE] = so[OWN]

    @pl.when(low_y & (chip == 0))
    def _():
        high[SA], low[SA] = high[SX], low[SX]
        so[BASE] = so[XO]

    @pl.when(low_y)
    def _():
        fold_at_once(SA, BASE, EVEN)

    send_offset(odd & (chip == 1), EVEN, EVEN, core, O_EVEN)

    @pl.when(odd & (chip == 0))
    def _():
        spread(EVEN, to_slot(SZ))

    @pl.when(odd & (chip == 1))
    def _():
        spread(YO, to_slot(SZ))

    @pl.when(odd & (chip == 2))
    def _():
        spread(XO, to_slot(SZ))

    @pl.when(odd & (chip < 3))
    def _():
        fold_whole(SM, g_ref, acc)

    @pl.when(odd & (chip == 3))
    def _():
        acc[...] = g_ref[...]

    @pl.when(odd & rest & (chip < 3))
    def _():
        got_factor(LAST)
        load_factor(LAST, SA)

    @pl.when(odd & rest & (chip == 3))
    def _():
        high[SA], low[SA] = high[SM], low[SM]

    for part, recv in ((0, R_FACTOR[ZF]), (2, R_ENDS)):
        @pl.when(bottom & even)
        def _(part=part, recv=recv):
            ref = factor(ZF)[part]
            copy(ref, ref, sent.at[0], got.at[recv], me).wait_recv()

        for i in range(2):
            send_factor(bottom & even & (b1 == i), ZF, ZF, px, E_X, (part + i,), recv=R_ZF2, last=None)
            send_factor(bottom & even & (b1 == i), ZF, YF, core, E_ALL, (part + i,), last=None)

    @pl.when(even)
    def _():
        got_offset(EVEN)
        spread(EVEN, to_ref(acc))

    @pl.when(bottom & even)
    def _():
        copy(half_tally, half_tally, sent.at[0], got.at[R_ZF2], me).wait_recv()

    for i in range(2):
        send_factor(bottom & even & (b1 != i), ZF, YF, core, E_ALL, (i, 2 + i), last=None)

    @pl.when(bottom & even)
    def _():
        load_factor(ZF, SR)

    @pl.when(odd)
    def _():
        split(other[...], qh_ref, ql_ref)

    @pl.when(even & (me > 0))
    def _():
        copy(prev, prev, n_send, n_recv, me).wait_recv()
        split(prev[...], qh_ref, ql_ref)

    @pl.when(me == 0)
    def _():
        qh_ref[...] = jnp.zeros_like(qh_ref)
        ql_ref[...] = jnp.zeros_like(ql_ref)

    apart = odd & rest & jnp.logical_not(chain)
    waits = rest & (even | jnp.logical_not(chain))
    drain()
    for s in range(2):
        take_edge(waits, apart, (2 * s, 2 * s + 1))

        @pl.when(rest)
        def _(s=s):
            spread(EDGE, to_slot(SZ), (s,))

    leave(apart, lambda: so.at[EDGE], O_TO)

    def got_given(s):
        ref = so.at[ZO, quarter(2 * s, 2), :]
        copy(ref, ref, sent.at[0], got.at[R_ZO[s]], me).wait_recv()

    for s in range(2):
        @pl.when(bottom & odd)
        def _(s=s):
            got_given(s)

        send_offset(bottom & odd, ZO, ZO, core, O_Z, (2 * s, 2 * s + 1), recv=R_ZO[s])

    leave(bottom & even, lambda: half_tally, E_X)
    leave(bottom & even, lambda: tally, E_ALL)

    @pl.when(bottom & odd)
    def _():
        got_factor(YF)
        load_factor(YF, SR)

    @pl.when(bottom)
    def _():
        fold_left(0, SR)
        fold_left(1, SR)

    @pl.when(bottom & even)
    def _():
        got_given(0)
        got_given(1)

    @pl.when(bottom)
    def _():
        fold_right(0, SR, ZO, CHAIN)
        fold_right(1, SR, ZO, CHAIN)
        spread(CHAIN, to_slot(SZ))

    @pl.when(rest)
    def _():
        fold_whole(SA, acc, x_ref, (xh_ref, xl_ref))

    @pl.when(top)
    def _():
        x_ref[...] = acc[...]
        split(acc[...], xh_ref, xl_ref)

    drain()


def finish(x_ref, xh, xl, qh, ql, d_any, c_any, c_ref, sem):
    copies = [pltpu.make_async_copy(x_ref, d_any, sem.at[0])]
    copies[0].start()
    half = x_ref.shape[0] // 2
    for i in range(2):
        rows = slice(i * half, (i + 1) * half)
        c_ref[rows, :] = product((xh.at[rows, :], xl.at[rows, :]), (qh, ql), NT)
        copies.append(pltpu.make_async_copy(c_ref.at[rows, :], c_any.at[rows, :], sem.at[1 + i]))
        copies[-1].start()
    for c in copies:
        c.wait()


def local(n, schur_inverse, sweep_factor):
    order = schur_inverse.shape[1]
    full = (order, order)
    f32, bf16 = jnp.float32, jnp.bfloat16
    dma = pltpu.SemaphoreType.DMA
    values = pl.pallas_call(
        functools.partial(kernel, n),
        out_shape=[pltpu.VMEM(full, f32)] + [pltpu.VMEM(full, bf16)] * 4,
        in_specs=[pl.BlockSpec(memory_space=pl.ANY)] * 2,
        out_specs=[pl.BlockSpec(memory_space=pltpu.VMEM)] * 5,
        scratch_shapes=[pltpu.VMEM(full, f32)] * 5 + [
            pltpu.VMEM((8,) + full, f32),
            pltpu.VMEM((8, order // 2, STRIP), f32),
            pltpu.VMEM((10, WIDE, WIDE), f32),
            pltpu.VMEM((13,) + full, bf16),
            pltpu.VMEM((13,) + full, bf16),
            pltpu.VMEM((order * WIDE // STRIP + order // 2, STRIP), f32),
            dma((9,)), dma((12 + PARTS,)), dma, dma, dma, dma, dma((2,)), pltpu.SemaphoreType.REGULAR,
        ],
        compiler_params=pltpu.CompilerParams(
            collective_id=0, has_side_effects=True
        ),
    )(schur_inverse[0], sweep_factor[0])
    diagonal, coupling = pl.pallas_call(
        finish,
        out_shape=[jax.ShapeDtypeStruct(full, f32)] * 2,
        in_specs=[pl.BlockSpec(memory_space=pltpu.VMEM)] * 5,
        out_specs=[pl.BlockSpec(memory_space=pl.ANY)] * 2,
        scratch_shapes=[pltpu.VMEM(full, f32), dma((3,))],
    )(*(pltpu.with_memory_space_constraint(v, pltpu.VMEM) for v in values))
    return diagonal[None], coupling[None]


def solution(mesh):
    n = mesh.shape["tm"]
    return jax.shard_map(
        functools.partial(local, n),
        mesh=mesh,
        in_specs=(P("tm", None, None), P("tm", None, None)),
        out_specs=(P("tm", None, None), P("tm", None, None)),
        check_vma=False,
    )
```

```python
import functools

import jax
import jax.numpy as jnp
from jax import lax
from jax.experimental import pallas as pl
from jax.experimental.pallas import tpu as pltpu
from jax.sharding import PartitionSpec as P

MESH = pl.DeviceIdType.MESH
STRIP = 128
WIDE = 2 * STRIP
GROUP = 8
NN = (((1,), (0,)), ((), ()))
NT = (((1,), (1,)), ((), ()))

OWN, PAIR, ALL, LAST, XF, YF, ZF, LOW = range(8)
CHAIN, EVEN, XO, YO, EDGE, ZO, BASE = range(3, 10)
SL, SM, SC, SX, SY, SP, SA, SB, SR, SZ, SW, SE, SV = range(13)
E_BASE, E_X, E_X2, E_LOW, E_PAIR, E_Y, E_Y2, E_ALL, E_LAST = range(9)
O_X, O_Y, O_TO, O_NEAR, O_NEAR2, O_FAR, O_FAR2, O_Z, O_EVEN = range(9)
R_FACTOR = {XF: 0, YF: 1, ZF: 2, LOW: 0, ALL: 3, LAST: 4}
R_OFFSET = {BASE: 5, EVEN: 5, XO: 6, YO: 7, ZO: 8, EDGE: 9}
R_ZF2, R_ENDS, R_ZO = 13, 14, (8, 15)
PARTS = 4


def dot(left, right, dims):
    return lax.dot_general(left, right, dims, preferred_element_type=jnp.float32)


def split(value, high, low):
    top = value.astype(jnp.bfloat16)
    high[...] = top
    low[...] = (value - top.astype(jnp.float32)).astype(jnp.bfloat16)


def product(left, right, dims):
    lh, ll = left
    rh, rl = right
    return (
        dot(lh[...], rl[...], dims) + dot(ll[...], rh[...], dims)
    ) + dot(lh[...], rh[...], dims)


def kernel(n, g_any, l_any, x_ref, xh_ref, xl_ref, qh_ref, ql_ref, *scratch):
    (g_ref, l_ref, other, prev, acc, pm, pt, so, high, low, tally,
     sent, got, l_send, l_recv, n_send, n_recv, in_sem, turn) = scratch
    order = g_ref.shape[0]
    half = order // 2
    tail = order - WIDE
    groups = n // GROUP
    joined = groups >= 3
    me = lax.axis_index("tm")
    j = lax.rem(me, GROUP)
    group = me // GROUP
    b0, b1, b2 = (lax.rem(j // d, 2) for d in (1, 2, 4))
    even, odd = b0 == 0, b0 == 1
    chip = j // 2
    xe, xl, ye, yl = b1 == 0, b1 == 1, b2 == 0, b2 == 1
    top = group == groups - 1
    rest = group < groups - 1
    bottom = (group == 0) & joined
    chain = rest & (group >= (2 if joined else 1))
    core = me + 1 - 2 * b0
    px = me + 2 - 4 * b1
    py = me + 4 - 8 * b2

    g_in = pltpu.make_async_copy(g_any, g_ref, in_sem.at[0])
    l_in = pltpu.make_async_copy(l_any, l_ref, in_sem.at[1])
    l_in.start()
    g_in.start()

    barrier = pltpu.get_barrier_semaphore()
    total = 0
    always = me >= 0
    for other_id, inside in (
        (core, always), (px, always), (py, always),
        (me + 2, odd & top & (chip == 1)), (me - 2, odd & top & (chip == 2)),
        (me - GROUP, group > 0), (me + GROUP, rest),
        (me - 2 * GROUP, odd & (group == 2)), (me + 2 * GROUP, odd & (group == 0) & (groups > 2)),
        (me - GROUP + 4, odd & top & ye & (group > 0)), (me + GROUP - 4, odd & yl & (group == groups - 2)),
        (me - 2 * GROUP + 4, odd & top & ye & (group == 2)),
        (me + 2 * GROUP - 4, odd & yl & (group == 0) & (groups == 3)),
        (me + 1, odd & (me < n - 1)), (me - 1, even & (me > 0)),
    ):
        total = total + inside.astype(jnp.int32)

        @pl.when(inside)
        def _(other_id=other_id):
            pl.semaphore_signal(barrier, inc=1, device_id=(other_id,), device_id_type=MESH)

    first, second, third = slice(0, STRIP), slice(STRIP, WIDE), slice(WIDE, order)
    left, right = slice(0, tail), slice(tail, 2 * tail)

    def slot(i, a=0, b=order):
        return high.at[i, a:b, :], low.at[i, a:b, :]

    def fill(i, value):
        split(value, *slot(i))

    def copy(src, dst, send, recv, target):
        return pltpu.make_async_remote_copy(
            src_ref=src, dst_ref=dst, send_sem=send, recv_sem=recv,
            device_id=(target,), device_id_type=MESH,
        )

    pending = []

    def start(condition, make):
        @pl.when(condition)
        def _():
            make().start()

    def send(condition, make):
        start(condition, make)
        pending.append((condition, make))

    def drain():
        for condition, make in pending:
            @pl.when(condition)
            def _(make=make):
                make().wait_send()
        pending.clear()

    def factor(i):
        mid = half // 2
        return tuple(pm.at[i, a:a + mid, :WIDE] for a in range(0, order, mid)) + (pt.at[i, :mid], pt.at[i, mid:])

    def quarter(s, count=1):
        return slice(s * WIDE // PARTS, (s + count) * WIDE // PARTS)

    half_tally = tally.at[:tally.shape[0] // 2, :]

    def leave(condition, make_ref, sem):
        def make():
            ref = make_ref()
            return copy(ref, ref, sent.at[sem], got.at[0], core)

        pending.append((condition, make))

    def send_factor(condition, src, dst, target, sem, parts=range(6), ends=None, recv=None, last=5):
        for s in parts:
            start(
                condition,
                lambda s=s: copy(
                    factor(src)[s], factor(dst)[s],
                    sent.at[ends if s >= 4 and ends is not None else sem],
                    got.at[R_FACTOR[dst] if recv is None else recv], target,
                ),
            )
        if last in parts and ends is None:
            leave(condition, lambda: tally, sem)

    def send_offset(condition, src, dst, target, sem, parts=range(PARTS), count=PARTS, recv=None, last=PARTS - 1):
        for s in parts:
            start(
                condition,
                lambda s=s: copy(
                    so.at[src, quarter(s), :], so.at[dst, quarter(s), :],
                    sent.at[sem],
                    got.at[R_OFFSET[dst] + (s if dst == EDGE else 0) if recv is None else recv], target,
                ),
            )
        if last in parts:
            leave(condition, lambda: so.at[src, quarter(0, count), :], sem)

    def wait_sent(condition, ref, sem):
        @pl.when(condition)
        def _():
            copy(ref, ref, sent.at[sem], got.at[0], core).wait_send()

    def got_factor(i):
        copy(tally, tally, sent.at[0], got.at[R_FACTOR[i]], me).wait_recv()

    def got_offset(i):
        copy(so.at[i], so.at[i], sent.at[0], got.at[R_OFFSET[i]], me).wait_recv()

    def got_edge(s):
        ref = so.at[EDGE, quarter(s), :]
        copy(ref, ref, sent.at[0], got.at[R_OFFSET[EDGE] + s], me).wait_recv()

    def load_factor(i, k):
        h, l = high.at[k], low.at[k]
        split(pm[i, :, :WIDE], h.at[:, :WIDE], l.at[:, :WIDE])
        ends = pt[i]
        split(ends[:, :tail], h.at[:half, third], l.at[:half, third])
        split(ends[:, tail:2 * tail], h.at[half:, third], l.at[half:, third])

    def multiply(a, b, k, r, out, into=None):
        value = product(slot(k, a, b), slot(r), NN)
        if out is not None:
            pm[out, a:b, :WIDE] = value[:, :WIDE]
            side, low_row = a // half, a // half * half
            pt[out, a - low_row:b - low_row, side * tail:(side + 1) * tail] = value[:, third]
        if into is not None:
            split(value, *slot(into, a, b))

    pieces = ((0, half // 2, (0,)), (half // 2, half, (1,)), (half, order, (2, 3)))

    def pack(ref, i):
        so[i, first, :] = ref[first, :WIDE]
        so[i, second, left] = ref[first, third]
        so[i, second, right] = ref[second, third]
        so[i, STRIP:STRIP + tail, second] = ref[STRIP:STRIP + tail, second]
        so[i, STRIP + tail:WIDE, STRIP + tail:] = ref[STRIP + tail:WIDE, STRIP + tail:WIDE]
        so[i, STRIP + tail:WIDE, STRIP:STRIP + tail] = ref[third, third]

    def spread(i, put, parts=(0, 1)):
        if 0 in parts:
            put(so[i, first, :], first, slice(0, WIDE))
            put(so[i, first, second].T, second, first)
        if 1 in parts:
            ends = so[i, second, first]
            turned = ends.T
            put(ends[:, :tail], first, third)
            put(ends[:, tail:2 * tail], second, third)
            put(turned[:tail], third, first)
            put(turned[tail:2 * tail], third, second)
            block = so[i, second, second]
            lanes = lax.broadcasted_iota(jnp.int32, (STRIP - tail, STRIP), 1)
            put(block[:tail], slice(STRIP, STRIP + tail), second)
            put(jnp.where(lanes < tail, block.T[tail:], block[tail:]), slice(STRIP + tail, WIDE), second)
            put(block[tail:, :tail], third, third)

    def to_slot(k):
        def put(value, rows, columns):
            split(value, high.at[k, rows, columns], low.at[k, rows, columns])
        return put

    def to_ref(ref):
        def put(value, rows, columns):
            ref[rows, columns] = value
        return put

    def fold_left(s, k, z=SZ, w=SW):
        a, b = ((0, STRIP), (STRIP, order))[s]
        split(product(slot(k, a, b), slot(z), NN), *slot(w, a, b))

    def fold_right(s, k, base, out, w=SW):
        a, b = ((0, STRIP), (STRIP, order))[s]
        term = product(slot(w, a, b), slot(k, a), NT)
        if s == 0:
            so[out, first, :] = so[base, first, :] + term[:, :WIDE]
            so[out, second, left] = so[base, second, left] + term[:, WIDE:]
        else:
            lower = slice(STRIP + tail, WIDE)
            so[out, second, right] = so[base, second, right] + term[:STRIP, STRIP:]
            so[out, STRIP:STRIP + tail, second] = so[base, STRIP:STRIP + tail, second] + term[:tail, :STRIP]
            so[out, lower, lower] = so[base, lower, lower] + term[tail:STRIP, tail:STRIP]
            so[out, lower, STRIP:STRIP + tail] = so[base, lower, STRIP:STRIP + tail] + term[STRIP:, STRIP:]

    def fold(condition, k, base, out, after):
        for s in range(2):
            @pl.when(condition)
            def _(s=s):
                fold_left(s, k)
                fold_right(s, k, base, out)
            after(s)

    def fold_at_once(k, base, out):
        fold_left(0, k)
        fold_left(1, k)
        fold_right(0, k, base, out)
        fold_right(1, k, base, out)

    def fold_whole(k, base, out, parts=None):
        for a in (0, half):
            split(product(slot(k, a, a + half), slot(SZ), NN), *slot(SW, a, a + half))
        for a in (0, half):
            value = base[a:a + half, :] + product(slot(SW, a, a + half), slot(k), NT)
            out[a:a + half, :] = value
            if parts is not None:
                split(value, parts[0].at[a:a + half, :], parts[1].at[a:a + half, :])

    l_in.wait()

    @pl.when(even)
    def _():
        fill(SL, l_ref[...])

    @pl.when(odd)
    def _():
        fill(SM, l_ref[...])

    g_in.wait()

    @pl.when(even)
    def _():
        pack(g_ref, BASE)

    @pl.when(odd)
    def _():
        fill(SZ, g_ref[...])

    pl.semaphore_wait(barrier, total)

    send(always, lambda: copy(l_ref, other, l_send, l_recv, core))
    send_offset(even, BASE, BASE, core, E_BASE)

    swap_x = even & (rest | ye)

    copy(other, other, l_send, l_recv, me).wait_recv()

    @pl.when(even)
    def _():
        fill(SM, other[...])

    for a, b, parts in pieces:
        @pl.when(even)
        def _(a=a, b=b):
            multiply(a, b, SL, SM, OWN, SC)
        send_factor(swap_x, OWN, XF, px, E_X, parts)
    send_factor(swap_x, OWN, XF, px, E_X, (4, 5), ends=E_X2)

    early_o = odd & top & (chip == 3)

    @pl.when(odd)
    def _():
        fill(SL, other[...])
        fold_left(0, SL)
        got_offset(BASE)
        fold_right(0, SL, BASE, OWN)

    send_offset(early_o, OWN, XO, px, O_X, (0, 1))

    @pl.when(odd)
    def _():
        fold_left(1, SL)
        fold_right(1, SL, BASE, OWN)

    send_offset(early_o, OWN, XO, px, O_X, (2, 3))

    @pl.when(odd)
    def _():
        for i in range(2):
            multiply(i * half, (i + 1) * half, SL, SM, None, SC)

    turns = rest | ye
    wait_sent(swap_x, pm.at[OWN, :, :WIDE], E_X)

    @pl.when(swap_x)
    def _():
        pl.semaphore_signal(turn, inc=1, device_id=(core,), device_id_type=MESH)

    @pl.when(odd & turns)
    def _():
        pl.semaphore_wait(turn, 1)

    send_offset(odd & turns, OWN, XO, px, O_X)

    def send_coupling(condition):
        send(odd & condition & (me < n - 1), lambda: copy(l_ref, prev, n_send, n_recv, me + 1))

    soon = (rest & xe) | (bottom & (chip == 1)) | (top & (chip == 0))
    late = (top & (chip > 0)) | (jnp.logical_not(bottom) & (chip == 1) & (group == groups - 2))
    send_coupling(soon)
    leave(swap_x, lambda: pt.at[OWN], E_X2)

    @pl.when(swap_x)
    def _():
        got_factor(XF)

    send_factor(swap_x, XF, LOW, core, E_LOW)

    @pl.when(swap_x)
    def _():
        load_factor(XF, SX)

    def ordered(condition, early, k, r, a, b):
        @pl.when(condition & early)
        def _():
            high[a], low[a], high[b], low[b] = high[k], low[k], high[r], low[r]

        @pl.when(condition & jnp.logical_not(early))
        def _():
            high[a], low[a], high[b], low[b] = high[r], low[r], high[k], low[k]

    ordered(swap_x, xe, SC, SX, SA, SB)
    swap_y = even & rest
    tells = rest & jnp.logical_not(bottom & (chip == 0))
    hears = rest & jnp.logical_not(bottom & (chip == 2))
    for a, b, parts in pieces:
        @pl.when(swap_x)
        def _(a=a, b=b):
            multiply(a, b, SA, SB, PAIR, SP)
        send_factor(even & tells, PAIR, YF, py, E_Y, parts)
    send_factor(even & tells, PAIR, YF, py, E_Y, (4, 5), ends=E_Y2)
    send_factor(swap_x & ye, PAIR, ZF, core, E_PAIR)

    o_fold = odd & (rest | (chip < 3))

    def neighbour(condition):
        @pl.when(condition)
        def _():
            got_factor(LOW)
            load_factor(LOW, SX)

    neighbour(odd & turns & xl)

    @pl.when(o_fold)
    def _():
        got_offset(XO)

    @pl.when(o_fold & xe)
    def _():
        spread(XO, to_slot(SZ))

    @pl.when(o_fold & xl)
    def _():
        spread(OWN, to_slot(SZ))

    stepped = odd & top & (chip == 2)

    def after_pair(s):
        parts = (2 * s, 2 * s + 1)
        send_offset(stepped, PAIR, YO, py, O_Y, parts)
        send_offset(stepped, PAIR, YO, me - 2, O_TO, parts)

    @pl.when(stepped)
    def _():
        fold(stepped, SC, OWN, PAIR, after_pair)

    @pl.when(o_fold & xe & jnp.logical_not(stepped))
    def _():
        fold_at_once(SC, OWN, PAIR)

    @pl.when(o_fold & xl)
    def _():
        fold_at_once(SX, XO, PAIR)

    wait_sent(even & tells, pm.at[PAIR, :, :WIDE], E_Y)

    @pl.when(swap_y)
    def _():
        pl.semaphore_signal(turn, inc=1, device_id=(core,), device_id_type=MESH)

    @pl.when(odd & rest)
    def _():
        pl.semaphore_wait(turn, 1)

    send_offset(odd & tells, PAIR, YO, py, O_Y)
    leave(even & tells, lambda: pt.at[PAIR], E_Y2)
    hears_late = even & hears & yl
    down = even & (group == 1) & rest & joined
    even_chain = even & chain
    hand = swap_y & (chip < 3)

    @pl.when(even)
    def _():

        @pl.when(even & hears)
        def _():
            got_factor(YF)

        send_factor(hears_late, YF, ZF, core, E_PAIR)

        @pl.when(even & hears)
        def _():
            load_factor(YF, SY)

        ordered(even & hears, ye, SP, SY, SA, SB)
        for i in range(2):
            @pl.when(even & hears)
            def _(i=i):
                multiply(i * half, (i + 1) * half, SA, SB, ALL, SR)
            send_factor(down & (b1 == i), ALL, ZF, me - GROUP, E_ALL, (2 * i, 2 * i + 1))
        for i in range(2):
            send_factor(down & (b1 == i), ALL, ZF, me - GROUP, E_ALL, (4 + i,), recv=R_ENDS, last=None)
        leave(down, lambda: half_tally, E_ALL)
        send_factor(even_chain, ALL, ALL, core, E_ALL)

        @pl.when(swap_y & (chip == 0))
        def _():
            for i in range(2):
                multiply(i * half, (i + 1) * half, SX, SY, None, SB)
            high[SA], low[SA] = high[SR], low[SR]

        @pl.when(swap_y & (chip == 1))
        def _():
            for i in range(2):
                multiply(i * half, (i + 1) * half, SC, SY, None, SA)
            high[SB], low[SB] = high[SY], low[SY]

        @pl.when(swap_y & (chip == 2))
        def _():
            high[SA], low[SA] = high[SP], low[SP]
            high[SB], low[SB] = high[SX], low[SX]

        @pl.when(swap_y & (chip == 3))
        def _():
            high[SA], low[SA] = high[SC], low[SC]


        @pl.when(hand)
        def _():
            for i in range(2):
                multiply(i * half, (i + 1) * half, SM, SB, LAST)

        send_factor(hand, LAST, LAST, core, E_LAST)

    z_fold = odd & (hears | (top & ye))

    @pl.when(z_fold)
    def _():
        got_factor(ZF)
        load_factor(ZF, SP)

    sharing = groups >= 4
    hands = odd & ye & (group == groups - 2) & sharing
    passes = odd & top & yl & sharing
    @pl.when(passes)
    def _():
        for q in range(PARTS // 2):
            @pl.when(passes)
            def _(q=q):
                got_edge(q)

            send_offset(passes, EDGE, EDGE, me - GROUP, O_NEAR, (q,), PARTS // 2, last=1)

    def take_edge(condition, hand_on, quarters):
        for q in quarters:
            @pl.when(condition)
            def _(q=q):
                got_edge(q)

            send_offset(hand_on, EDGE, EDGE, core, O_TO, (q,), last=None)

    take_edge(hands, hands, (0, 1))

    @pl.when(hands)
    def _():
        spread(EDGE, to_slot(SE), (0,))

    @pl.when(z_fold)
    def _():
        got_offset(YO)

    send_coupling(jnp.logical_not(soon | late))

    @pl.when(odd & hears & yl)
    def _():
        spread(PAIR, to_slot(SZ))

    @pl.when(z_fold & ye)
    def _():
        spread(YO, to_slot(SZ))

    far = group == 2 if joined else me < 0
    near = (group >= 2) if joined else (group >= 1)

    shared = (2, 3) if sharing else range(PARTS)
    heads = odd & top & ye
    heads_near, heads_far, heads_share = heads & near, heads & far, heads & sharing

    def after_all(s):
        parts = (2 * s, 2 * s + 1)
        send_offset(heads_near, ALL, EDGE, me - GROUP, O_NEAR, parts)
        send_offset(heads_far, ALL, EDGE, me - 2 * GROUP, O_FAR, parts)
        if s == 0:
            send_offset(heads_share, ALL, EDGE, py, O_TO, parts, PARTS // 2, last=1)
        else:
            send_offset(heads_near, ALL, EDGE, me - GROUP + 4, O_NEAR2, shared, len(shared))

    gives = odd & rest & (group == 1) & joined

    @pl.when(odd & hears & ye & jnp.logical_not(hands | gives))
    def _():
        fold_at_once(SP, PAIR, ALL)

    @pl.when(odd & hears & yl & jnp.logical_not(gives))
    def _():
        fold_at_once(SP, YO, ALL)

    def after_given(s):
        send_offset(gives, ALL, ZO, me - GROUP, O_Z, (2 * s, 2 * s + 1), recv=R_ZO[s])

    @pl.when(gives)
    def _():
        @pl.when(gives & ye)
        def _():
            so[BASE] = so[PAIR]

        @pl.when(gives & yl)
        def _():
            so[BASE] = so[YO]

        fold(gives & jnp.logical_not(hands), SP, BASE, ALL, after_given)

    @pl.when(heads)
    def _():
        fold(heads, SP, PAIR, ALL, after_all)
        send_offset(heads_far, ALL, EDGE, me - 2 * GROUP + 4, O_FAR2)

    @pl.when(odd & chain)
    def _():
        got_factor(ALL)
        load_factor(ALL, SR)

    alone = odd & chain & jnp.logical_not(hands)
    for s in range(2):
        taken = alone if s == 0 else odd & chain
        take_edge(taken, taken, (2 * s, 2 * s + 1))

        @pl.when(taken)
        def _(s=s):
            spread(EDGE, to_slot(SE), (s,))

    leave(odd & chain, lambda: so.at[EDGE], O_TO)

    routes = {
        who: (condition & near & jnp.logical_not(far), condition & near & far, condition & far)
        for who, condition in (("hands", hands), ("alone", alone))
    }

    def after_chain(who, s):
        parts = (2 * s, 2 * s + 1)
        only, also, to_far = routes[who]
        send_offset(to_far, CHAIN, EDGE, me - 2 * GROUP, O_FAR, parts)
        send_offset(only, CHAIN, EDGE, me - GROUP, O_NEAR, parts)
        if s == 1:
            send_offset(also, CHAIN, EDGE, me - GROUP, O_NEAR2)

    @pl.when(hands)
    def _():
        for s in range(2):
            @pl.when(hands)
            def _(s=s):
                fold_left(s, SR, SE, SV)
                fold_left(s, SP)
                fold_right(s, SP, PAIR, ALL)
                fold_right(s, SR, ALL, CHAIN, SV)

            after_chain("hands", s)

    @pl.when(alone)
    def _():
        for s in range(2):
            @pl.when(alone)
            def _(s=s):
                fold_left(s, SR, SE)
                fold_right(s, SR, ALL, CHAIN)

            after_chain("alone", s)

    neighbour(odd & turns & xe)
    send_coupling(late)

    send_offset(odd & (chip == 0), ALL, EVEN, core, O_EVEN)
    send_offset(odd & (chip == 2), PAIR, EVEN, core, O_EVEN)
    send_offset(odd & (chip == 3), OWN, EVEN, core, O_EVEN)
    low_y = odd & ye

    @pl.when(low_y)
    def _():
        spread(YO, to_slot(SZ))

    @pl.when(low_y & (chip == 1))
    def _():
        high[SA], low[SA] = high[SC], low[SC]
        so[BASE] = so[OWN]

    @pl.when(low_y & (chip == 0))
    def _():
        high[SA], low[SA] = high[SX], low[SX]
        so[BASE] = so[XO]

    @pl.when(low_y)
    def _():
        fold_at_once(SA, BASE, EVEN)

    send_offset(odd & (chip == 1), EVEN, EVEN, core, O_EVEN)

    @pl.when(odd & (chip == 0))
    def _():
        spread(EVEN, to_slot(SZ))

    @pl.when(odd & (chip == 1))
    def _():
        spread(YO, to_slot(SZ))

    @pl.when(odd & (chip == 2))
    def _():
        spread(XO, to_slot(SZ))

    @pl.when(odd & (chip < 3))
    def _():
        fold_whole(SM, g_ref, acc)

    @pl.when(odd & (chip == 3))
    def _():
        acc[...] = g_ref[...]

    @pl.when(odd & rest & (chip < 3))
    def _():
        got_factor(LAST)
        load_factor(LAST, SA)

    @pl.when(odd & rest & (chip == 3))
    def _():
        high[SA], low[SA] = high[SM], low[SM]

    for parts, ref, recv in (
        ((0, 1, 2, 3), pm.at[ZF, :half, :WIDE], R_FACTOR[ZF]), ((4, 5), factor(ZF)[4], R_ENDS),
    ):
        @pl.when(bottom & even)
        def _(ref=ref, recv=recv):
            copy(ref, ref, sent.at[0], got.at[recv], me).wait_recv()

        count = len(parts) // 2
        for i in range(2):
            mine = parts[i * count:(i + 1) * count]
            send_factor(bottom & even & (b1 == i), ZF, ZF, px, E_X, mine, recv=R_ZF2, last=None)
            send_factor(bottom & even & (b1 == i), ZF, YF, core, E_ALL, mine, last=None)

    @pl.when(even)
    def _():
        got_offset(EVEN)
        spread(EVEN, to_ref(acc))

    @pl.when(bottom & even)
    def _():
        copy(half_tally, half_tally, sent.at[0], got.at[R_ZF2], me).wait_recv()

    for i in range(2):
        send_factor(bottom & even & (b1 != i), ZF, YF, core, E_ALL, (2 * i, 2 * i + 1, 4 + i), last=None)

    @pl.when(bottom & even)
    def _():
        load_factor(ZF, SR)

    @pl.when(odd)
    def _():
        split(other[...], qh_ref, ql_ref)

    @pl.when(even & (me > 0))
    def _():
        copy(prev, prev, n_send, n_recv, me).wait_recv()
        split(prev[...], qh_ref, ql_ref)

    @pl.when(me == 0)
    def _():
        qh_ref[...] = jnp.zeros_like(qh_ref)
        ql_ref[...] = jnp.zeros_like(ql_ref)

    apart = odd & rest & jnp.logical_not(chain)
    waits = rest & (even | jnp.logical_not(chain))
    drain()
    for s in range(2):
        take_edge(waits, apart, (2 * s, 2 * s + 1))

        @pl.when(rest)
        def _(s=s):
            spread(EDGE, to_slot(SZ), (s,))

    leave(apart, lambda: so.at[EDGE], O_TO)

    def got_given(s):
        ref = so.at[ZO, quarter(2 * s, 2), :]
        copy(ref, ref, sent.at[0], got.at[R_ZO[s]], me).wait_recv()

    for s in range(2):
        @pl.when(bottom & odd)
        def _(s=s):
            got_given(s)

        send_offset(bottom & odd, ZO, ZO, core, O_Z, (2 * s, 2 * s + 1), recv=R_ZO[s])

    leave(bottom & even, lambda: half_tally, E_X)
    leave(bottom & even, lambda: tally, E_ALL)

    @pl.when(bottom & odd)
    def _():
        got_factor(YF)
        load_factor(YF, SR)

    @pl.when(bottom)
    def _():
        fold_left(0, SR)
        fold_left(1, SR)

    @pl.when(bottom & even)
    def _():
        got_given(0)
        got_given(1)

    @pl.when(bottom)
    def _():
        fold_right(0, SR, ZO, CHAIN)
        fold_right(1, SR, ZO, CHAIN)
        spread(CHAIN, to_slot(SZ))

    @pl.when(rest)
    def _():
        fold_whole(SA, acc, x_ref, (xh_ref, xl_ref))

    @pl.when(top)
    def _():
        x_ref[...] = acc[...]
        split(acc[...], xh_ref, xl_ref)

    drain()


def finish(x_ref, xh, xl, qh, ql, d_any, c_any, c_ref, sem):
    copies = [pltpu.make_async_copy(x_ref, d_any, sem.at[0])]
    copies[0].start()
    half = x_ref.shape[0] // 2
    for i in range(2):
        rows = slice(i * half, (i + 1) * half)
        c_ref[rows, :] = product((xh.at[rows, :], xl.at[rows, :]), (qh, ql), NT)
        copies.append(pltpu.make_async_copy(c_ref.at[rows, :], c_any.at[rows, :], sem.at[1 + i]))
        copies[-1].start()
    for c in copies:
        c.wait()


def local(n, schur_inverse, sweep_factor):
    order = schur_inverse.shape[1]
    full = (order, order)
    f32, bf16 = jnp.float32, jnp.bfloat16
    dma = pltpu.SemaphoreType.DMA
    values = pl.pallas_call(
        functools.partial(kernel, n),
        out_shape=[pltpu.VMEM(full, f32)] + [pltpu.VMEM(full, bf16)] * 4,
        in_specs=[pl.BlockSpec(memory_space=pl.ANY)] * 2,
        out_specs=[pl.BlockSpec(memory_space=pltpu.VMEM)] * 5,
        scratch_shapes=[pltpu.VMEM(full, f32)] * 5 + [
            pltpu.VMEM((8,) + full, f32),
            pltpu.VMEM((8, order // 2, STRIP), f32),
            pltpu.VMEM((10, WIDE, WIDE), f32),
            pltpu.VMEM((13,) + full, bf16),
            pltpu.VMEM((13,) + full, bf16),
            pltpu.VMEM((order * WIDE // STRIP + order // 2, STRIP), f32),
            dma((9,)), dma((12 + PARTS,)), dma, dma, dma, dma, dma((2,)), pltpu.SemaphoreType.REGULAR,
        ],
        compiler_params=pltpu.CompilerParams(
            collective_id=0, has_side_effects=True
        ),
    )(schur_inverse[0], sweep_factor[0])
    diagonal, coupling = pl.pallas_call(
        finish,
        out_shape=[jax.ShapeDtypeStruct(full, f32)] * 2,
        in_specs=[pl.BlockSpec(memory_space=pltpu.VMEM)] * 5,
        out_specs=[pl.BlockSpec(memory_space=pl.ANY)] * 2,
        scratch_shapes=[pltpu.VMEM(full, f32), dma((3,))],
    )(*(pltpu.with_memory_space_constraint(v, pltpu.VMEM) for v in values))
    return diagonal[None], coupling[None]


def solution(mesh):
    n = mesh.shape["tm"]
    return jax.shard_map(
        functools.partial(local, n),
        mesh=mesh,
        in_specs=(P("tm", None, None), P("tm", None, None)),
        out_specs=(P("tm", None, None), P("tm", None, None)),
        check_vma=False,
    )
```

```python
import functools

import jax
import jax.numpy as jnp
from jax import lax
from jax.experimental import pallas as pl
from jax.experimental.pallas import tpu as pltpu
from jax.sharding import PartitionSpec as P

MESH = pl.DeviceIdType.MESH
STRIP = 128
WIDE = 2 * STRIP
GROUP = 8
NN = (((1,), (0,)), ((), ()))
NT = (((1,), (1,)), ((), ()))

OWN, PAIR, ALL, LAST, XF, YF, ZF, LOW = range(8)
CHAIN, EVEN, XO, YO, EDGE, ZO, BASE = range(3, 10)
SL, SM, SC, SX, SY, SP, SA, SB, SR, SZ, SW, SE, SV = range(13)
E_BASE, E_X, E_X2, E_LOW, E_PAIR, E_Y, E_Y2, E_ALL, E_LAST = range(9)
O_X, O_Y, O_TO, O_NEAR, O_NEAR2, O_FAR, O_FAR2, O_Z, O_EVEN = range(9)
R_FACTOR = {XF: 0, YF: 1, ZF: 2, LOW: 0, ALL: 3, LAST: 4}
R_OFFSET = {BASE: 5, EVEN: 5, XO: 6, YO: 7, ZO: 8, EDGE: 9}
R_ZF2, R_ENDS, R_ZO = 13, 14, (8, 15)
PARTS = 4


def dot(left, right, dims):
    return lax.dot_general(left, right, dims, preferred_element_type=jnp.float32)


def split(value, high, low):
    top = value.astype(jnp.bfloat16)
    high[...] = top
    low[...] = (value - top.astype(jnp.float32)).astype(jnp.bfloat16)


def product(left, right, dims):
    lh, ll = left
    rh, rl = right
    return (
        dot(lh[...], rl[...], dims) + dot(ll[...], rh[...], dims)
    ) + dot(lh[...], rh[...], dims)


def kernel(n, g_any, l_any, x_ref, xh_ref, xl_ref, qh_ref, ql_ref, *scratch):
    (g_ref, l_ref, other, prev, acc, pm, pt, so, high, low, tally,
     sent, got, l_send, l_recv, n_send, n_recv, in_sem, turn) = scratch
    order = g_ref.shape[0]
    half = order // 2
    tail = order - WIDE
    groups = n // GROUP
    joined = groups >= 3
    me = lax.axis_index("tm")
    j = lax.rem(me, GROUP)
    group = me // GROUP
    b0, b1, b2 = (lax.rem(j // d, 2) for d in (1, 2, 4))
    even, odd = b0 == 0, b0 == 1
    chip = j // 2
    xe, xl, ye, yl = b1 == 0, b1 == 1, b2 == 0, b2 == 1
    top = group == groups - 1
    rest = group < groups - 1
    bottom = (group == 0) & joined
    chain = rest & (group >= (2 if joined else 1))
    core = me + 1 - 2 * b0
    px = me + 2 - 4 * b1
    py = me + 4 - 8 * b2

    g_in = pltpu.make_async_copy(g_any, g_ref, in_sem.at[0])
    l_in = pltpu.make_async_copy(l_any, l_ref, in_sem.at[1])
    l_in.start()
    g_in.start()

    barrier = pltpu.get_barrier_semaphore()
    total = 0
    always = me >= 0
    for other_id, inside in (
        (core, always), (px, always), (py, always),
        (me + 2, odd & top & (chip == 1)), (me - 2, odd & top & (chip == 2)),
        (me - GROUP, group > 0), (me + GROUP, rest),
        (me - 2 * GROUP, odd & (group == 2)), (me + 2 * GROUP, odd & (group == 0) & (groups > 2)),
        (me - GROUP + 4, odd & top & ye & (group > 0)), (me + GROUP - 4, odd & yl & (group == groups - 2)),
        (me - 2 * GROUP + 4, odd & top & ye & (group == 2)),
        (me + 2 * GROUP - 4, odd & yl & (group == 0) & (groups == 3)),
        (me + 1, odd & (me < n - 1)), (me - 1, even & (me > 0)),
    ):
        total = total + inside.astype(jnp.int32)

        @pl.when(inside)
        def _(other_id=other_id):
            pl.semaphore_signal(barrier, inc=1, device_id=(other_id,), device_id_type=MESH)

    first, second, third = slice(0, STRIP), slice(STRIP, WIDE), slice(WIDE, order)
    left, right = slice(0, tail), slice(tail, 2 * tail)

    def slot(i, a=0, b=order):
        return high.at[i, a:b, :], low.at[i, a:b, :]

    def fill(i, value):
        split(value, *slot(i))

    def copy(src, dst, send, recv, target):
        return pltpu.make_async_remote_copy(
            src_ref=src, dst_ref=dst, send_sem=send, recv_sem=recv,
            device_id=(target,), device_id_type=MESH,
        )

    pending = []

    def start(condition, make):
        @pl.when(condition)
        def _():
            make().start()

    def send(condition, make):
        start(condition, make)
        pending.append((condition, make))

    def drain():
        for condition, make in pending:
            @pl.when(condition)
            def _(make=make):
                make().wait_send()
        pending.clear()

    def factor(i):
        mid = half // 2
        return tuple(pm.at[i, a:a + mid, :WIDE] for a in range(0, order, mid)) + (pt.at[i, :mid], pt.at[i, mid:])

    def quarter(s, count=1):
        return slice(s * WIDE // PARTS, (s + count) * WIDE // PARTS)

    half_tally = tally.at[:tally.shape[0] // 2, :]

    def leave(condition, make_ref, sem):
        def make():
            ref = make_ref()
            return copy(ref, ref, sent.at[sem], got.at[0], core)

        pending.append((condition, make))

    def send_factor(condition, src, dst, target, sem, parts=range(6), ends=None, recv=None, last=5):
        for s in parts:
            start(
                condition,
                lambda s=s: copy(
                    factor(src)[s], factor(dst)[s],
                    sent.at[ends if s >= 4 and ends is not None else sem],
                    got.at[R_FACTOR[dst] if recv is None else recv], target,
                ),
            )
        if last in parts and ends is None:
            leave(condition, lambda: tally, sem)

    def send_offset(condition, src, dst, target, sem, parts=range(PARTS), count=PARTS, recv=None, last=PARTS - 1):
        for s in parts:
            start(
                condition,
                lambda s=s: copy(
                    so.at[src, quarter(s), :], so.at[dst, quarter(s), :],
                    sent.at[sem],
                    got.at[R_OFFSET[dst] + (s if dst == EDGE else 0) if recv is None else recv], target,
                ),
            )
        if last in parts:
            leave(condition, lambda: so.at[src, quarter(0, count), :], sem)

    def wait_sent(condition, ref, sem):
        @pl.when(condition)
        def _():
            copy(ref, ref, sent.at[sem], got.at[0], core).wait_send()

    def got_factor(i):
        copy(tally, tally, sent.at[0], got.at[R_FACTOR[i]], me).wait_recv()

    def got_offset(i):
        copy(so.at[i], so.at[i], sent.at[0], got.at[R_OFFSET[i]], me).wait_recv()

    def got_edge(s):
        ref = so.at[EDGE, quarter(s), :]
        copy(ref, ref, sent.at[0], got.at[R_OFFSET[EDGE] + s], me).wait_recv()

    def load_factor(i, k):
        h, l = high.at[k], low.at[k]
        split(pm[i, :, :WIDE], h.at[:, :WIDE], l.at[:, :WIDE])
        ends = pt[i]
        split(ends[:, :tail], h.at[:half, third], l.at[:half, third])
        split(ends[:, tail:2 * tail], h.at[half:, third], l.at[half:, third])

    def multiply(a, b, k, r, out, into=None):
        value = product(slot(k, a, b), slot(r), NN)
        if out is not None:
            pm[out, a:b, :WIDE] = value[:, :WIDE]
            side, low_row = a // half, a // half * half
            pt[out, a - low_row:b - low_row, side * tail:(side + 1) * tail] = value[:, third]
        if into is not None:
            split(value, *slot(into, a, b))

    pieces = ((0, half // 2, (0,)), (half // 2, half, (1,)), (half, order, (2, 3)))

    def pack(ref, i):
        so[i, first, :] = ref[first, :WIDE]
        so[i, second, left] = ref[first, third]
        so[i, second, right] = ref[second, third]
        so[i, STRIP:STRIP + tail, second] = ref[STRIP:STRIP + tail, second]
        so[i, STRIP + tail:WIDE, STRIP + tail:] = ref[STRIP + tail:WIDE, STRIP + tail:WIDE]
        so[i, STRIP + tail:WIDE, STRIP:STRIP + tail] = ref[third, third]

    def spread(i, put, parts=(0, 1)):
        if 0 in parts:
            put(so[i, first, :], first, slice(0, WIDE))
            put(so[i, first, second].T, second, first)
        if 1 in parts:
            ends = so[i, second, first]
            turned = ends.T
            put(ends[:, :tail], first, third)
            put(ends[:, tail:2 * tail], second, third)
            put(turned[:tail], third, first)
            put(turned[tail:2 * tail], third, second)
            block = so[i, second, second]
            lanes = lax.broadcasted_iota(jnp.int32, (STRIP - tail, STRIP), 1)
            put(block[:tail], slice(STRIP, STRIP + tail), second)
            put(jnp.where(lanes < tail, block.T[tail:], block[tail:]), slice(STRIP + tail, WIDE), second)
            put(block[tail:, :tail], third, third)

    def to_slot(k):
        def put(value, rows, columns):
            split(value, high.at[k, rows, columns], low.at[k, rows, columns])
        return put

    def to_ref(ref):
        def put(value, rows, columns):
            ref[rows, columns] = value
        return put

    def fold_left(s, k, z=SZ, w=SW):
        a, b = ((0, STRIP), (STRIP, order))[s]
        split(product(slot(k, a, b), slot(z), NN), *slot(w, a, b))

    def fold_right(s, k, base, out, w=SW):
        a, b = ((0, STRIP), (STRIP, order))[s]
        term = product(slot(w, a, b), slot(k, a), NT)
        if s == 0:
            so[out, first, :] = so[base, first, :] + term[:, :WIDE]
            so[out, second, left] = so[base, second, left] + term[:, WIDE:]
        else:
            lower = slice(STRIP + tail, WIDE)
            so[out, second, right] = so[base, second, right] + term[:STRIP, STRIP:]
            so[out, STRIP:STRIP + tail, second] = so[base, STRIP:STRIP + tail, second] + term[:tail, :STRIP]
            so[out, lower, lower] = so[base, lower, lower] + term[tail:STRIP, tail:STRIP]
            so[out, lower, STRIP:STRIP + tail] = so[base, lower, STRIP:STRIP + tail] + term[STRIP:, STRIP:]

    def fold(condition, k, base, out, after):
        for s in range(2):
            @pl.when(condition)
            def _(s=s):
                fold_left(s, k)
                fold_right(s, k, base, out)
            after(s)

    def fold_at_once(k, base, out):
        fold_left(0, k)
        fold_left(1, k)
        fold_right(0, k, base, out)
        fold_right(1, k, base, out)

    def fold_whole(k, base, out, parts=None):
        for a in (0, half):
            split(product(slot(k, a, a + half), slot(SZ), NN), *slot(SW, a, a + half))
        for a in (0, half):
            value = base[a:a + half, :] + product(slot(SW, a, a + half), slot(k), NT)
            out[a:a + half, :] = value
            if parts is not None:
                split(value, parts[0].at[a:a + half, :], parts[1].at[a:a + half, :])

    l_in.wait()

    @pl.when(even)
    def _():
        fill(SL, l_ref[...])

    @pl.when(odd)
    def _():
        fill(SM, l_ref[...])

    g_in.wait()

    @pl.when(even)
    def _():
        pack(g_ref, BASE)

    @pl.when(odd)
    def _():
        fill(SZ, g_ref[...])

    pl.semaphore_wait(barrier, total)

    send(always, lambda: copy(l_ref, other, l_send, l_recv, core))
    send_offset(even, BASE, BASE, core, E_BASE)

    swap_x = even & (rest | ye)

    copy(other, other, l_send, l_recv, me).wait_recv()

    @pl.when(even)
    def _():
        fill(SM, other[...])

    for a, b, parts in pieces:
        @pl.when(even)
        def _(a=a, b=b):
            multiply(a, b, SL, SM, OWN, SC)
        send_factor(swap_x, OWN, XF, px, E_X, parts)
    send_factor(swap_x, OWN, XF, px, E_X, (4, 5), ends=E_X2)

    early_o = odd & top & (chip == 3)

    @pl.when(odd)
    def _():
        fill(SL, other[...])
        fold_left(0, SL)
        got_offset(BASE)
        fold_right(0, SL, BASE, OWN)

    send_offset(early_o, OWN, XO, px, O_X, (0, 1))

    @pl.when(odd)
    def _():
        fold_left(1, SL)
        fold_right(1, SL, BASE, OWN)

    send_offset(early_o, OWN, XO, px, O_X, (2, 3))

    @pl.when(odd)
    def _():
        for i in range(2):
            multiply(i * half, (i + 1) * half, SL, SM, None, SC)

    turns = rest | ye
    wait_sent(swap_x, pm.at[OWN, :, :WIDE], E_X)

    @pl.when(swap_x)
    def _():
        pl.semaphore_signal(turn, inc=1, device_id=(core,), device_id_type=MESH)

    @pl.when(odd & turns)
    def _():
        pl.semaphore_wait(turn, 1)

    send_offset(odd & turns, OWN, XO, px, O_X)

    def send_coupling(condition):
        send(odd & condition & (me < n - 1), lambda: copy(l_ref, prev, n_send, n_recv, me + 1))

    soon = (rest & xe) | (bottom & (chip == 1)) | (top & (chip == 0))
    late = (top & (chip > 0)) | (jnp.logical_not(bottom) & (chip == 1) & (group == groups - 2))
    send_coupling(soon)
    leave(swap_x, lambda: pt.at[OWN], E_X2)

    @pl.when(swap_x)
    def _():
        got_factor(XF)

    send_factor(swap_x, XF, LOW, core, E_LOW)

    @pl.when(swap_x)
    def _():
        load_factor(XF, SX)

    def ordered(condition, early, k, r, a, b):
        @pl.when(condition & early)
        def _():
            high[a], low[a], high[b], low[b] = high[k], low[k], high[r], low[r]

        @pl.when(condition & jnp.logical_not(early))
        def _():
            high[a], low[a], high[b], low[b] = high[r], low[r], high[k], low[k]

    ordered(swap_x, xe, SC, SX, SA, SB)
    swap_y = even & rest
    tells = rest & jnp.logical_not(bottom & (chip == 0))
    hears = rest & jnp.logical_not(bottom & (chip == 2))
    for a, b, parts in pieces:
        @pl.when(swap_x)
        def _(a=a, b=b):
            multiply(a, b, SA, SB, PAIR, SP)
        send_factor(even & tells, PAIR, YF, py, E_Y, parts)
    send_factor(even & tells, PAIR, YF, py, E_Y, (4, 5), ends=E_Y2)
    send_factor(swap_x & ye, PAIR, ZF, core, E_PAIR)

    o_fold = odd & (rest | (chip < 3))

    def neighbour(condition):
        @pl.when(condition)
        def _():
            got_factor(LOW)
            load_factor(LOW, SX)

    neighbour(odd & turns & xl)

    @pl.when(o_fold)
    def _():
        got_offset(XO)

    @pl.when(o_fold & xe)
    def _():
        spread(XO, to_slot(SZ))

    @pl.when(o_fold & xl)
    def _():
        spread(OWN, to_slot(SZ))

    stepped = odd & top & (chip == 2)

    def after_pair(s):
        parts = (2 * s, 2 * s + 1)
        send_offset(stepped, PAIR, YO, py, O_Y, parts)
        send_offset(stepped, PAIR, YO, me - 2, O_TO, parts)

    @pl.when(stepped)
    def _():
        fold(stepped, SC, OWN, PAIR, after_pair)

    @pl.when(o_fold & xe & jnp.logical_not(stepped))
    def _():
        fold_at_once(SC, OWN, PAIR)

    @pl.when(o_fold & xl)
    def _():
        fold_at_once(SX, XO, PAIR)

    wait_sent(even & tells, pm.at[PAIR, :, :WIDE], E_Y)

    @pl.when(swap_y)
    def _():
        pl.semaphore_signal(turn, inc=1, device_id=(core,), device_id_type=MESH)

    @pl.when(odd & rest)
    def _():
        pl.semaphore_wait(turn, 1)

    send_offset(odd & tells, PAIR, YO, py, O_Y)
    leave(even & tells, lambda: pt.at[PAIR], E_Y2)
    hears_late = even & hears & yl
    down = even & (group == 1) & rest & joined
    even_chain = even & chain
    hand = swap_y & (chip < 3)

    @pl.when(even)
    def _():

        @pl.when(even & hears)
        def _():
            got_factor(YF)

        send_factor(hears_late, YF, ZF, core, E_PAIR)

        @pl.when(even & hears)
        def _():
            load_factor(YF, SY)

        ordered(even & hears, ye, SP, SY, SA, SB)
        for i in range(2):
            @pl.when(even & hears)
            def _(i=i):
                multiply(i * half, (i + 1) * half, SA, SB, ALL, SR)
            send_factor(even_chain, ALL, ALL, core, E_ALL, (2 * i, 2 * i + 1))
            send_factor(down & (b1 == i), ALL, ZF, me - GROUP, E_ALL, (2 * i, 2 * i + 1))
        for i in range(2):
            send_factor(down & (b1 == i), ALL, ZF, me - GROUP, E_ALL, (4 + i,), recv=R_ENDS, last=None)
        leave(down, lambda: half_tally, E_ALL)
        send_factor(even_chain, ALL, ALL, core, E_ALL, (4, 5))

        @pl.when(swap_y & (chip == 0))
        def _():
            for i in range(2):
                multiply(i * half, (i + 1) * half, SX, SY, None, SB)
            high[SA], low[SA] = high[SR], low[SR]

        @pl.when(swap_y & (chip == 1))
        def _():
            for i in range(2):
                multiply(i * half, (i + 1) * half, SC, SY, None, SA)
            high[SB], low[SB] = high[SY], low[SY]

        @pl.when(swap_y & (chip == 2))
        def _():
            high[SA], low[SA] = high[SP], low[SP]
            high[SB], low[SB] = high[SX], low[SX]

        @pl.when(swap_y & (chip == 3))
        def _():
            high[SA], low[SA] = high[SC], low[SC]


        @pl.when(hand)
        def _():
            for i in range(2):
                multiply(i * half, (i + 1) * half, SM, SB, LAST)

        send_factor(hand, LAST, LAST, core, E_LAST)

    z_fold = odd & (hears | (top & ye))

    @pl.when(z_fold)
    def _():
        got_factor(ZF)
        load_factor(ZF, SP)

    sharing = groups >= 4
    hands = odd & ye & (group == groups - 2) & sharing
    passes = odd & top & yl & sharing
    @pl.when(passes)
    def _():
        for q in range(PARTS // 2):
            @pl.when(passes)
            def _(q=q):
                got_edge(q)

            send_offset(passes, EDGE, EDGE, me - GROUP, O_NEAR, (q,), PARTS // 2, last=1)

    def take_edge(condition, hand_on, quarters):
        for q in quarters:
            @pl.when(condition)
            def _(q=q):
                got_edge(q)

            send_offset(hand_on, EDGE, EDGE, core, O_TO, (q,), last=None)

    take_edge(hands, hands, (0, 1))

    @pl.when(hands)
    def _():
        spread(EDGE, to_slot(SE), (0,))

    @pl.when(z_fold)
    def _():
        got_offset(YO)

    send_coupling(jnp.logical_not(soon | late))

    @pl.when(odd & hears & yl)
    def _():
        spread(PAIR, to_slot(SZ))

    @pl.when(z_fold & ye)
    def _():
        spread(YO, to_slot(SZ))

    far = group == 2 if joined else me < 0
    near = (group >= 2) if joined else (group >= 1)

    shared = (2, 3) if sharing else range(PARTS)
    heads = odd & top & ye
    heads_near, heads_far, heads_share = heads & near, heads & far, heads & sharing

    def after_all(s):
        parts = (2 * s, 2 * s + 1)
        send_offset(heads_near, ALL, EDGE, me - GROUP, O_NEAR, parts)
        send_offset(heads_far, ALL, EDGE, me - 2 * GROUP, O_FAR, parts)
        if s == 0:
            send_offset(heads_share, ALL, EDGE, py, O_TO, parts, PARTS // 2, last=1)
        else:
            send_offset(heads_near, ALL, EDGE, me - GROUP + 4, O_NEAR2, shared, len(shared))

    gives = odd & rest & (group == 1) & joined

    @pl.when(odd & hears & ye & jnp.logical_not(hands | gives))
    def _():
        fold_at_once(SP, PAIR, ALL)

    @pl.when(odd & hears & yl & jnp.logical_not(gives))
    def _():
        fold_at_once(SP, YO, ALL)

    def after_given(s):
        send_offset(gives, ALL, ZO, me - GROUP, O_Z, (2 * s, 2 * s + 1), recv=R_ZO[s])

    @pl.when(gives)
    def _():
        @pl.when(gives & ye)
        def _():
            so[BASE] = so[PAIR]

        @pl.when(gives & yl)
        def _():
            so[BASE] = so[YO]

        fold(gives & jnp.logical_not(hands), SP, BASE, ALL, after_given)

    @pl.when(heads)
    def _():
        fold(heads, SP, PAIR, ALL, after_all)
        send_offset(heads_far, ALL, EDGE, me - 2 * GROUP + 4, O_FAR2)

    @pl.when(odd & chain)
    def _():
        got_factor(ALL)
        load_factor(ALL, SR)

    alone = odd & chain & jnp.logical_not(hands)
    for s in range(2):
        taken = alone if s == 0 else odd & chain
        take_edge(taken, taken, (2 * s, 2 * s + 1))

        @pl.when(taken)
        def _(s=s):
            spread(EDGE, to_slot(SE), (s,))

    leave(odd & chain, lambda: so.at[EDGE], O_TO)

    routes = {
        who: (condition & near & jnp.logical_not(far), condition & near & far, condition & far)
        for who, condition in (("hands", hands), ("alone", alone))
    }

    def after_chain(who, s):
        parts = (2 * s, 2 * s + 1)
        only, also, to_far = routes[who]
        send_offset(to_far, CHAIN, EDGE, me - 2 * GROUP, O_FAR, parts)
        send_offset(only, CHAIN, EDGE, me - GROUP, O_NEAR, parts)
        if s == 1:
            send_offset(also, CHAIN, EDGE, me - GROUP, O_NEAR2)

    @pl.when(hands)
    def _():
        for s in range(2):
            @pl.when(hands)
            def _(s=s):
                fold_left(s, SR, SE, SV)
                fold_left(s, SP)
                fold_right(s, SP, PAIR, ALL)
                fold_right(s, SR, ALL, CHAIN, SV)

            after_chain("hands", s)

    @pl.when(alone)
    def _():
        for s in range(2):
            @pl.when(alone)
            def _(s=s):
                fold_left(s, SR, SE)
                fold_right(s, SR, ALL, CHAIN)

            after_chain("alone", s)

    neighbour(odd & turns & xe)
    send_coupling(late)

    send_offset(odd & (chip == 0), ALL, EVEN, core, O_EVEN)
    send_offset(odd & (chip == 2), PAIR, EVEN, core, O_EVEN)
    send_offset(odd & (chip == 3), OWN, EVEN, core, O_EVEN)
    low_y = odd & ye

    @pl.when(low_y)
    def _():
        spread(YO, to_slot(SZ))

    @pl.when(low_y & (chip == 1))
    def _():
        high[SA], low[SA] = high[SC], low[SC]
        so[BASE] = so[OWN]

    @pl.when(low_y & (chip == 0))
    def _():
        high[SA], low[SA] = high[SX], low[SX]
        so[BASE] = so[XO]

    @pl.when(low_y)
    def _():
        fold_at_once(SA, BASE, EVEN)

    send_offset(odd & (chip == 1), EVEN, EVEN, core, O_EVEN)

    @pl.when(odd & (chip == 0))
    def _():
        spread(EVEN, to_slot(SZ))

    @pl.when(odd & (chip == 1))
    def _():
        spread(YO, to_slot(SZ))

    @pl.when(odd & (chip == 2))
    def _():
        spread(XO, to_slot(SZ))

    @pl.when(odd & (chip < 3))
    def _():
        fold_whole(SM, g_ref, acc)

    @pl.when(odd & (chip == 3))
    def _():
        acc[...] = g_ref[...]

    @pl.when(odd & rest & (chip < 3))
    def _():
        got_factor(LAST)
        load_factor(LAST, SA)

    @pl.when(odd & rest & (chip == 3))
    def _():
        high[SA], low[SA] = high[SM], low[SM]

    for parts, ref, recv in (
        ((0, 1, 2, 3), pm.at[ZF, :half, :WIDE], R_FACTOR[ZF]), ((4, 5), factor(ZF)[4], R_ENDS),
    ):
        @pl.when(bottom & even)
        def _(ref=ref, recv=recv):
            copy(ref, ref, sent.at[0], got.at[recv], me).wait_recv()

        count = len(parts) // 2
        for i in range(2):
            mine = parts[i * count:(i + 1) * count]
            send_factor(bottom & even & (b1 == i), ZF, ZF, px, E_X, mine, recv=R_ZF2, last=None)
            send_factor(bottom & even & (b1 == i), ZF, YF, core, E_ALL, mine, last=None)

    @pl.when(even)
    def _():
        got_offset(EVEN)
        spread(EVEN, to_ref(acc))

    @pl.when(bottom & even)
    def _():
        copy(half_tally, half_tally, sent.at[0], got.at[R_ZF2], me).wait_recv()

    for i in range(2):
        send_factor(bottom & even & (b1 != i), ZF, YF, core, E_ALL, (2 * i, 2 * i + 1, 4 + i), last=None)

    @pl.when(bottom & even)
    def _():
        load_factor(ZF, SR)

    @pl.when(odd)
    def _():
        split(other[...], qh_ref, ql_ref)

    @pl.when(even & (me > 0))
    def _():
        copy(prev, prev, n_send, n_recv, me).wait_recv()
        split(prev[...], qh_ref, ql_ref)

    @pl.when(me == 0)
    def _():
        qh_ref[...] = jnp.zeros_like(qh_ref)
        ql_ref[...] = jnp.zeros_like(ql_ref)

    apart = odd & rest & jnp.logical_not(chain)
    waits = rest & (even | jnp.logical_not(chain))
    drain()
    for s in range(2):
        take_edge(waits, apart, (2 * s, 2 * s + 1))

        @pl.when(rest)
        def _(s=s):
            spread(EDGE, to_slot(SZ), (s,))

    leave(apart, lambda: so.at[EDGE], O_TO)

    def got_given(s):
        ref = so.at[ZO, quarter(2 * s, 2), :]
        copy(ref, ref, sent.at[0], got.at[R_ZO[s]], me).wait_recv()

    for s in range(2):
        @pl.when(bottom & odd)
        def _(s=s):
            got_given(s)

        send_offset(bottom & odd, ZO, ZO, core, O_Z, (2 * s, 2 * s + 1), recv=R_ZO[s])

    leave(bottom & even, lambda: half_tally, E_X)
    leave(bottom & even, lambda: tally, E_ALL)

    @pl.when(bottom & odd)
    def _():
        got_factor(YF)
        load_factor(YF, SR)

    @pl.when(bottom)
    def _():
        fold_left(0, SR)
        fold_left(1, SR)

    @pl.when(bottom & even)
    def _():
        got_given(0)
        got_given(1)

    @pl.when(bottom)
    def _():
        fold_right(0, SR, ZO, CHAIN)
        fold_right(1, SR, ZO, CHAIN)
        spread(CHAIN, to_slot(SZ))

    @pl.when(rest)
    def _():
        fold_whole(SA, acc, x_ref, (xh_ref, xl_ref))

    @pl.when(top)
    def _():
        x_ref[...] = acc[...]
        split(acc[...], xh_ref, xl_ref)

    drain()


def finish(x_ref, xh, xl, qh, ql, d_any, c_any, c_ref, sem):
    copies = [pltpu.make_async_copy(x_ref, d_any, sem.at[0])]
    copies[0].start()
    half = x_ref.shape[0] // 2
    for i in range(2):
        rows = slice(i * half, (i + 1) * half)
        c_ref[rows, :] = product((xh.at[rows, :], xl.at[rows, :]), (qh, ql), NT)
        copies.append(pltpu.make_async_copy(c_ref.at[rows, :], c_any.at[rows, :], sem.at[1 + i]))
        copies[-1].start()
    for c in copies:
        c.wait()


def local(n, schur_inverse, sweep_factor):
    order = schur_inverse.shape[1]
    full = (order, order)
    f32, bf16 = jnp.float32, jnp.bfloat16
    dma = pltpu.SemaphoreType.DMA
    values = pl.pallas_call(
        functools.partial(kernel, n),
        out_shape=[pltpu.VMEM(full, f32)] + [pltpu.VMEM(full, bf16)] * 4,
        in_specs=[pl.BlockSpec(memory_space=pl.ANY)] * 2,
        out_specs=[pl.BlockSpec(memory_space=pltpu.VMEM)] * 5,
        scratch_shapes=[pltpu.VMEM(full, f32)] * 5 + [
            pltpu.VMEM((8,) + full, f32),
            pltpu.VMEM((8, order // 2, STRIP), f32),
            pltpu.VMEM((10, WIDE, WIDE), f32),
            pltpu.VMEM((13,) + full, bf16),
            pltpu.VMEM((13,) + full, bf16),
            pltpu.VMEM((order * WIDE // STRIP + order // 2, STRIP), f32),
            dma((9,)), dma((12 + PARTS,)), dma, dma, dma, dma, dma((2,)), pltpu.SemaphoreType.REGULAR,
        ],
        compiler_params=pltpu.CompilerParams(
            collective_id=0, has_side_effects=True
        ),
    )(schur_inverse[0], sweep_factor[0])
    diagonal, coupling = pl.pallas_call(
        finish,
        out_shape=[jax.ShapeDtypeStruct(full, f32)] * 2,
        in_specs=[pl.BlockSpec(memory_space=pltpu.VMEM)] * 5,
        out_specs=[pl.BlockSpec(memory_space=pl.ANY)] * 2,
        scratch_shapes=[pltpu.VMEM(full, f32), dma((3,))],
    )(*(pltpu.with_memory_space_constraint(v, pltpu.VMEM) for v in values))
    return diagonal[None], coupling[None]


def solution(mesh):
    n = mesh.shape["tm"]
    return jax.shard_map(
        functools.partial(local, n),
        mesh=mesh,
        in_specs=(P("tm", None, None), P("tm", None, None)),
        out_specs=(P("tm", None, None), P("tm", None, None)),
        check_vma=False,
    )
```
